128 devices in a mesh: dp: 64 (over z, y_lo, x, core), mp: 2 (over y_hi).
Axes of the slice: x: 4, y: 4 (y_hi: 2, y_lo: 2; y = y_hi * 2 + y_lo), z: 4, core: 2. Of those that a mesh axis runs over, the one named last changes fastest.
Arguments:
- images: bfloat16 [128, 197, 384], P('dp'), may hold values from -6 to 6
- routes: int32 [1, 128, 197, 2], P(None, 'dp'), may hold values from 0 to 3, all different within a row; in each aligned block of 197 rows (0 to 196, 197 to 393, ..., all dimensions but the last counted through in order) at most 104 rows name the same one
- w_qkv: bfloat16 [1, 384, 3, 384], P(None, 'dp', None, 'mp'), may hold values from -0.3125 to 0.3125
- w_proj: bfloat16 [1, 384, 384], P(None, 'mp', 'dp'), may hold values from -2 to 2
- w_in: bfloat16 [1, 4, 384, 1536], P(None, None, 'dp', 'mp'), may hold values from -0.3125 to 0.3125
- w_out: bfloat16 [1, 4, 1536, 384], P(None, None, 'mp', 'dp'), may hold values from -0.3125 to 0.3125
- w_router: bfloat16 [1, 384, 4], P(None, 'dp'), may hold values from -0.625 to 0.625
- ln_gain: bfloat16 [1, 2, 384], P(None, None, 'dp'), may hold values from 0.5 to 1.5
- ln_bias: bfloat16 [1, 2, 384], P(None, None, 'dp'), may hold values from -3 to 3
- cotangent: bfloat16 [128, 197, 384], P('dp'), may hold values from -6 to 6
Outputs:
- activations: float32 [128, 197, 384], P('dp')
- grad_images: float32 [128, 197, 384], P('dp')
- grad_qkv: float32 [1, 384, 3, 384], P(None, 'dp', None, 'mp')
- grad_proj: float32 [1, 384, 384], P(None, 'mp', 'dp')
- grad_in: float32 [1, 4, 384, 1536], P(None, None, 'dp', 'mp')
- grad_out: float32 [1, 4, 1536, 384], P(None, None, 'mp', 'dp')
- grad_router: float32 [1, 384, 4], P(None, 'dp')
- grad_gain: float32 [1, 2, 384], P(None, None, 'dp')
- grad_bias: float32 [1, 2, 384], P(None, None, 'dp')
The draws below stay inside these ranges and needn't reach their ends.
Inputs may be any that keep to these rules, and one draw needn't show every extreme that they name: `routes`: in each block, each aligned group of 1 images names every expert in at most 104 of its tokens, and some group names some expert in exactly 104; a token's two experts differ.
All inputs are finite; a program needn't handle non-finite values.
Results may differ from the reference program's by a relative error of at most 0.024.
Values may be sent and summed in bfloat16 or wider, within the bound.
A program may use at most 128 MiB of HBM per device.

```python
import math
import jax
import jax.numpy as jnp
import numpy as np
from jax import lax

D = 384
HEADS = 6
HD = 64
FF = 1536
EXPERTS = 4
TOPK = 2
SEQ = 197
LAYERS = 1
IMG_MB = 1
CAP = 104
IMAGES = 128


def level_of(stream_key, dims, shards, smallest, largest):
    factor_of = 1.0
    for dim, blocks in shards:
        steps = jax.random.uniform(jax.random.fold_in(jax.random.fold_in(stream_key, 6), dim), (blocks,), jnp.float32, smallest / len(shards), largest / len(shards))
        factor_of = factor_of * jnp.repeat(jnp.exp(steps), dims[dim] // blocks).reshape((-1,) + (1,) * (len(dims) - 1 - dim))
    return factor_of


def assign_block(stream_key, own, number, rows, count, top, most, skew):
    sequence = jax.random.permutation(stream_key, count)
    crowded, usual = portions_of(count, rows * top, most, skew, True), portions_of(count, rows * top, most, skew, False)
    places = jnp.arange(count)

    def named(lengths, turn):
        used = int((lengths > 0).sum())
        fixed = max(1, used // 4)
        moved = fixed + (places - fixed + turn * (used - fixed)) % max(1, count - fixed)
        return jnp.zeros((count,), jnp.int32).at[sequence[jnp.where(places < fixed, places, moved)]].set(jnp.asarray(lengths, jnp.int32))

    lengths = jnp.where(number % 4 == 0, named(crowded, number // 4), named(usual, number - number // 4 - 1))
    mixed = jax.random.permutation(jax.random.fold_in(own, 3), count)
    giver, sink = mixed[0:count // 2 * 2:2], mixed[1:count // 2 * 2:2]
    room = jnp.minimum(lengths[giver] - 1, most - lengths[sink]) // 2
    room = jnp.where((giver == sequence[0]) | (sink == sequence[0]) | (lengths[sink] == 0), 0, jnp.maximum(room, 0))
    moved = jax.random.randint(jax.random.fold_in(own, 4), (count // 2,), 0, 1 << 20) % (room + 1)
    lengths = lengths.at[giver].add(-moved).at[sink].add(moved)
    items = jnp.searchsorted(jnp.cumsum(lengths), jnp.arange(rows * top), side="right").astype(jnp.int32)
    grid = items.reshape(top, rows).T
    grid = grid[jax.random.permutation(jax.random.fold_in(own, 1), rows)]
    turn = jax.random.randint(jax.random.fold_in(own, 2), (rows, 1), 0, top)
    return jnp.take_along_axis(grid, (jnp.arange(top)[None, :] + turn) % top, axis=1)


def portions_of(amount, total, most, lean, full):
    weights = [(1 << 20) // math.isqrt(standing ** lean) + 1 for standing in range(1, amount + 1)]
    largest = most if full else min(most, max(-(-total // amount), total * weights[0] // sum(weights)))
    least = 1 if total - largest >= amount - 1 else 0
    counts, surplus = [largest] + [least] * (amount - 1), total - largest - least * (amount - 1)
    while surplus > 0:
        candidates = [i for i in range(1, amount) if counts[i] < largest] or [i for i in range(1, amount) if counts[i] < most]
        pool, left = sum([weights[i] for i in candidates]), surplus
        for i in candidates:
            addition = min(most - counts[i], max(1, left * weights[i] // pool), surplus)
            counts[i] = counts[i] + addition
            surplus = surplus - addition
    return np.array(counts)


def bell_draw(rng, shape, width, limit, cuts=(), kind=jnp.bfloat16):
    entries = width * jax.random.normal(rng, shape, jnp.float32)
    if cuts:
        entries = entries * level_of(rng, shape, cuts, -0.22, 0.18)
    return jnp.clip(entries, -limit, limit).astype(kind)


def setup_inputs(seed: int = 0) -> dict:
    splits = jax.random.split(jax.random.key(seed), 11)
    images = bell_draw(splits[0], (IMAGES, SEQ, D), 1.0, 6.0, ((0, 64),))
    routes_keys = jax.random.split(jax.random.fold_in(splits[1], 1), LAYERS * IMAGES * SEQ // (IMG_MB * SEQ))
    routes_turns = jax.random.permutation(jax.random.fold_in(splits[1], 3), LAYERS * IMAGES * SEQ // (IMG_MB * SEQ))
    routes = jax.vmap(lambda own, number: assign_block(jax.random.fold_in(splits[1], 2), own, number, IMG_MB * SEQ, EXPERTS, TOPK, CAP, 0))(routes_keys, routes_turns).reshape((LAYERS, IMAGES, SEQ, TOPK))
    w_qkv = bell_draw(splits[2], (LAYERS, D, 3, HEADS * HD), D ** -0.5, 0.3125, ((1, 64), (3, 2)))
    w_proj = bell_draw(splits[3], (LAYERS, HEADS * HD, D), (max(D // 64, 8)) ** -0.5, 2.0, ((1, 2), (2, 64)))
    w_in = bell_draw(splits[4], (LAYERS, EXPERTS, D, FF), D ** -0.5, 0.3125, ((2, 64), (3, 2)))
    w_out = bell_draw(splits[5], (LAYERS, EXPERTS, FF, D), (FF // 4) ** -0.5, 0.3125, ((2, 2), (3, 64)))
    w_router = bell_draw(splits[6], (LAYERS, D, EXPERTS), (D // 4) ** -0.5, 0.625, ((1, 64),))
    ln_gain = jnp.clip(1.0 + 0.1 * jax.random.normal(splits[7], (LAYERS, 2, D), jnp.float32), 0.5, 1.5).astype(jnp.bfloat16)
    ln_bias = bell_draw(splits[8], (LAYERS, 2, D), 0.3, 3.0, ((2, 64),))
    cotangent = bell_draw(splits[9], (IMAGES, SEQ, D), 1.0, 6.0, ((0, 64),))
    return dict(images=images, routes=routes, w_qkv=w_qkv, w_proj=w_proj, w_in=w_in, w_out=w_out, w_router=w_router, ln_gain=ln_gain, ln_bias=ln_bias, cotangent=cotangent)


EPSILON = 1e-06
HIGHEST = lax.Precision.HIGHEST

@jax.custom_vjp
def low(v):
    return lax.optimization_barrier(v.astype(jnp.bfloat16)).astype(jnp.float32)

@jax.custom_vjp
def low_back(v):
    return v

def low_keep(v):
    return (low(v), None)

def low_pass(kept, grad):
    return (grad,)

def back_keep(v):
    return (v, None)

def back_low(kept, grad):
    return (low(grad),)
low.defvjp(low_keep, low_pass)
low_back.defvjp(back_keep, back_low)

def layer_norm(field, gain_row, shift_row):
    mean_value = lax.optimization_barrier(jnp.mean(field, axis=-1, keepdims=True))
    centered = field - mean_value
    variance = lax.optimization_barrier(jnp.mean(centered * centered, axis=-1, keepdims=True))
    return centered * lax.rsqrt(variance + EPSILON) * gain_row + shift_row

def slot_positions(chosen_ids):
    labels = jnp.arange(EXPERTS, dtype=jnp.int32)
    hit_counts = lax.optimization_barrier(jnp.sum((chosen_ids[:, :, None] == labels).astype(jnp.int32), axis=1))
    before = jnp.cumsum(hit_counts, axis=0) - hit_counts
    return jnp.take_along_axis(before, chosen_ids, axis=1).astype(jnp.int32)

def moe_block(field, chosen_ids, w_qkv, w_proj, w_in, w_out, w_router, ln_gain, ln_bias):
    image_count, length, model_width = field.shape
    row_count = image_count * length
    head_count = w_qkv.shape[2] // HD
    normed = low(layer_norm(field, ln_gain[0], ln_bias[0]))
    projected = low(low_back(jnp.einsum('bsd,dcf->bscf', normed, w_qkv, precision=HIGHEST)))
    queries = projected[:, :, 0].reshape(image_count, length, head_count, HD)
    key_rows = projected[:, :, 1].reshape(image_count, length, head_count, HD)
    value_rows = projected[:, :, 2].reshape(image_count, length, head_count, HD)
    scores = low_back(jnp.einsum('bqhe,bkhe->bhqk', queries, key_rows, precision=HIGHEST) * HD ** (-0.5))
    weights = jax.nn.softmax(scores, axis=-1)
    attended = jnp.einsum('bhqk,bkhe->bqhe', low(weights), value_rows, precision=HIGHEST)
    attended = low(low_back(attended.reshape(image_count, length, head_count * HD)))
    hidden = field + low_back(jnp.einsum('bsf,fd->bsd', attended, w_proj, precision=HIGHEST))
    second = low(layer_norm(hidden, ln_gain[1], ln_bias[1])).reshape(row_count, model_width)
    logits = low_back(jnp.dot(second, w_router, precision=HIGHEST))
    router = jax.nn.softmax(logits, axis=-1)
    labels = jnp.arange(EXPERTS, dtype=jnp.int32)
    chosen = (chosen_ids[:, :, None] == labels).astype(jnp.float32)
    gate_values = lax.optimization_barrier(jnp.sum(router[:, None, :] * chosen, axis=-1))
    slot_index = (chosen_ids * CAP + slot_positions(chosen_ids)).reshape(-1).astype(jnp.int32)
    slot_rows = jnp.zeros((EXPERTS * CAP, model_width), jnp.float32).at[slot_index].add(jnp.repeat(second, TOPK, axis=0))
    slot_rows = slot_rows.reshape(EXPERTS, CAP, model_width)
    inner_pre = low_back(jnp.einsum('ecd,edf->ecf', slot_rows, w_in, precision=HIGHEST))
    activated = low(jax.nn.gelu(inner_pre, approximate=False))
    produced = low_back(jnp.einsum('ecf,efd->ecd', activated, w_out, precision=HIGHEST))
    produced = produced.reshape(EXPERTS * CAP, model_width)
    picked = jnp.take(produced, slot_index, axis=0).reshape(row_count, TOPK, model_width)
    combined = lax.optimization_barrier(jnp.sum(gate_values[:, :, None] * picked, axis=1))
    return hidden + combined.reshape(image_count, length, model_width)

def run_group(field, group_routes, params):
    for layer_index in range(LAYERS):
        field = moe_block(field, group_routes[layer_index], *[tensor[layer_index] for tensor in params])
    return field

def reference(images, routes, w_qkv, w_proj, w_in, w_out, w_router, ln_gain, ln_bias, cotangent):
    group_count = images.shape[0] // IMG_MB
    inputs = images.astype(jnp.float32).reshape(group_count, IMG_MB, SEQ, D)
    grouped = routes.reshape(LAYERS, group_count, IMG_MB * SEQ, TOPK).transpose(1, 0, 2, 3)
    params = (w_qkv.astype(jnp.float32), w_proj.astype(jnp.float32), w_in.astype(jnp.float32), w_out.astype(jnp.float32), w_router.astype(jnp.float32), ln_gain.astype(jnp.float32), ln_bias.astype(jnp.float32))
    checked = jax.checkpoint(run_group)

    def forward(inputs, params):

        def step_fn(carry, item):
            return (carry, checked(item[0], item[1], params))
        carry_out, outputs = lax.scan(step_fn, jnp.zeros((), jnp.float32), (inputs, grouped))
        return outputs
    outputs, pull_back = jax.vjp(forward, inputs, params)
    grad_inputs, grad_params = pull_back(cotangent.astype(jnp.float32).reshape(outputs.shape))
    return (outputs.reshape(images.shape), grad_inputs.reshape(images.shape), grad_params[0], grad_params[1], grad_params[2], grad_params[3], grad_params[4], grad_params[5], grad_params[6])
```

```python
import jax
import jax.numpy as jnp
from jax import lax
from jax.sharding import PartitionSpec as P

HD = 64
EXPERTS = 4
TOPK = 2
CAP = 104
EPSILON = 1e-06


def norm_forward(field, gain_row, shift_row):
    mean_value = jnp.mean(field, axis=-1, keepdims=True)
    centered = field - mean_value
    inverse = lax.rsqrt(jnp.mean(centered * centered, axis=-1, keepdims=True) + EPSILON)
    normed = centered * inverse
    return (normed * gain_row + shift_row, normed, inverse)


def norm_backward(grad_out, normed, inverse, gain_row):
    grad_gain = jnp.sum(grad_out * normed, axis=0)
    grad_shift = jnp.sum(grad_out, axis=0)
    scaled = grad_out * gain_row
    grad_in = inverse * (
        scaled
        - jnp.mean(scaled, axis=-1, keepdims=True)
        - normed * jnp.mean(scaled * normed, axis=-1, keepdims=True)
    )
    return (grad_in, grad_gain, grad_shift)


def slot_positions(chosen_ids):
    labels = jnp.arange(EXPERTS, dtype=jnp.int32)
    hit_counts = jnp.sum((chosen_ids[..., None] == labels).astype(jnp.int32), axis=-2)
    before = jnp.cumsum(hit_counts, axis=1) - hit_counts
    return jnp.take_along_axis(before, chosen_ids, axis=-1)


def gelu_slope(inner_pre):
    cumulative = 0.5 * (1.0 + jax.scipy.special.erf(inner_pre * 0.7071067811865476))
    density = jnp.exp(-0.5 * inner_pre * inner_pre) * 0.3989422804014327
    return cumulative + inner_pre * density


def shard_sizes(w_qkv, w_proj, w_in, w_out, w_router, ln_gain, ln_bias):
    return [a.size for a in (w_qkv, w_proj, w_in, w_out, w_router, ln_gain, ln_bias)]


def gather_weights(w_qkv, w_proj, w_in, w_out, w_router, ln_gain, ln_bias, n):
    parts = (w_qkv, w_proj, w_in, w_out, w_router, ln_gain, ln_bias)
    flat = jnp.concatenate([a.reshape(-1) for a in parts])
    full = lax.all_gather(flat, "dp", axis=0, tiled=True).reshape(n, -1)
    pieces = []
    start = 0
    for a in parts:
        pieces.append(full[:, start:start + a.size])
        start += a.size
    q, p, i, o, r, g, b = pieces
    _, rq, cq, fq = w_qkv.shape
    gq = q.reshape(n * rq, cq, fq)
    _, fp, dp_ = w_proj.shape
    gp = p.reshape(n, fp, dp_).transpose(1, 0, 2).reshape(fp, n * dp_)
    _, ei, di, fi = w_in.shape
    gi = i.reshape(n, ei, di, fi).transpose(1, 0, 2, 3).reshape(ei, n * di, fi)
    _, eo, fo, do_ = w_out.shape
    go = o.reshape(n, eo, fo, do_).transpose(1, 2, 0, 3).reshape(eo, fo, n * do_)
    _, dr, er = w_router.shape
    gr = r.reshape(n * dr, er)
    _, two, dg = ln_gain.shape
    gg = g.reshape(n, two, dg).transpose(1, 0, 2).reshape(two, n * dg)
    gb = b.reshape(n, two, dg).transpose(1, 0, 2).reshape(two, n * dg)
    return (gq, gp, gi, go, gr, gg, gb)


def scatter_grads(grads, n, shapes):
    gq, gp, gi, go, gr, gg, gb = grads
    rows = [
        gq.reshape(n, -1),
        gp.reshape(gp.shape[0], n, -1).transpose(1, 0, 2).reshape(n, -1),
        gi.reshape(gi.shape[0], n, -1, gi.shape[2]).transpose(1, 0, 2, 3).reshape(n, -1),
        go.reshape(go.shape[0], go.shape[1], n, -1).transpose(2, 0, 1, 3).reshape(n, -1),
        gr.reshape(n, -1),
        gg.reshape(gg.shape[0], n, -1).transpose(1, 0, 2).reshape(n, -1),
        gb.reshape(gb.shape[0], n, -1).transpose(1, 0, 2).reshape(n, -1),
    ]
    packed = jnp.concatenate(rows, axis=1)
    mine = lax.psum_scatter(packed.reshape(-1), "dp", scatter_dimension=0, tiled=True)
    outs = []
    start = 0
    for shape in shapes:
        size = 1
        for s in shape:
            size *= s
        outs.append(mine[start:start + size].reshape(shape))
        start += size
    return outs


def layer_forward(field, chosen_ids, weights):
    w_qkv, w_proj, w_in, w_out, w_router, ln_gain, ln_bias = weights
    image_count, length, model_width = field.shape
    row_count = image_count * length
    head_count = w_qkv.shape[2] // HD
    score_scale = HD ** (-0.5)
    gain_rows = ln_gain.astype(jnp.float32)
    shift_rows = ln_bias.astype(jnp.float32)
    flat = field.reshape(row_count, model_width)
    first, normed_one, inverse_one = norm_forward(flat, gain_rows[0], shift_rows[0])
    first = first.astype(jnp.bfloat16)
    projected = jnp.einsum("rd,dcf->rcf", first, w_qkv, preferred_element_type=jnp.float32).astype(
        jnp.bfloat16
    )
    projected = projected.reshape(image_count, length, 3, head_count, HD)
    queries = projected[:, :, 0]
    key_rows = projected[:, :, 1]
    value_rows = projected[:, :, 2]
    scores = (
        jnp.einsum("bqhe,bkhe->bhqk", queries, key_rows, preferred_element_type=jnp.float32)
        * score_scale
    )
    log_total = jax.nn.logsumexp(scores, axis=-1)
    attn_weights = jnp.exp(scores - log_total[..., None]).astype(jnp.bfloat16)
    attended = jnp.einsum(
        "bhqk,bkhe->bqhe", attn_weights, value_rows, preferred_element_type=jnp.float32
    )
    attended = attended.astype(jnp.bfloat16).reshape(row_count, head_count * HD)
    partial_attn = jnp.dot(attended, w_proj, preferred_element_type=jnp.float32)
    hidden = flat + lax.psum(partial_attn, "mp")
    second, normed_two, inverse_two = norm_forward(hidden, gain_rows[1], shift_rows[1])
    second = second.astype(jnp.bfloat16)
    logits = jnp.dot(second, w_router, preferred_element_type=jnp.float32)
    router = jax.nn.softmax(logits, axis=-1)
    labels = jnp.arange(EXPERTS, dtype=jnp.int32)
    ids_flat = chosen_ids.reshape(row_count, TOPK)
    chosen = (ids_flat[:, :, None] == labels).astype(jnp.float32)
    gate_values = jnp.sum(router[:, None, :] * chosen, axis=-1)
    per_image = EXPERTS * CAP
    image_base = (jnp.arange(image_count, dtype=jnp.int32) * per_image)[:, None, None]
    slot_index = (chosen_ids * CAP + slot_positions(chosen_ids) + image_base).reshape(-1)
    owners = (
        jnp.full((image_count * per_image,), row_count, jnp.int32)
        .at[slot_index]
        .set(jnp.repeat(jnp.arange(row_count, dtype=jnp.int32), TOPK))
    )
    slot_gate = (
        jnp.zeros((image_count * per_image,), jnp.float32).at[slot_index].set(gate_values.reshape(-1))
    )
    padded = jnp.concatenate([second, jnp.zeros((1, model_width), jnp.bfloat16)], axis=0)
    slot_rows = jnp.take(padded, owners, axis=0).reshape(image_count, EXPERTS, CAP, model_width)
    inner_pre = jnp.einsum("becd,edf->becf", slot_rows, w_in, preferred_element_type=jnp.float32)
    activated = jax.nn.gelu(inner_pre, approximate=False).astype(jnp.bfloat16)
    produced = jnp.einsum("becf,efd->becd", activated, w_out, preferred_element_type=jnp.float32)
    produced = produced.reshape(image_count * per_image, model_width)
    picked = jnp.take(produced, slot_index, axis=0).reshape(row_count, TOPK, model_width)
    partial_moe = jnp.sum(gate_values[:, :, None] * picked, axis=1)
    output = hidden + lax.psum(partial_moe.astype(jnp.bfloat16), "mp").astype(jnp.float32)
    record = (
        normed_one, inverse_one, first, projected, log_total, attended, normed_two, inverse_two,
        second, router, chosen, slot_index, owners, slot_gate, slot_rows, inner_pre, activated, picked,
    )
    return (output.reshape(image_count, length, model_width), record)


def layer_backward(grad_field, record, weights):
    w_qkv, w_proj, w_in, w_out, w_router, ln_gain, ln_bias = weights
    (
        normed_one, inverse_one, first, projected, log_total, attended, normed_two, inverse_two,
        second, router, chosen, slot_index, owners, slot_gate, slot_rows, inner_pre, activated, picked,
    ) = record
    image_count, length, model_width = grad_field.shape
    row_count = image_count * length
    head_count = projected.shape[3]
    score_scale = HD ** (-0.5)
    gain_rows = ln_gain.astype(jnp.float32)
    grad_flat = grad_field.reshape(row_count, model_width)
    padded_grad = jnp.concatenate([grad_flat, jnp.zeros((1, model_width), jnp.float32)], axis=0)
    grad_slots = (jnp.take(padded_grad, owners, axis=0) * slot_gate[:, None]).astype(jnp.bfloat16)
    grad_slots = grad_slots.reshape(image_count, EXPERTS, CAP, model_width)
    grad_w_out = jnp.einsum(
        "becf,becd->efd", activated, grad_slots, preferred_element_type=jnp.float32
    )
    grad_act = jnp.einsum("becd,efd->becf", grad_slots, w_out, preferred_element_type=jnp.float32)
    grad_inner = (grad_act * gelu_slope(inner_pre)).astype(jnp.bfloat16)
    grad_w_in = jnp.einsum(
        "becd,becf->edf", slot_rows, grad_inner, preferred_element_type=jnp.float32
    )
    grad_slot_rows = jnp.einsum(
        "becf,edf->becd", grad_inner, w_in, preferred_element_type=jnp.float32
    )
    grad_slot_rows = grad_slot_rows.reshape(image_count * EXPERTS * CAP, model_width)
    partial_second = jnp.sum(
        jnp.take(grad_slot_rows, slot_index, axis=0).reshape(row_count, TOPK, model_width), axis=1
    )
    partial_gate = jnp.sum(picked * grad_flat[:, None, :], axis=-1)
    grad_second, grad_gate = lax.psum((partial_second, partial_gate), "mp")
    grad_router = jnp.sum(grad_gate[:, :, None] * chosen, axis=1)
    grad_logits = router * (grad_router - jnp.sum(router * grad_router, axis=-1, keepdims=True))
    grad_logits = grad_logits.astype(jnp.bfloat16)
    grad_w_router = jnp.dot(second.T, grad_logits, preferred_element_type=jnp.float32)
    grad_second = grad_second + jnp.dot(grad_logits, w_router.T, preferred_element_type=jnp.float32)
    grad_from_norm, grad_gain_two, grad_shift_two = norm_backward(
        grad_second, normed_two, inverse_two, gain_rows[1]
    )
    grad_hidden = grad_flat + grad_from_norm
    grad_hidden_low = grad_hidden.astype(jnp.bfloat16)
    grad_w_proj = jnp.dot(attended.T, grad_hidden_low, preferred_element_type=jnp.float32)
    grad_attended = jnp.dot(grad_hidden_low, w_proj.T, preferred_element_type=jnp.float32).astype(
        jnp.bfloat16
    )
    grad_attended = grad_attended.reshape(image_count, length, head_count, HD)
    queries = projected[:, :, 0]
    key_rows = projected[:, :, 1]
    value_rows = projected[:, :, 2]
    scores = (
        jnp.einsum("bqhe,bkhe->bhqk", queries, key_rows, preferred_element_type=jnp.float32)
        * score_scale
    )
    probs = jnp.exp(scores - log_total[..., None])
    grad_values = jnp.einsum(
        "bhqk,bqhe->bkhe", probs.astype(jnp.bfloat16), grad_attended,
        preferred_element_type=jnp.float32,
    )
    grad_probs = jnp.einsum(
        "bqhe,bkhe->bhqk", grad_attended, value_rows, preferred_element_type=jnp.float32
    )
    grad_scores = (
        probs * (grad_probs - jnp.sum(probs * grad_probs, axis=-1, keepdims=True))
    ).astype(jnp.bfloat16)
    grad_queries = (
        jnp.einsum("bhqk,bkhe->bqhe", grad_scores, key_rows, preferred_element_type=jnp.float32)
        * score_scale
    )
    grad_keys = (
        jnp.einsum("bhqk,bqhe->bkhe", grad_scores, queries, preferred_element_type=jnp.float32)
        * score_scale
    )
    grad_projected = jnp.stack([grad_queries, grad_keys, grad_values], axis=2).astype(jnp.bfloat16)
    grad_projected = grad_projected.reshape(row_count, 3, head_count * HD)
    grad_w_qkv = jnp.einsum(
        "rd,rcf->dcf", first, grad_projected, preferred_element_type=jnp.float32
    )
    partial_first = jnp.einsum(
        "rcf,dcf->rd", grad_projected, w_qkv, preferred_element_type=jnp.float32
    )
    grad_first = lax.psum(partial_first.astype(jnp.bfloat16), "mp").astype(jnp.float32)
    grad_input_norm, grad_gain_one, grad_shift_one = norm_backward(
        grad_first, normed_one, inverse_one, gain_rows[0]
    )
    grad_input = grad_hidden + grad_input_norm
    grads = (
        grad_w_qkv,
        grad_w_proj,
        grad_w_in,
        grad_w_out,
        grad_w_router,
        jnp.stack([grad_gain_one, grad_gain_two]),
        jnp.stack([grad_shift_one, grad_shift_two]),
    )
    return (grad_input.reshape(image_count, length, model_width), grads)


def make_local(n):
    def local(images, routes, w_qkv, w_proj, w_in, w_out, w_router, ln_gain, ln_bias, cotangent):
        shapes = [a.shape for a in (w_qkv, w_proj, w_in, w_out, w_router, ln_gain, ln_bias)]
        weights = gather_weights(w_qkv, w_proj, w_in, w_out, w_router, ln_gain, ln_bias, n)
        field = images.astype(jnp.float32)
        output, record = layer_forward(field, routes[0], weights)
        grad_input, grads = layer_backward(cotangent.astype(jnp.float32), record, weights)
        shards = scatter_grads(grads, n, [(1,) + tuple(s[1:]) for s in shapes])
        return (output, grad_input, *shards)

    return local


def solution(mesh):
    n = mesh.shape["dp"]
    in_specs = (
        P("dp", None, None),
        P(None, "dp", None, None),
        P(None, "dp", None, "mp"),
        P(None, "mp", "dp"),
        P(None, None, "dp", "mp"),
        P(None, None, "mp", "dp"),
        P(None, "dp", None),
        P(None, None, "dp"),
        P(None, None, "dp"),
        P("dp", None, None),
    )
    out_specs = (
        P("dp", None, None),
        P("dp", None, None),
        P(None, "dp", None, "mp"),
        P(None, "mp", "dp"),
        P(None, None, "dp", "mp"),
        P(None, None, "mp", "dp"),
        P(None, "dp", None),
        P(None, None, "dp"),
        P(None, None, "dp"),
    )
    return jax.shard_map(make_local(n), mesh=mesh, in_specs=in_specs, out_specs=out_specs, check_vma=False)
```

```python
import functools

import jax
import jax.numpy as jnp
from jax import lax
from jax.sharding import PartitionSpec as P
from jax.experimental import pallas as pl
from jax.experimental.pallas import tpu as pltpu

MESH = pl.DeviceIdType.MESH
LANES = 128

HD = 64
EXPERTS = 4
TOPK = 2
CAP = 104
EPSILON = 1e-06


def norm_forward(field, gain_row, shift_row):
    mean_value = jnp.mean(field, axis=-1, keepdims=True)
    centered = field - mean_value
    inverse = lax.rsqrt(jnp.mean(centered * centered, axis=-1, keepdims=True) + EPSILON)
    normed = centered * inverse
    return (normed * gain_row + shift_row, normed, inverse)


def norm_backward(grad_out, normed, inverse, gain_row):
    grad_gain = jnp.sum(grad_out * normed, axis=0)
    grad_shift = jnp.sum(grad_out, axis=0)
    scaled = grad_out * gain_row
    grad_in = inverse * (
        scaled
        - jnp.mean(scaled, axis=-1, keepdims=True)
        - normed * jnp.mean(scaled * normed, axis=-1, keepdims=True)
    )
    return (grad_in, grad_gain, grad_shift)


def slot_positions(chosen_ids):
    labels = jnp.arange(EXPERTS, dtype=jnp.int32)
    hit_counts = jnp.sum((chosen_ids[..., None] == labels).astype(jnp.int32), axis=-2)
    before = jnp.cumsum(hit_counts, axis=1) - hit_counts
    return jnp.take_along_axis(before, chosen_ids, axis=-1)


def gelu_slope(inner_pre):
    cumulative = 0.5 * (1.0 + jax.scipy.special.erf(inner_pre * 0.7071067811865476))
    density = jnp.exp(-0.5 * inner_pre * inner_pre) * 0.3989422804014327
    return cumulative + inner_pre * density


def exchange_kernel(n, gather, x_ref, out_ref, send_sem, recv_sem, local_sem):
    me = lax.axis_index("dp")
    mp = lax.axis_index("mp")
    barrier = pltpu.get_barrier_semaphore()

    def greet(k, carry):
        peer = lax.rem(me + k, n)
        pl.semaphore_signal(barrier, inc=1, device_id=(peer, mp), device_id_type=MESH)
        return carry

    lax.fori_loop(1, n, greet, 0)
    pl.semaphore_wait(barrier, n - 1)
    own = pltpu.make_async_copy(x_ref if gather else x_ref.at[me], out_ref.at[me], local_sem)
    own.start()

    def describe(k):
        peer = lax.rem(me + k, n)
        return pltpu.make_async_remote_copy(
            src_ref=x_ref if gather else x_ref.at[peer],
            dst_ref=out_ref.at[me],
            send_sem=send_sem.at[k],
            recv_sem=recv_sem.at[k],
            device_id=(peer, mp),
            device_id_type=MESH,
        )

    def start(k, carry):
        describe(k).start()
        return carry

    def finish(k, carry):
        describe(k).wait()
        return carry

    lax.fori_loop(1, n, start, 0)
    lax.fori_loop(1, n, finish, 0)
    own.wait()


def exchange(x, n, gather, collective_id):
    rows = x.shape[-2]
    block_bytes = rows * LANES * x.dtype.itemsize
    return pl.pallas_call(
        functools.partial(exchange_kernel, n, gather),
        out_shape=jax.ShapeDtypeStruct((n, rows, LANES), x.dtype),
        in_specs=[pl.BlockSpec(memory_space=pl.ANY)],
        out_specs=pl.BlockSpec(memory_space=pl.ANY),
        scratch_shapes=[
            pltpu.SemaphoreType.DMA((n,)),
            pltpu.SemaphoreType.DMA((n,)),
            pltpu.SemaphoreType.DMA(()),
        ],
        compiler_params=pltpu.CompilerParams(collective_id=collective_id, has_side_effects=True),
        cost_estimate=pl.CostEstimate(flops=0, bytes_accessed=2 * n * block_bytes, transcendentals=0),
    )(x)


def padded_rows(size, dtype_rows=16):
    rows = -(-size // LANES)
    return -(-rows // dtype_rows) * dtype_rows


def shard_sizes(w_qkv, w_proj, w_in, w_out, w_router, ln_gain, ln_bias):
    return [a.size for a in (w_qkv, w_proj, w_in, w_out, w_router, ln_gain, ln_bias)]


def gather_weights(w_qkv, w_proj, w_in, w_out, w_router, ln_gain, ln_bias, n):
    parts = (w_qkv, w_proj, w_in, w_out, w_router, ln_gain, ln_bias)
    flat = jnp.concatenate([a.reshape(-1) for a in parts])
    total = flat.shape[0]
    rows = padded_rows(total)
    flat = jnp.pad(flat, (0, rows * LANES - total)).reshape(rows, LANES)
    full = exchange(flat, n, True, 0).reshape(n, rows * LANES)
    pieces = []
    start = 0
    for a in parts:
        pieces.append(full[:, start:start + a.size])
        start += a.size
    q, p, i, o, r, g, b = pieces
    _, rq, cq, fq = w_qkv.shape
    gq = q.reshape(n * rq, cq, fq)
    _, fp, dp_ = w_proj.shape
    gp = p.reshape(n, fp, dp_).transpose(1, 0, 2).reshape(fp, n * dp_)
    _, ei, di, fi = w_in.shape
    gi = i.reshape(n, ei, di, fi).transpose(1, 0, 2, 3).reshape(ei, n * di, fi)
    _, eo, fo, do_ = w_out.shape
    go = o.reshape(n, eo, fo, do_).transpose(1, 2, 0, 3).reshape(eo, fo, n * do_)
    _, dr, er = w_router.shape
    gr = r.reshape(n * dr, er)
    _, two, dg = ln_gain.shape
    gg = g.reshape(n, two, dg).transpose(1, 0, 2).reshape(two, n * dg)
    gb = b.reshape(n, two, dg).transpose(1, 0, 2).reshape(two, n * dg)
    return (gq, gp, gi, go, gr, gg, gb)


def scatter_grads(grads, n, shapes):
    gq, gp, gi, go, gr, gg, gb = grads
    rows = [
        gq.reshape(n, -1),
        gp.reshape(gp.shape[0], n, -1).transpose(1, 0, 2).reshape(n, -1),
        gi.reshape(gi.shape[0], n, -1, gi.shape[2]).transpose(1, 0, 2, 3).reshape(n, -1),
        go.reshape(go.shape[0], go.shape[1], n, -1).transpose(2, 0, 1, 3).reshape(n, -1),
        gr.reshape(n, -1),
        gg.reshape(gg.shape[0], n, -1).transpose(1, 0, 2).reshape(n, -1),
        gb.reshape(gb.shape[0], n, -1).transpose(1, 0, 2).reshape(n, -1),
    ]
    packed = jnp.concatenate(rows, axis=1)
    total = packed.shape[1]
    count = padded_rows(total)
    packed = jnp.pad(packed, ((0, 0), (0, count * LANES - total))).reshape(n, count, LANES)
    mine = jnp.sum(exchange(packed, n, False, 1), axis=0).reshape(-1)
    outs = []
    start = 0
    for shape in shapes:
        size = 1
        for s in shape:
            size *= s
        outs.append(mine[start:start + size].reshape(shape))
        start += size
    return outs


def layer_forward(field, chosen_ids, weights):
    w_qkv, w_proj, w_in, w_out, w_router, ln_gain, ln_bias = weights
    image_count, length, model_width = field.shape
    row_count = image_count * length
    head_count = w_qkv.shape[2] // HD
    score_scale = HD ** (-0.5)
    gain_rows = ln_gain.astype(jnp.float32)
    shift_rows = ln_bias.astype(jnp.float32)
    flat = field.reshape(row_count, model_width)
    first, normed_one, inverse_one = norm_forward(flat, gain_rows[0], shift_rows[0])
    first = first.astype(jnp.bfloat16)
    projected = jnp.einsum("rd,dcf->rcf", first, w_qkv, preferred_element_type=jnp.float32).astype(
        jnp.bfloat16
    )
    projected = projected.reshape(image_count, length, 3, head_count, HD)
    queries = projected[:, :, 0]
    key_rows = projected[:, :, 1]
    value_rows = projected[:, :, 2]
    scores = (
        jnp.einsum("bqhe,bkhe->bhqk", queries, key_rows, preferred_element_type=jnp.float32)
        * score_scale
    )
    log_total = jax.nn.logsumexp(scores, axis=-1)
    attn_weights = jnp.exp(scores - log_total[..., None]).astype(jnp.bfloat16)
    attended = jnp.einsum(
        "bhqk,bkhe->bqhe", attn_weights, value_rows, preferred_element_type=jnp.float32
    )
    attended = attended.astype(jnp.bfloat16).reshape(row_count, head_count * HD)
    partial_attn = jnp.dot(attended, w_proj, preferred_element_type=jnp.float32)
    hidden = flat + lax.psum(partial_attn, "mp")
    second, normed_two, inverse_two = norm_forward(hidden, gain_rows[1], shift_rows[1])
    second = second.astype(jnp.bfloat16)
    logits = jnp.dot(second, w_router, preferred_element_type=jnp.float32)
    router = jax.nn.softmax(logits, axis=-1)
    labels = jnp.arange(EXPERTS, dtype=jnp.int32)
    ids_flat = chosen_ids.reshape(row_count, TOPK)
    chosen = (ids_flat[:, :, None] == labels).astype(jnp.float32)
    gate_values = jnp.sum(router[:, None, :] * chosen, axis=-1)
    per_image = EXPERTS * CAP
    image_base = (jnp.arange(image_count, dtype=jnp.int32) * per_image)[:, None, None]
    slot_index = (chosen_ids * CAP + slot_positions(chosen_ids) + image_base).reshape(-1)
    owners = (
        jnp.full((image_count * per_image,), row_count, jnp.int32)
        .at[slot_index]
        .set(jnp.repeat(jnp.arange(row_count, dtype=jnp.int32), TOPK))
    )
    slot_gate = (
        jnp.zeros((image_count * per_image,), jnp.float32).at[slot_index].set(gate_values.reshape(-1))
    )
    padded = jnp.concatenate([second, jnp.zeros((1, model_width), jnp.bfloat16)], axis=0)
    slot_rows = jnp.take(padded, owners, axis=0).reshape(image_count, EXPERTS, CAP, model_width)
    inner_pre = jnp.einsum("becd,edf->becf", slot_rows, w_in, preferred_element_type=jnp.float32)
    activated = jax.nn.gelu(inner_pre, approximate=False).astype(jnp.bfloat16)
    produced = jnp.einsum("becf,efd->becd", activated, w_out, preferred_element_type=jnp.float32)
    produced = produced.reshape(image_count * per_image, model_width)
    picked = jnp.take(produced, slot_index, axis=0).reshape(row_count, TOPK, model_width)
    partial_moe = jnp.sum(gate_values[:, :, None] * picked, axis=1)
    output = hidden + lax.psum(partial_moe.astype(jnp.bfloat16), "mp").astype(jnp.float32)
    record = (
        normed_one, inverse_one, first, projected, log_total, attended, normed_two, inverse_two,
        second, router, chosen, slot_index, owners, slot_gate, slot_rows, inner_pre, activated, picked,
    )
    return (output.reshape(image_count, length, model_width), record)


def layer_backward(grad_field, record, weights):
    w_qkv, w_proj, w_in, w_out, w_router, ln_gain, ln_bias = weights
    (
        normed_one, inverse_one, first, projected, log_total, attended, normed_two, inverse_two,
        second, router, chosen, slot_index, owners, slot_gate, slot_rows, inner_pre, activated, picked,
    ) = record
    image_count, length, model_width = grad_field.shape
    row_count = image_count * length
    head_count = projected.shape[3]
    score_scale = HD ** (-0.5)
    gain_rows = ln_gain.astype(jnp.float32)
    grad_flat = grad_field.reshape(row_count, model_width)
    padded_grad = jnp.concatenate([grad_flat, jnp.zeros((1, model_width), jnp.float32)], axis=0)
    grad_slots = (jnp.take(padded_grad, owners, axis=0) * slot_gate[:, None]).astype(jnp.bfloat16)
    grad_slots = grad_slots.reshape(image_count, EXPERTS, CAP, model_width)
    grad_w_out = jnp.einsum(
        "becf,becd->efd", activated, grad_slots, preferred_element_type=jnp.float32
    )
    grad_act = jnp.einsum("becd,efd->becf", grad_slots, w_out, preferred_element_type=jnp.float32)
    grad_inner = (grad_act * gelu_slope(inner_pre)).astype(jnp.bfloat16)
    grad_w_in = jnp.einsum(
        "becd,becf->edf", slot_rows, grad_inner, preferred_element_type=jnp.float32
    )
    grad_slot_rows = jnp.einsum(
        "becf,edf->becd", grad_inner, w_in, preferred_element_type=jnp.float32
    )
    grad_slot_rows = grad_slot_rows.reshape(image_count * EXPERTS * CAP, model_width)
    partial_second = jnp.sum(
        jnp.take(grad_slot_rows, slot_index, axis=0).reshape(row_count, TOPK, model_width), axis=1
    )
    partial_gate = jnp.sum(picked * grad_flat[:, None, :], axis=-1)
    grad_second, grad_gate = lax.psum((partial_second, partial_gate), "mp")
    grad_router = jnp.sum(grad_gate[:, :, None] * chosen, axis=1)
    grad_logits = router * (grad_router - jnp.sum(router * grad_router, axis=-1, keepdims=True))
    grad_logits = grad_logits.astype(jnp.bfloat16)
    grad_w_router = jnp.dot(second.T, grad_logits, preferred_element_type=jnp.float32)
    grad_second = grad_second + jnp.dot(grad_logits, w_router.T, preferred_element_type=jnp.float32)
    grad_from_norm, grad_gain_two, grad_shift_two = norm_backward(
        grad_second, normed_two, inverse_two, gain_rows[1]
    )
    grad_hidden = grad_flat + grad_from_norm
    grad_hidden_low = grad_hidden.astype(jnp.bfloat16)
    grad_w_proj = jnp.dot(attended.T, grad_hidden_low, preferred_element_type=jnp.float32)
    grad_attended = jnp.dot(grad_hidden_low, w_proj.T, preferred_element_type=jnp.float32).astype(
        jnp.bfloat16
    )
    grad_attended = grad_attended.reshape(image_count, length, head_count, HD)
    queries = projected[:, :, 0]
    key_rows = projected[:, :, 1]
    value_rows = projected[:, :, 2]
    scores = (
        jnp.einsum("bqhe,bkhe->bhqk", queries, key_rows, preferred_element_type=jnp.float32)
        * score_scale
    )
    probs = jnp.exp(scores - log_total[..., None])
    grad_values = jnp.einsum(
        "bhqk,bqhe->bkhe", probs.astype(jnp.bfloat16), grad_attended,
        preferred_element_type=jnp.float32,
    )
    grad_probs = jnp.einsum(
        "bqhe,bkhe->bhqk", grad_attended, value_rows, preferred_element_type=jnp.float32
    )
    grad_scores = (
        probs * (grad_probs - jnp.sum(probs * grad_probs, axis=-1, keepdims=True))
    ).astype(jnp.bfloat16)
    grad_queries = (
        jnp.einsum("bhqk,bkhe->bqhe", grad_scores, key_rows, preferred_element_type=jnp.float32)
        * score_scale
    )
    grad_keys = (
        jnp.einsum("bhqk,bqhe->bkhe", grad_scores, queries, preferred_element_type=jnp.float32)
        * score_scale
    )
    grad_projected = jnp.stack([grad_queries, grad_keys, grad_values], axis=2).astype(jnp.bfloat16)
    grad_projected = grad_projected.reshape(row_count, 3, head_count * HD)
    grad_w_qkv = jnp.einsum(
        "rd,rcf->dcf", first, grad_projected, preferred_element_type=jnp.float32
    )
    partial_first = jnp.einsum(
        "rcf,dcf->rd", grad_projected, w_qkv, preferred_element_type=jnp.float32
    )
    grad_first = lax.psum(partial_first.astype(jnp.bfloat16), "mp").astype(jnp.float32)
    grad_input_norm, grad_gain_one, grad_shift_one = norm_backward(
        grad_first, normed_one, inverse_one, gain_rows[0]
    )
    grad_input = grad_hidden + grad_input_norm
    grads = (
        grad_w_qkv,
        grad_w_proj,
        grad_w_in,
        grad_w_out,
        grad_w_router,
        jnp.stack([grad_gain_one, grad_gain_two]),
        jnp.stack([grad_shift_one, grad_shift_two]),
    )
    return (grad_input.reshape(image_count, length, model_width), grads)


def make_local(n):
    def local(images, routes, w_qkv, w_proj, w_in, w_out, w_router, ln_gain, ln_bias, cotangent):
        shapes = [a.shape for a in (w_qkv, w_proj, w_in, w_out, w_router, ln_gain, ln_bias)]
        weights = gather_weights(w_qkv, w_proj, w_in, w_out, w_router, ln_gain, ln_bias, n)
        field = images.astype(jnp.float32)
        output, record = layer_forward(field, routes[0], weights)
        grad_input, grads = layer_backward(cotangent.astype(jnp.float32), record, weights)
        shards = scatter_grads(grads, n, [(1,) + tuple(s[1:]) for s in shapes])
        return (output, grad_input, *shards)

    return local


def solution(mesh):
    n = mesh.shape["dp"]
    in_specs = (
        P("dp", None, None),
        P(None, "dp", None, None),
        P(None, "dp", None, "mp"),
        P(None, "mp", "dp"),
        P(None, None, "dp", "mp"),
        P(None, None, "mp", "dp"),
        P(None, "dp", None),
        P(None, None, "dp"),
        P(None, None, "dp"),
        P("dp", None, None),
    )
    out_specs = (
        P("dp", None, None),
        P("dp", None, None),
        P(None, "dp", None, "mp"),
        P(None, "mp", "dp"),
        P(None, None, "dp", "mp"),
        P(None, None, "mp", "dp"),
        P(None, "dp", None),
        P(None, None, "dp"),
        P(None, None, "dp"),
    )
    return jax.shard_map(make_local(n), mesh=mesh, in_specs=in_specs, out_specs=out_specs, check_vma=False)
```

```python
import functools

import jax
import jax.numpy as jnp
from jax import lax
from jax.sharding import PartitionSpec as P
from jax.experimental import pallas as pl
from jax.experimental.pallas import tpu as pltpu

MESH = pl.DeviceIdType.MESH
LANES = 128

HD = 64
EXPERTS = 4
TOPK = 2
CAP = 104
EPSILON = 1e-06


def norm_forward(field, gain_row, shift_row):
    mean_value = jnp.mean(field, axis=-1, keepdims=True)
    centered = field - mean_value
    inverse = lax.rsqrt(jnp.mean(centered * centered, axis=-1, keepdims=True) + EPSILON)
    normed = centered * inverse
    return (normed * gain_row + shift_row, normed, inverse)


def norm_backward(grad_out, normed, inverse, gain_row):
    grad_gain = jnp.sum(grad_out * normed, axis=0)
    grad_shift = jnp.sum(grad_out, axis=0)
    scaled = grad_out * gain_row
    grad_in = inverse * (
        scaled
        - jnp.mean(scaled, axis=-1, keepdims=True)
        - normed * jnp.mean(scaled * normed, axis=-1, keepdims=True)
    )
    return (grad_in, grad_gain, grad_shift)


def slot_positions(chosen_ids):
    labels = jnp.arange(EXPERTS, dtype=jnp.int32)
    hit_counts = jnp.sum((chosen_ids[..., None] == labels).astype(jnp.int32), axis=-2)
    before = jnp.cumsum(hit_counts, axis=1) - hit_counts
    return jnp.take_along_axis(before, chosen_ids, axis=-1)


def gelu_slope(inner_pre):
    cumulative = 0.5 * (1.0 + jax.scipy.special.erf(inner_pre * 0.7071067811865476))
    density = jnp.exp(-0.5 * inner_pre * inner_pre) * 0.3989422804014327
    return cumulative + inner_pre * density


def exchange_kernel(n, gather, x_ref, out_ref, send_sem, recv_sem, local_sem):
    me = lax.axis_index("dp")
    mp = lax.axis_index("mp")
    barrier = pltpu.get_barrier_semaphore()

    def greet(k, carry):
        peer = lax.rem(me + k, n)
        pl.semaphore_signal(barrier, inc=1, device_id=(peer, mp), device_id_type=MESH)
        return carry

    lax.fori_loop(1, n, greet, 0)
    pl.semaphore_wait(barrier, n - 1)
    own = pltpu.make_async_copy(x_ref if gather else x_ref.at[me], out_ref.at[me], local_sem)
    own.start()

    def describe(k):
        peer = lax.rem(me + k, n)
        return pltpu.make_async_remote_copy(
            src_ref=x_ref if gather else x_ref.at[peer],
            dst_ref=out_ref.at[me],
            send_sem=send_sem.at[k],
            recv_sem=recv_sem.at[k],
            device_id=(peer, mp),
            device_id_type=MESH,
        )

    def start(k, carry):
        describe(k).start()
        return carry

    def finish(k, carry):
        describe(k).wait()
        return carry

    lax.fori_loop(1, n, start, 0)
    lax.fori_loop(1, n, finish, 0)
    own.wait()


def exchange(x, n, gather, collective_id):
    rows = x.shape[-2]
    block_bytes = rows * LANES * x.dtype.itemsize
    return pl.pallas_call(
        functools.partial(exchange_kernel, n, gather),
        out_shape=jax.ShapeDtypeStruct((n, rows, LANES), x.dtype),
        in_specs=[pl.BlockSpec(memory_space=pl.ANY)],
        out_specs=pl.BlockSpec(memory_space=pl.ANY),
        scratch_shapes=[
            pltpu.SemaphoreType.DMA((n,)),
            pltpu.SemaphoreType.DMA((n,)),
            pltpu.SemaphoreType.DMA(()),
        ],
        compiler_params=pltpu.CompilerParams(collective_id=collective_id, has_side_effects=True),
        cost_estimate=pl.CostEstimate(flops=0, bytes_accessed=2 * n * block_bytes, transcendentals=0),
    )(x)


def padded_rows(size, dtype_rows=16):
    rows = -(-size // LANES)
    return -(-rows // dtype_rows) * dtype_rows


def shard_sizes(w_qkv, w_proj, w_in, w_out, w_router, ln_gain, ln_bias):
    return [a.size for a in (w_qkv, w_proj, w_in, w_out, w_router, ln_gain, ln_bias)]


def gather_weights(w_qkv, w_proj, w_in, w_out, w_router, ln_gain, ln_bias, n):
    parts = (w_qkv, w_proj, w_in, w_out, w_router, ln_gain, ln_bias)
    flat = jnp.concatenate([a.reshape(-1) for a in parts])
    total = flat.shape[0]
    rows = padded_rows(total)
    flat = jnp.pad(flat, (0, rows * LANES - total)).reshape(rows, LANES)
    full = exchange(flat, n, True, 0).reshape(n, rows * LANES)
    pieces = []
    start = 0
    for a in parts:
        pieces.append(full[:, start:start + a.size])
        start += a.size
    q, p, i, o, r, g, b = pieces
    _, rq, cq, fq = w_qkv.shape
    gq = q.reshape(n * rq, cq, fq)
    _, fp, dp_ = w_proj.shape
    gp = p.reshape(n, fp, dp_).transpose(1, 0, 2).reshape(fp, n * dp_)
    _, ei, di, fi = w_in.shape
    gi = i.reshape(n, ei, di, fi).transpose(1, 0, 2, 3).reshape(ei, n * di, fi)
    _, eo, fo, do_ = w_out.shape
    go = o.reshape(n, eo, fo, do_).transpose(1, 2, 0, 3).reshape(eo, fo, n * do_)
    _, dr, er = w_router.shape
    gr = r.reshape(n * dr, er)
    _, two, dg = ln_gain.shape
    gg = g.reshape(n, two, dg).transpose(1, 0, 2).reshape(two, n * dg)
    gb = b.reshape(n, two, dg).transpose(1, 0, 2).reshape(two, n * dg)
    return (gq, gp, gi, go, gr, gg, gb)


def scatter_grads(grads, n, shapes):
    gq, gp, gi, go, gr, gg, gb = grads
    rows = [
        gq.reshape(n, -1),
        gp.reshape(gp.shape[0], n, -1).transpose(1, 0, 2).reshape(n, -1),
        gi.reshape(gi.shape[0], n, -1, gi.shape[2]).transpose(1, 0, 2, 3).reshape(n, -1),
        go.reshape(go.shape[0], go.shape[1], n, -1).transpose(2, 0, 1, 3).reshape(n, -1),
        gr.reshape(n, -1),
        gg.reshape(gg.shape[0], n, -1).transpose(1, 0, 2).reshape(n, -1),
        gb.reshape(gb.shape[0], n, -1).transpose(1, 0, 2).reshape(n, -1),
    ]
    packed = jnp.concatenate(rows, axis=1)
    total = packed.shape[1]
    count = padded_rows(total)
    packed = jnp.pad(packed, ((0, 0), (0, count * LANES - total))).reshape(n, count, LANES)
    received = exchange(packed.astype(jnp.bfloat16), n, False, 1)
    mine = jnp.sum(received.astype(jnp.float32), axis=0).reshape(-1)
    outs = []
    start = 0
    for shape in shapes:
        size = 1
        for s in shape:
            size *= s
        outs.append(mine[start:start + size].reshape(shape))
        start += size
    return outs


def layer_forward(field, chosen_ids, weights):
    w_qkv, w_proj, w_in, w_out, w_router, ln_gain, ln_bias = weights
    image_count, length, model_width = field.shape
    row_count = image_count * length
    head_count = w_qkv.shape[2] // HD
    score_scale = HD ** (-0.5)
    gain_rows = ln_gain.astype(jnp.float32)
    shift_rows = ln_bias.astype(jnp.float32)
    flat = field.reshape(row_count, model_width)
    first, normed_one, inverse_one = norm_forward(flat, gain_rows[0], shift_rows[0])
    first = first.astype(jnp.bfloat16)
    projected = jnp.einsum("rd,dcf->rcf", first, w_qkv, preferred_element_type=jnp.float32).astype(
        jnp.bfloat16
    )
    projected = projected.reshape(image_count, length, 3, head_count, HD)
    queries = projected[:, :, 0]
    key_rows = projected[:, :, 1]
    value_rows = projected[:, :, 2]
    scores = (
        jnp.einsum("bqhe,bkhe->bhqk", queries, key_rows, preferred_element_type=jnp.float32)
        * score_scale
    )
    log_total = jax.nn.logsumexp(scores, axis=-1)
    attn_weights = jnp.exp(scores - log_total[..., None]).astype(jnp.bfloat16)
    attended = jnp.einsum(
        "bhqk,bkhe->bqhe", attn_weights, value_rows, preferred_element_type=jnp.float32
    )
    attended = attended.astype(jnp.bfloat16).reshape(row_count, head_count * HD)
    partial_attn = jnp.dot(attended, w_proj, preferred_element_type=jnp.float32)
    hidden = flat + lax.psum(partial_attn, "mp")
    second, normed_two, inverse_two = norm_forward(hidden, gain_rows[1], shift_rows[1])
    second = second.astype(jnp.bfloat16)
    logits = jnp.dot(second, w_router, preferred_element_type=jnp.float32)
    router = jax.nn.softmax(logits, axis=-1)
    labels = jnp.arange(EXPERTS, dtype=jnp.int32)
    ids_flat = chosen_ids.reshape(row_count, TOPK)
    chosen = (ids_flat[:, :, None] == labels).astype(jnp.float32)
    gate_values = jnp.sum(router[:, None, :] * chosen, axis=-1)
    per_image = EXPERTS * CAP
    image_base = (jnp.arange(image_count, dtype=jnp.int32) * per_image)[:, None, None]
    slot_index = (chosen_ids * CAP + slot_positions(chosen_ids) + image_base).reshape(-1)
    owners = (
        jnp.full((image_count * per_image,), row_count, jnp.int32)
        .at[slot_index]
        .set(jnp.repeat(jnp.arange(row_count, dtype=jnp.int32), TOPK))
    )
    slot_gate = (
        jnp.zeros((image_count * per_image,), jnp.float32).at[slot_index].set(gate_values.reshape(-1))
    )
    padded = jnp.concatenate([second, jnp.zeros((1, model_width), jnp.bfloat16)], axis=0)
    slot_rows = jnp.take(padded, owners, axis=0).reshape(image_count, EXPERTS, CAP, model_width)
    inner_pre = jnp.einsum("becd,edf->becf", slot_rows, w_in, preferred_element_type=jnp.float32)
    activated = jax.nn.gelu(inner_pre, approximate=False).astype(jnp.bfloat16)
    produced = jnp.einsum("becf,efd->becd", activated, w_out, preferred_element_type=jnp.float32)
    produced = produced.reshape(image_count * per_image, model_width)
    picked = jnp.take(produced, slot_index, axis=0).reshape(row_count, TOPK, model_width)
    partial_moe = jnp.sum(gate_values[:, :, None] * picked, axis=1)
    output = hidden + lax.psum(partial_moe.astype(jnp.bfloat16), "mp").astype(jnp.float32)
    record = (
        normed_one, inverse_one, first, projected, log_total, attended, normed_two, inverse_two,
        second, router, chosen, slot_index, owners, slot_gate, slot_rows, inner_pre, activated, picked,
    )
    return (output.reshape(image_count, length, model_width), record)


def layer_backward(grad_field, record, weights):
    w_qkv, w_proj, w_in, w_out, w_router, ln_gain, ln_bias = weights
    (
        normed_one, inverse_one, first, projected, log_total, attended, normed_two, inverse_two,
        second, router, chosen, slot_index, owners, slot_gate, slot_rows, inner_pre, activated, picked,
    ) = record
    image_count, length, model_width = grad_field.shape
    row_count = image_count * length
    head_count = projected.shape[3]
    score_scale = HD ** (-0.5)
    gain_rows = ln_gain.astype(jnp.float32)
    grad_flat = grad_field.reshape(row_count, model_width)
    padded_grad = jnp.concatenate([grad_flat, jnp.zeros((1, model_width), jnp.float32)], axis=0)
    grad_slots = (jnp.take(padded_grad, owners, axis=0) * slot_gate[:, None]).astype(jnp.bfloat16)
    grad_slots = grad_slots.reshape(image_count, EXPERTS, CAP, model_width)
    grad_w_out = jnp.einsum(
        "becf,becd->efd", activated, grad_slots, preferred_element_type=jnp.float32
    )
    grad_act = jnp.einsum("becd,efd->becf", grad_slots, w_out, preferred_element_type=jnp.float32)
    grad_inner = (grad_act * gelu_slope(inner_pre)).astype(jnp.bfloat16)
    grad_w_in = jnp.einsum(
        "becd,becf->edf", slot_rows, grad_inner, preferred_element_type=jnp.float32
    )
    grad_slot_rows = jnp.einsum(
        "becf,edf->becd", grad_inner, w_in, preferred_element_type=jnp.float32
    )
    grad_slot_rows = grad_slot_rows.reshape(image_count * EXPERTS * CAP, model_width)
    partial_second = jnp.sum(
        jnp.take(grad_slot_rows, slot_index, axis=0).reshape(row_count, TOPK, model_width), axis=1
    )
    partial_gate = jnp.sum(picked * grad_flat[:, None, :], axis=-1)
    grad_second, grad_gate = lax.psum((partial_second, partial_gate), "mp")
    grad_router = jnp.sum(grad_gate[:, :, None] * chosen, axis=1)
    grad_logits = router * (grad_router - jnp.sum(router * grad_router, axis=-1, keepdims=True))
    grad_logits = grad_logits.astype(jnp.bfloat16)
    grad_w_router = jnp.dot(second.T, grad_logits, preferred_element_type=jnp.float32)
    grad_second = grad_second + jnp.dot(grad_logits, w_router.T, preferred_element_type=jnp.float32)
    grad_from_norm, grad_gain_two, grad_shift_two = norm_backward(
        grad_second, normed_two, inverse_two, gain_rows[1]
    )
    grad_hidden = grad_flat + grad_from_norm
    grad_hidden_low = grad_hidden.astype(jnp.bfloat16)
    grad_w_proj = jnp.dot(attended.T, grad_hidden_low, preferred_element_type=jnp.float32)
    grad_attended = jnp.dot(grad_hidden_low, w_proj.T, preferred_element_type=jnp.float32).astype(
        jnp.bfloat16
    )
    grad_attended = grad_attended.reshape(image_count, length, head_count, HD)
    queries = projected[:, :, 0]
    key_rows = projected[:, :, 1]
    value_rows = projected[:, :, 2]
    scores = (
        jnp.einsum("bqhe,bkhe->bhqk", queries, key_rows, preferred_element_type=jnp.float32)
        * score_scale
    )
    probs = jnp.exp(scores - log_total[..., None])
    grad_values = jnp.einsum(
        "bhqk,bqhe->bkhe", probs.astype(jnp.bfloat16), grad_attended,
        preferred_element_type=jnp.float32,
    )
    grad_probs = jnp.einsum(
        "bqhe,bkhe->bhqk", grad_attended, value_rows, preferred_element_type=jnp.float32
    )
    grad_scores = (
        probs * (grad_probs - jnp.sum(probs * grad_probs, axis=-1, keepdims=True))
    ).astype(jnp.bfloat16)
    grad_queries = (
        jnp.einsum("bhqk,bkhe->bqhe", grad_scores, key_rows, preferred_element_type=jnp.float32)
        * score_scale
    )
    grad_keys = (
        jnp.einsum("bhqk,bqhe->bkhe", grad_scores, queries, preferred_element_type=jnp.float32)
        * score_scale
    )
    grad_projected = jnp.stack([grad_queries, grad_keys, grad_values], axis=2).astype(jnp.bfloat16)
    grad_projected = grad_projected.reshape(row_count, 3, head_count * HD)
    grad_w_qkv = jnp.einsum(
        "rd,rcf->dcf", first, grad_projected, preferred_element_type=jnp.float32
    )
    partial_first = jnp.einsum(
        "rcf,dcf->rd", grad_projected, w_qkv, preferred_element_type=jnp.float32
    )
    grad_first = lax.psum(partial_first.astype(jnp.bfloat16), "mp").astype(jnp.float32)
    grad_input_norm, grad_gain_one, grad_shift_one = norm_backward(
        grad_first, normed_one, inverse_one, gain_rows[0]
    )
    grad_input = grad_hidden + grad_input_norm
    grads = (
        grad_w_qkv,
        grad_w_proj,
        grad_w_in,
        grad_w_out,
        grad_w_router,
        jnp.stack([grad_gain_one, grad_gain_two]),
        jnp.stack([grad_shift_one, grad_shift_two]),
    )
    return (grad_input.reshape(image_count, length, model_width), grads)


def make_local(n):
    def local(images, routes, w_qkv, w_proj, w_in, w_out, w_router, ln_gain, ln_bias, cotangent):
        shapes = [a.shape for a in (w_qkv, w_proj, w_in, w_out, w_router, ln_gain, ln_bias)]
        weights = gather_weights(w_qkv, w_proj, w_in, w_out, w_router, ln_gain, ln_bias, n)
        field = images.astype(jnp.float32)
        output, record = layer_forward(field, routes[0], weights)
        grad_input, grads = layer_backward(cotangent.astype(jnp.float32), record, weights)
        shards = scatter_grads(grads, n, [(1,) + tuple(s[1:]) for s in shapes])
        return (output, grad_input, *shards)

    return local


def solution(mesh):
    n = mesh.shape["dp"]
    in_specs = (
        P("dp", None, None),
        P(None, "dp", None, None),
        P(None, "dp", None, "mp"),
        P(None, "mp", "dp"),
        P(None, None, "dp", "mp"),
        P(None, None, "mp", "dp"),
        P(None, "dp", None),
        P(None, None, "dp"),
        P(None, None, "dp"),
        P("dp", None, None),
    )
    out_specs = (
        P("dp", None, None),
        P("dp", None, None),
        P(None, "dp", None, "mp"),
        P(None, "mp", "dp"),
        P(None, None, "dp", "mp"),
        P(None, None, "mp", "dp"),
        P(None, "dp", None),
        P(None, None, "dp"),
        P(None, None, "dp"),
    )
    return jax.shard_map(make_local(n), mesh=mesh, in_specs=in_specs, out_specs=out_specs, check_vma=False)
```

```python
import functools

import jax
import jax.numpy as jnp
from jax import lax
from jax.sharding import PartitionSpec as P
from jax.experimental import pallas as pl
from jax.experimental.pallas import tpu as pltpu

MESH = pl.DeviceIdType.MESH
LANES = 128

HD = 64
EXPERTS = 4
TOPK = 2
CAP = 104
EPSILON = 1e-06


def norm_forward(field, gain_row, shift_row):
    mean_value = jnp.mean(field, axis=-1, keepdims=True)
    centered = field - mean_value
    inverse = lax.rsqrt(jnp.mean(centered * centered, axis=-1, keepdims=True) + EPSILON)
    normed = centered * inverse
    return (normed * gain_row + shift_row, normed, inverse)


def norm_backward(grad_out, normed, inverse, gain_row):
    grad_gain = jnp.sum(grad_out * normed, axis=0)
    grad_shift = jnp.sum(grad_out, axis=0)
    scaled = grad_out * gain_row
    grad_in = inverse * (
        scaled
        - jnp.mean(scaled, axis=-1, keepdims=True)
        - normed * jnp.mean(scaled * normed, axis=-1, keepdims=True)
    )
    return (grad_in, grad_gain, grad_shift)


def slot_positions(chosen_ids):
    labels = jnp.arange(EXPERTS, dtype=jnp.int32)
    hit_counts = jnp.sum((chosen_ids[..., None] == labels).astype(jnp.int32), axis=-2)
    before = jnp.cumsum(hit_counts, axis=1) - hit_counts
    return jnp.take_along_axis(before, chosen_ids, axis=-1)


def gelu_slope(inner_pre):
    cumulative = 0.5 * (1.0 + jax.scipy.special.erf(inner_pre * 0.7071067811865476))
    density = jnp.exp(-0.5 * inner_pre * inner_pre) * 0.3989422804014327
    return cumulative + inner_pre * density


def group_of(kind):
    def chips():
        dp, mp = lax.axis_index("dp"), lax.axis_index("mp")
        return dp // 2, lambda i: (2 * i + dp % 2, mp)

    def cores():
        dp, mp = lax.axis_index("dp"), lax.axis_index("mp")
        return dp % 2, lambda i: (2 * (dp // 2) + i, mp)

    def pair():
        dp, mp = lax.axis_index("dp"), lax.axis_index("mp")
        return mp, lambda i: (dp, i)

    return {"chips": chips, "cores": cores, "pair": pair}[kind]


def exchange_kernel(m, gather, kind, x_ref, out_ref, send_sem, recv_sem, local_sem):
    me, device_of = group_of(kind)()
    barrier = pltpu.get_barrier_semaphore()

    def greet(k, carry):
        pl.semaphore_signal(
            barrier, inc=1, device_id=device_of(lax.rem(me + k, m)), device_id_type=MESH
        )
        return carry

    lax.fori_loop(1, m, greet, 0)
    pl.semaphore_wait(barrier, m - 1)
    own = pltpu.make_async_copy(x_ref if gather else x_ref.at[me], out_ref.at[me], local_sem)
    own.start()

    def describe(k):
        peer = lax.rem(me + k, m)
        return pltpu.make_async_remote_copy(
            src_ref=x_ref if gather else x_ref.at[peer],
            dst_ref=out_ref.at[me],
            send_sem=send_sem.at[k],
            recv_sem=recv_sem.at[k],
            device_id=device_of(peer),
            device_id_type=MESH,
        )

    def start(k, carry):
        describe(k).start()
        return carry

    def finish(k, carry):
        describe(k).wait()
        return carry

    lax.fori_loop(1, m, start, 0)
    lax.fori_loop(1, m, finish, 0)
    own.wait()


def exchange(x, m, gather, kind, collective_id):
    block = x.shape if gather else x.shape[1:]
    block_bytes = x.dtype.itemsize
    for d in block:
        block_bytes *= d
    return pl.pallas_call(
        functools.partial(exchange_kernel, m, gather, kind),
        out_shape=jax.ShapeDtypeStruct((m,) + tuple(block), x.dtype),
        in_specs=[pl.BlockSpec(memory_space=pl.ANY)],
        out_specs=pl.BlockSpec(memory_space=pl.ANY),
        scratch_shapes=[
            pltpu.SemaphoreType.DMA((m,)),
            pltpu.SemaphoreType.DMA((m,)),
            pltpu.SemaphoreType.DMA(()),
        ],
        compiler_params=pltpu.CompilerParams(collective_id=collective_id, has_side_effects=True),
        cost_estimate=pl.CostEstimate(flops=0, bytes_accessed=2 * m * block_bytes, transcendentals=0),
    )(x)


def padded_rows(size, dtype_rows=16):
    rows = -(-size // LANES)
    return -(-rows // dtype_rows) * dtype_rows


def shard_sizes(w_qkv, w_proj, w_in, w_out, w_router, ln_gain, ln_bias):
    return [a.size for a in (w_qkv, w_proj, w_in, w_out, w_router, ln_gain, ln_bias)]


def gather_weights(w_qkv, w_proj, w_in, w_out, w_router, ln_gain, ln_bias, n):
    parts = (w_qkv, w_proj, w_in, w_out, w_router, ln_gain, ln_bias)
    flat = jnp.concatenate([a.reshape(-1) for a in parts])
    total = flat.shape[0]
    rows = padded_rows(total)
    flat = jnp.pad(flat, (0, rows * LANES - total)).reshape(rows, LANES)
    same_core = exchange(flat, n // 2, True, "chips", 0)
    both = exchange(same_core, 2, True, "cores", 1)
    full = both.transpose(1, 0, 2, 3).reshape(n, rows * LANES)
    pieces = []
    start = 0
    for a in parts:
        pieces.append(full[:, start:start + a.size])
        start += a.size
    q, p, i, o, r, g, b = pieces
    _, rq, cq, fq = w_qkv.shape
    gq = q.reshape(n * rq, cq, fq)
    _, fp, dp_ = w_proj.shape
    gp = p.reshape(n, fp, dp_).transpose(1, 0, 2).reshape(fp, n * dp_)
    _, ei, di, fi = w_in.shape
    gi = i.reshape(n, ei, di, fi).transpose(1, 0, 2, 3).reshape(ei, n * di, fi)
    _, eo, fo, do_ = w_out.shape
    go = o.reshape(n, eo, fo, do_).transpose(1, 2, 0, 3).reshape(eo, fo, n * do_)
    _, dr, er = w_router.shape
    gr = r.reshape(n * dr, er)
    _, two, dg = ln_gain.shape
    gg = g.reshape(n, two, dg).transpose(1, 0, 2).reshape(two, n * dg)
    gb = b.reshape(n, two, dg).transpose(1, 0, 2).reshape(two, n * dg)
    return (gq, gp, gi, go, gr, gg, gb)


def scatter_grads(grads, n, shapes):
    gq, gp, gi, go, gr, gg, gb = grads
    rows = [
        gq.reshape(n, -1),
        gp.reshape(gp.shape[0], n, -1).transpose(1, 0, 2).reshape(n, -1),
        gi.reshape(gi.shape[0], n, -1, gi.shape[2]).transpose(1, 0, 2, 3).reshape(n, -1),
        go.reshape(go.shape[0], go.shape[1], n, -1).transpose(2, 0, 1, 3).reshape(n, -1),
        gr.reshape(n, -1),
        gg.reshape(gg.shape[0], n, -1).transpose(1, 0, 2).reshape(n, -1),
        gb.reshape(gb.shape[0], n, -1).transpose(1, 0, 2).reshape(n, -1),
    ]
    packed = jnp.concatenate(rows, axis=1)
    total = packed.shape[1]
    count = padded_rows(total)
    packed = jnp.pad(packed, ((0, 0), (0, count * LANES - total))).reshape(n, count, LANES)
    by_core = packed.astype(jnp.bfloat16).reshape(n // 2, 2, count, LANES).transpose(1, 0, 2, 3)
    halves = exchange(by_core, 2, False, "cores", 2).astype(jnp.float32)
    chip_sum = (halves[0] + halves[1]).astype(jnp.bfloat16)
    received = exchange(chip_sum, n // 2, False, "chips", 3)
    mine = jnp.sum(received.astype(jnp.float32), axis=0).reshape(-1)
    outs = []
    start = 0
    for shape in shapes:
        size = 1
        for s in shape:
            size *= s
        outs.append(mine[start:start + size].reshape(shape))
        start += size
    return outs


def layer_forward(field, chosen_ids, weights):
    w_qkv, w_proj, w_in, w_out, w_router, ln_gain, ln_bias = weights
    image_count, length, model_width = field.shape
    row_count = image_count * length
    head_count = w_qkv.shape[2] // HD
    score_scale = HD ** (-0.5)
    gain_rows = ln_gain.astype(jnp.float32)
    shift_rows = ln_bias.astype(jnp.float32)
    flat = field.reshape(row_count, model_width)
    first, normed_one, inverse_one = norm_forward(flat, gain_rows[0], shift_rows[0])
    first = first.astype(jnp.bfloat16)
    projected = jnp.einsum("rd,dcf->rcf", first, w_qkv, preferred_element_type=jnp.float32).astype(
        jnp.bfloat16
    )
    projected = projected.reshape(image_count, length, 3, head_count, HD)
    queries = projected[:, :, 0]
    key_rows = projected[:, :, 1]
    value_rows = projected[:, :, 2]
    scores = (
        jnp.einsum("bqhe,bkhe->bhqk", queries, key_rows, preferred_element_type=jnp.float32)
        * score_scale
    )
    log_total = jax.nn.logsumexp(scores, axis=-1)
    attn_weights = jnp.exp(scores - log_total[..., None]).astype(jnp.bfloat16)
    attended = jnp.einsum(
        "bhqk,bkhe->bqhe", attn_weights, value_rows, preferred_element_type=jnp.float32
    )
    attended = attended.astype(jnp.bfloat16).reshape(row_count, head_count * HD)
    partial_attn = jnp.dot(attended, w_proj, preferred_element_type=jnp.float32)
    hidden = flat + lax.psum(partial_attn, "mp")
    second, normed_two, inverse_two = norm_forward(hidden, gain_rows[1], shift_rows[1])
    second = second.astype(jnp.bfloat16)
    logits = jnp.dot(second, w_router, preferred_element_type=jnp.float32)
    router = jax.nn.softmax(logits, axis=-1)
    labels = jnp.arange(EXPERTS, dtype=jnp.int32)
    ids_flat = chosen_ids.reshape(row_count, TOPK)
    chosen = (ids_flat[:, :, None] == labels).astype(jnp.float32)
    gate_values = jnp.sum(router[:, None, :] * chosen, axis=-1)
    per_image = EXPERTS * CAP
    image_base = (jnp.arange(image_count, dtype=jnp.int32) * per_image)[:, None, None]
    slot_index = (chosen_ids * CAP + slot_positions(chosen_ids) + image_base).reshape(-1)
    owners = (
        jnp.full((image_count * per_image,), row_count, jnp.int32)
        .at[slot_index]
        .set(jnp.repeat(jnp.arange(row_count, dtype=jnp.int32), TOPK))
    )
    slot_gate = (
        jnp.zeros((image_count * per_image,), jnp.float32).at[slot_index].set(gate_values.reshape(-1))
    )
    padded = jnp.concatenate([second, jnp.zeros((1, model_width), jnp.bfloat16)], axis=0)
    slot_rows = jnp.take(padded, owners, axis=0).reshape(image_count, EXPERTS, CAP, model_width)
    inner_pre = jnp.einsum("becd,edf->becf", slot_rows, w_in, preferred_element_type=jnp.float32)
    activated = jax.nn.gelu(inner_pre, approximate=False).astype(jnp.bfloat16)
    produced = jnp.einsum("becf,efd->becd", activated, w_out, preferred_element_type=jnp.float32)
    produced = produced.reshape(image_count * per_image, model_width)
    picked = jnp.take(produced, slot_index, axis=0).reshape(row_count, TOPK, model_width)
    partial_moe = jnp.sum(gate_values[:, :, None] * picked, axis=1)
    output = hidden + lax.psum(partial_moe.astype(jnp.bfloat16), "mp").astype(jnp.float32)
    record = (
        normed_one, inverse_one, first, projected, log_total, attended, normed_two, inverse_two,
        second, router, chosen, slot_index, owners, slot_gate, slot_rows, inner_pre, activated, picked,
    )
    return (output.reshape(image_count, length, model_width), record)


def layer_backward(grad_field, record, weights):
    w_qkv, w_proj, w_in, w_out, w_router, ln_gain, ln_bias = weights
    (
        normed_one, inverse_one, first, projected, log_total, attended, normed_two, inverse_two,
        second, router, chosen, slot_index, owners, slot_gate, slot_rows, inner_pre, activated, picked,
    ) = record
    image_count, length, model_width = grad_field.shape
    row_count = image_count * length
    head_count = projected.shape[3]
    score_scale = HD ** (-0.5)
    gain_rows = ln_gain.astype(jnp.float32)
    grad_flat = grad_field.reshape(row_count, model_width)
    padded_grad = jnp.concatenate([grad_flat, jnp.zeros((1, model_width), jnp.float32)], axis=0)
    grad_slots = (jnp.take(padded_grad, owners, axis=0) * slot_gate[:, None]).astype(jnp.bfloat16)
    grad_slots = grad_slots.reshape(image_count, EXPERTS, CAP, model_width)
    grad_w_out = jnp.einsum(
        "becf,becd->efd", activated, grad_slots, preferred_element_type=jnp.float32
    )
    grad_act = jnp.einsum("becd,efd->becf", grad_slots, w_out, preferred_element_type=jnp.float32)
    grad_inner = (grad_act * gelu_slope(inner_pre)).astype(jnp.bfloat16)
    grad_w_in = jnp.einsum(
        "becd,becf->edf", slot_rows, grad_inner, preferred_element_type=jnp.float32
    )
    grad_slot_rows = jnp.einsum(
        "becf,edf->becd", grad_inner, w_in, preferred_element_type=jnp.float32
    )
    grad_slot_rows = grad_slot_rows.reshape(image_count * EXPERTS * CAP, model_width)
    partial_second = jnp.sum(
        jnp.take(grad_slot_rows, slot_index, axis=0).reshape(row_count, TOPK, model_width), axis=1
    )
    partial_gate = jnp.sum(picked * grad_flat[:, None, :], axis=-1)
    grad_second, grad_gate = lax.psum((partial_second, partial_gate), "mp")
    grad_router = jnp.sum(grad_gate[:, :, None] * chosen, axis=1)
    grad_logits = router * (grad_router - jnp.sum(router * grad_router, axis=-1, keepdims=True))
    grad_logits = grad_logits.astype(jnp.bfloat16)
    grad_w_router = jnp.dot(second.T, grad_logits, preferred_element_type=jnp.float32)
    grad_second = grad_second + jnp.dot(grad_logits, w_router.T, preferred_element_type=jnp.float32)
    grad_from_norm, grad_gain_two, grad_shift_two = norm_backward(
        grad_second, normed_two, inverse_two, gain_rows[1]
    )
    grad_hidden = grad_flat + grad_from_norm
    grad_hidden_low = grad_hidden.astype(jnp.bfloat16)
    grad_w_proj = jnp.dot(attended.T, grad_hidden_low, preferred_element_type=jnp.float32)
    grad_attended = jnp.dot(grad_hidden_low, w_proj.T, preferred_element_type=jnp.float32).astype(
        jnp.bfloat16
    )
    grad_attended = grad_attended.reshape(image_count, length, head_count, HD)
    queries = projected[:, :, 0]
    key_rows = projected[:, :, 1]
    value_rows = projected[:, :, 2]
    scores = (
        jnp.einsum("bqhe,bkhe->bhqk", queries, key_rows, preferred_element_type=jnp.float32)
        * score_scale
    )
    probs = jnp.exp(scores - log_total[..., None])
    grad_values = jnp.einsum(
        "bhqk,bqhe->bkhe", probs.astype(jnp.bfloat16), grad_attended,
        preferred_element_type=jnp.float32,
    )
    grad_probs = jnp.einsum(
        "bqhe,bkhe->bhqk", grad_attended, value_rows, preferred_element_type=jnp.float32
    )
    grad_scores = (
        probs * (grad_probs - jnp.sum(probs * grad_probs, axis=-1, keepdims=True))
    ).astype(jnp.bfloat16)
    grad_queries = (
        jnp.einsum("bhqk,bkhe->bqhe", grad_scores, key_rows, preferred_element_type=jnp.float32)
        * score_scale
    )
    grad_keys = (
        jnp.einsum("bhqk,bqhe->bkhe", grad_scores, queries, preferred_element_type=jnp.float32)
        * score_scale
    )
    grad_projected = jnp.stack([grad_queries, grad_keys, grad_values], axis=2).astype(jnp.bfloat16)
    grad_projected = grad_projected.reshape(row_count, 3, head_count * HD)
    grad_w_qkv = jnp.einsum(
        "rd,rcf->dcf", first, grad_projected, preferred_element_type=jnp.float32
    )
    partial_first = jnp.einsum(
        "rcf,dcf->rd", grad_projected, w_qkv, preferred_element_type=jnp.float32
    )
    grad_first = lax.psum(partial_first.astype(jnp.bfloat16), "mp").astype(jnp.float32)
    grad_input_norm, grad_gain_one, grad_shift_one = norm_backward(
        grad_first, normed_one, inverse_one, gain_rows[0]
    )
    grad_input = grad_hidden + grad_input_norm
    grads = (
        grad_w_qkv,
        grad_w_proj,
        grad_w_in,
        grad_w_out,
        grad_w_router,
        jnp.stack([grad_gain_one, grad_gain_two]),
        jnp.stack([grad_shift_one, grad_shift_two]),
    )
    return (grad_input.reshape(image_count, length, model_width), grads)


def make_local(n):
    def local(images, routes, w_qkv, w_proj, w_in, w_out, w_router, ln_gain, ln_bias, cotangent):
        shapes = [a.shape for a in (w_qkv, w_proj, w_in, w_out, w_router, ln_gain, ln_bias)]
        weights = gather_weights(w_qkv, w_proj, w_in, w_out, w_router, ln_gain, ln_bias, n)
        field = images.astype(jnp.float32)
        output, record = layer_forward(field, routes[0], weights)
        grad_input, grads = layer_backward(cotangent.astype(jnp.float32), record, weights)
        shards = scatter_grads(grads, n, [(1,) + tuple(s[1:]) for s in shapes])
        return (output, grad_input, *shards)

    return local


def solution(mesh):
    n = mesh.shape["dp"]
    in_specs = (
        P("dp", None, None),
        P(None, "dp", None, None),
        P(None, "dp", None, "mp"),
        P(None, "mp", "dp"),
        P(None, None, "dp", "mp"),
        P(None, None, "mp", "dp"),
        P(None, "dp", None),
        P(None, None, "dp"),
        P(None, None, "dp"),
        P("dp", None, None),
    )
    out_specs = (
        P("dp", None, None),
        P("dp", None, None),
        P(None, "dp", None, "mp"),
        P(None, "mp", "dp"),
        P(None, None, "dp", "mp"),
        P(None, None, "mp", "dp"),
        P(None, "dp", None),
        P(None, None, "dp"),
        P(None, None, "dp"),
    )
    return jax.shard_map(make_local(n), mesh=mesh, in_specs=in_specs, out_specs=out_specs, check_vma=False)
```

```python
import functools

import jax
import jax.numpy as jnp
from jax import lax
from jax.sharding import PartitionSpec as P
from jax.experimental import pallas as pl
from jax.experimental.pallas import tpu as pltpu

MESH = pl.DeviceIdType.MESH
LANES = 128

HD = 64
EXPERTS = 4
TOPK = 2
CAP = 104
EPSILON = 1e-06


def norm_forward(field, gain_row, shift_row):
    mean_value = jnp.mean(field, axis=-1, keepdims=True)
    centered = field - mean_value
    inverse = lax.rsqrt(jnp.mean(centered * centered, axis=-1, keepdims=True) + EPSILON)
    normed = centered * inverse
    return (normed * gain_row + shift_row, normed, inverse)


def norm_backward(grad_out, normed, inverse, gain_row):
    grad_gain = jnp.sum(grad_out * normed, axis=0)
    grad_shift = jnp.sum(grad_out, axis=0)
    scaled = grad_out * gain_row
    grad_in = inverse * (
        scaled
        - jnp.mean(scaled, axis=-1, keepdims=True)
        - normed * jnp.mean(scaled * normed, axis=-1, keepdims=True)
    )
    return (grad_in, grad_gain, grad_shift)


def slot_positions(chosen_ids):
    labels = jnp.arange(EXPERTS, dtype=jnp.int32)
    hit_counts = jnp.sum((chosen_ids[..., None] == labels).astype(jnp.int32), axis=-2)
    before = jnp.cumsum(hit_counts, axis=1) - hit_counts
    return jnp.take_along_axis(before, chosen_ids, axis=-1)


def gelu_slope(inner_pre):
    cumulative = 0.5 * (1.0 + jax.scipy.special.erf(inner_pre * 0.7071067811865476))
    density = jnp.exp(-0.5 * inner_pre * inner_pre) * 0.3989422804014327
    return cumulative + inner_pre * density


def group_of(kind):
    def chips():
        dp, mp = lax.axis_index("dp"), lax.axis_index("mp")
        return dp // 2, lambda i: (2 * i + dp % 2, mp)

    def cores():
        dp, mp = lax.axis_index("dp"), lax.axis_index("mp")
        return dp % 2, lambda i: (2 * (dp // 2) + i, mp)

    def pair():
        dp, mp = lax.axis_index("dp"), lax.axis_index("mp")
        return mp, lambda i: (dp, i)

    return {"chips": chips, "cores": cores, "pair": pair}[kind]


def exchange_kernel(m, pieces, gather, kind, x_ref, out_ref, send_sem, recv_sem, local_sem):
    me, device_of = group_of(kind)()
    step = out_ref.shape[1] // pieces
    barrier = pltpu.get_barrier_semaphore()

    def greet(k, carry):
        pl.semaphore_signal(
            barrier, inc=1, device_id=device_of(lax.rem(me + k, m)), device_id_type=MESH
        )
        return carry

    lax.fori_loop(1, m, greet, 0)
    pl.semaphore_wait(barrier, m - 1)
    own = pltpu.make_async_copy(x_ref if gather else x_ref.at[me], out_ref.at[me], local_sem)
    own.start()

    def describe(t):
        k = 1 + t // pieces
        part = pl.ds(pl.multiple_of((t % pieces) * step, step), step)
        peer = lax.rem(me + k, m)
        return pltpu.make_async_remote_copy(
            src_ref=x_ref.at[part] if gather else x_ref.at[peer, part],
            dst_ref=out_ref.at[me, part],
            send_sem=send_sem.at[t],
            recv_sem=recv_sem.at[t],
            device_id=device_of(peer),
            device_id_type=MESH,
        )

    def start(t, carry):
        describe(t).start()
        return carry

    def finish(t, carry):
        describe(t).wait()
        return carry

    count = (m - 1) * pieces
    lax.fori_loop(0, count, start, 0)
    lax.fori_loop(0, count, finish, 0)
    own.wait()


def exchange(x, m, gather, kind, collective_id, pieces=1):
    block = x.shape if gather else x.shape[1:]
    block_bytes = x.dtype.itemsize
    for d in block:
        block_bytes *= d
    count = (m - 1) * pieces
    return pl.pallas_call(
        functools.partial(exchange_kernel, m, pieces, gather, kind),
        out_shape=jax.ShapeDtypeStruct((m,) + tuple(block), x.dtype),
        in_specs=[pl.BlockSpec(memory_space=pl.ANY)],
        out_specs=pl.BlockSpec(memory_space=pl.ANY),
        scratch_shapes=[
            pltpu.SemaphoreType.DMA((count,)),
            pltpu.SemaphoreType.DMA((count,)),
            pltpu.SemaphoreType.DMA(()),
        ],
        compiler_params=pltpu.CompilerParams(collective_id=collective_id, has_side_effects=True),
        cost_estimate=pl.CostEstimate(flops=0, bytes_accessed=2 * m * block_bytes, transcendentals=0),
    )(x)


def padded_rows(size, dtype_rows=16):
    rows = -(-size // LANES)
    return -(-rows // dtype_rows) * dtype_rows


def shard_sizes(w_qkv, w_proj, w_in, w_out, w_router, ln_gain, ln_bias):
    return [a.size for a in (w_qkv, w_proj, w_in, w_out, w_router, ln_gain, ln_bias)]


def gather_weights(w_qkv, w_proj, w_in, w_out, w_router, ln_gain, ln_bias, n):
    parts = (w_qkv, w_proj, w_in, w_out, w_router, ln_gain, ln_bias)
    flat = jnp.concatenate([a.reshape(-1) for a in parts])
    total = flat.shape[0]
    rows = padded_rows(total)
    flat = jnp.pad(flat, (0, rows * LANES - total)).reshape(rows, LANES)
    same_core = exchange(flat, n // 2, True, "chips", 0)
    both = exchange(same_core, 2, True, "cores", 1, pieces=16)
    full = both.transpose(1, 0, 2, 3).reshape(n, rows * LANES)
    pieces = []
    start = 0
    for a in parts:
        pieces.append(full[:, start:start + a.size])
        start += a.size
    q, p, i, o, r, g, b = pieces
    _, rq, cq, fq = w_qkv.shape
    gq = q.reshape(n * rq, cq, fq)
    _, fp, dp_ = w_proj.shape
    gp = p.reshape(n, fp, dp_).transpose(1, 0, 2).reshape(fp, n * dp_)
    _, ei, di, fi = w_in.shape
    gi = i.reshape(n, ei, di, fi).transpose(1, 0, 2, 3).reshape(ei, n * di, fi)
    _, eo, fo, do_ = w_out.shape
    go = o.reshape(n, eo, fo, do_).transpose(1, 2, 0, 3).reshape(eo, fo, n * do_)
    _, dr, er = w_router.shape
    gr = r.reshape(n * dr, er)
    _, two, dg = ln_gain.shape
    gg = g.reshape(n, two, dg).transpose(1, 0, 2).reshape(two, n * dg)
    gb = b.reshape(n, two, dg).transpose(1, 0, 2).reshape(two, n * dg)
    return (gq, gp, gi, go, gr, gg, gb)


def scatter_grads(grads, n, shapes):
    gq, gp, gi, go, gr, gg, gb = grads
    rows = [
        gq.reshape(n, -1),
        gp.reshape(gp.shape[0], n, -1).transpose(1, 0, 2).reshape(n, -1),
        gi.reshape(gi.shape[0], n, -1, gi.shape[2]).transpose(1, 0, 2, 3).reshape(n, -1),
        go.reshape(go.shape[0], go.shape[1], n, -1).transpose(2, 0, 1, 3).reshape(n, -1),
        gr.reshape(n, -1),
        gg.reshape(gg.shape[0], n, -1).transpose(1, 0, 2).reshape(n, -1),
        gb.reshape(gb.shape[0], n, -1).transpose(1, 0, 2).reshape(n, -1),
    ]
    packed = jnp.concatenate(rows, axis=1)
    total = packed.shape[1]
    count = padded_rows(total)
    packed = jnp.pad(packed, ((0, 0), (0, count * LANES - total))).reshape(n, count, LANES)
    by_core = packed.astype(jnp.bfloat16).reshape(n // 2, 2, count, LANES).transpose(1, 0, 2, 3)
    halves = exchange(by_core, 2, False, "cores", 2, pieces=16).astype(jnp.float32)
    chip_sum = (halves[0] + halves[1]).astype(jnp.bfloat16)
    received = exchange(chip_sum, n // 2, False, "chips", 3)
    mine = jnp.sum(received.astype(jnp.float32), axis=0).reshape(-1)
    outs = []
    start = 0
    for shape in shapes:
        size = 1
        for s in shape:
            size *= s
        outs.append(mine[start:start + size].reshape(shape))
        start += size
    return outs


def layer_forward(field, chosen_ids, weights):
    w_qkv, w_proj, w_in, w_out, w_router, ln_gain, ln_bias = weights
    image_count, length, model_width = field.shape
    row_count = image_count * length
    head_count = w_qkv.shape[2] // HD
    score_scale = HD ** (-0.5)
    gain_rows = ln_gain.astype(jnp.float32)
    shift_rows = ln_bias.astype(jnp.float32)
    flat = field.reshape(row_count, model_width)
    first, normed_one, inverse_one = norm_forward(flat, gain_rows[0], shift_rows[0])
    first = first.astype(jnp.bfloat16)
    projected = jnp.einsum("rd,dcf->rcf", first, w_qkv, preferred_element_type=jnp.float32).astype(
        jnp.bfloat16
    )
    projected = projected.reshape(image_count, length, 3, head_count, HD)
    queries = projected[:, :, 0]
    key_rows = projected[:, :, 1]
    value_rows = projected[:, :, 2]
    scores = (
        jnp.einsum("bqhe,bkhe->bhqk", queries, key_rows, preferred_element_type=jnp.float32)
        * score_scale
    )
    log_total = jax.nn.logsumexp(scores, axis=-1)
    attn_weights = jnp.exp(scores - log_total[..., None]).astype(jnp.bfloat16)
    attended = jnp.einsum(
        "bhqk,bkhe->bqhe", attn_weights, value_rows, preferred_element_type=jnp.float32
    )
    attended = attended.astype(jnp.bfloat16).reshape(row_count, head_count * HD)
    partial_attn = jnp.dot(attended, w_proj, preferred_element_type=jnp.float32)
    hidden = flat + lax.psum(partial_attn, "mp")
    second, normed_two, inverse_two = norm_forward(hidden, gain_rows[1], shift_rows[1])
    second = second.astype(jnp.bfloat16)
    logits = jnp.dot(second, w_router, preferred_element_type=jnp.float32)
    router = jax.nn.softmax(logits, axis=-1)
    labels = jnp.arange(EXPERTS, dtype=jnp.int32)
    ids_flat = chosen_ids.reshape(row_count, TOPK)
    chosen = (ids_flat[:, :, None] == labels).astype(jnp.float32)
    gate_values = jnp.sum(router[:, None, :] * chosen, axis=-1)
    per_image = EXPERTS * CAP
    image_base = (jnp.arange(image_count, dtype=jnp.int32) * per_image)[:, None, None]
    slot_index = (chosen_ids * CAP + slot_positions(chosen_ids) + image_base).reshape(-1)
    owners = (
        jnp.full((image_count * per_image,), row_count, jnp.int32)
        .at[slot_index]
        .set(jnp.repeat(jnp.arange(row_count, dtype=jnp.int32), TOPK))
    )
    slot_gate = (
        jnp.zeros((image_count * per_image,), jnp.float32).at[slot_index].set(gate_values.reshape(-1))
    )
    padded = jnp.concatenate([second, jnp.zeros((1, model_width), jnp.bfloat16)], axis=0)
    slot_rows = jnp.take(padded, owners, axis=0).reshape(image_count, EXPERTS, CAP, model_width)
    inner_pre = jnp.einsum("becd,edf->becf", slot_rows, w_in, preferred_element_type=jnp.float32)
    activated = jax.nn.gelu(inner_pre, approximate=False).astype(jnp.bfloat16)
    produced = jnp.einsum("becf,efd->becd", activated, w_out, preferred_element_type=jnp.float32)
    produced = produced.reshape(image_count * per_image, model_width)
    picked = jnp.take(produced, slot_index, axis=0).reshape(row_count, TOPK, model_width)
    partial_moe = jnp.sum(gate_values[:, :, None] * picked, axis=1)
    output = hidden + lax.psum(partial_moe.astype(jnp.bfloat16), "mp").astype(jnp.float32)
    record = (
        normed_one, inverse_one, first, projected, log_total, attended, normed_two, inverse_two,
        second, router, chosen, slot_index, owners, slot_gate, slot_rows, inner_pre, activated, picked,
    )
    return (output.reshape(image_count, length, model_width), record)


def layer_backward(grad_field, record, weights):
    w_qkv, w_proj, w_in, w_out, w_router, ln_gain, ln_bias = weights
    (
        normed_one, inverse_one, first, projected, log_total, attended, normed_two, inverse_two,
        second, router, chosen, slot_index, owners, slot_gate, slot_rows, inner_pre, activated, picked,
    ) = record
    image_count, length, model_width = grad_field.shape
    row_count = image_count * length
    head_count = projected.shape[3]
    score_scale = HD ** (-0.5)
    gain_rows = ln_gain.astype(jnp.float32)
    grad_flat = grad_field.reshape(row_count, model_width)
    padded_grad = jnp.concatenate([grad_flat, jnp.zeros((1, model_width), jnp.float32)], axis=0)
    grad_slots = (jnp.take(padded_grad, owners, axis=0) * slot_gate[:, None]).astype(jnp.bfloat16)
    grad_slots = grad_slots.reshape(image_count, EXPERTS, CAP, model_width)
    grad_w_out = jnp.einsum(
        "becf,becd->efd", activated, grad_slots, preferred_element_type=jnp.float32
    )
    grad_act = jnp.einsum("becd,efd->becf", grad_slots, w_out, preferred_element_type=jnp.float32)
    grad_inner = (grad_act * gelu_slope(inner_pre)).astype(jnp.bfloat16)
    grad_w_in = jnp.einsum(
        "becd,becf->edf", slot_rows, grad_inner, preferred_element_type=jnp.float32
    )
    grad_slot_rows = jnp.einsum(
        "becf,edf->becd", grad_inner, w_in, preferred_element_type=jnp.float32
    )
    grad_slot_rows = grad_slot_rows.reshape(image_count * EXPERTS * CAP, model_width)
    partial_second = jnp.sum(
        jnp.take(grad_slot_rows, slot_index, axis=0).reshape(row_count, TOPK, model_width), axis=1
    )
    partial_gate = jnp.sum(picked * grad_flat[:, None, :], axis=-1)
    grad_second, grad_gate = lax.psum((partial_second, partial_gate), "mp")
    grad_router = jnp.sum(grad_gate[:, :, None] * chosen, axis=1)
    grad_logits = router * (grad_router - jnp.sum(router * grad_router, axis=-1, keepdims=True))
    grad_logits = grad_logits.astype(jnp.bfloat16)
    grad_w_router = jnp.dot(second.T, grad_logits, preferred_element_type=jnp.float32)
    grad_second = grad_second + jnp.dot(grad_logits, w_router.T, preferred_element_type=jnp.float32)
    grad_from_norm, grad_gain_two, grad_shift_two = norm_backward(
        grad_second, normed_two, inverse_two, gain_rows[1]
    )
    grad_hidden = grad_flat + grad_from_norm
    grad_hidden_low = grad_hidden.astype(jnp.bfloat16)
    grad_w_proj = jnp.dot(attended.T, grad_hidden_low, preferred_element_type=jnp.float32)
    grad_attended = jnp.dot(grad_hidden_low, w_proj.T, preferred_element_type=jnp.float32).astype(
        jnp.bfloat16
    )
    grad_attended = grad_attended.reshape(image_count, length, head_count, HD)
    queries = projected[:, :, 0]
    key_rows = projected[:, :, 1]
    value_rows = projected[:, :, 2]
    scores = (
        jnp.einsum("bqhe,bkhe->bhqk", queries, key_rows, preferred_element_type=jnp.float32)
        * score_scale
    )
    probs = jnp.exp(scores - log_total[..., None])
    grad_values = jnp.einsum(
        "bhqk,bqhe->bkhe", probs.astype(jnp.bfloat16), grad_attended,
        preferred_element_type=jnp.float32,
    )
    grad_probs = jnp.einsum(
        "bqhe,bkhe->bhqk", grad_attended, value_rows, preferred_element_type=jnp.float32
    )
    grad_scores = (
        probs * (grad_probs - jnp.sum(probs * grad_probs, axis=-1, keepdims=True))
    ).astype(jnp.bfloat16)
    grad_queries = (
        jnp.einsum("bhqk,bkhe->bqhe", grad_scores, key_rows, preferred_element_type=jnp.float32)
        * score_scale
    )
    grad_keys = (
        jnp.einsum("bhqk,bqhe->bkhe", grad_scores, queries, preferred_element_type=jnp.float32)
        * score_scale
    )
    grad_projected = jnp.stack([grad_queries, grad_keys, grad_values], axis=2).astype(jnp.bfloat16)
    grad_projected = grad_projected.reshape(row_count, 3, head_count * HD)
    grad_w_qkv = jnp.einsum(
        "rd,rcf->dcf", first, grad_projected, preferred_element_type=jnp.float32
    )
    partial_first = jnp.einsum(
        "rcf,dcf->rd", grad_projected, w_qkv, preferred_element_type=jnp.float32
    )
    grad_first = lax.psum(partial_first.astype(jnp.bfloat16), "mp").astype(jnp.float32)
    grad_input_norm, grad_gain_one, grad_shift_one = norm_backward(
        grad_first, normed_one, inverse_one, gain_rows[0]
    )
    grad_input = grad_hidden + grad_input_norm
    grads = (
        grad_w_qkv,
        grad_w_proj,
        grad_w_in,
        grad_w_out,
        grad_w_router,
        jnp.stack([grad_gain_one, grad_gain_two]),
        jnp.stack([grad_shift_one, grad_shift_two]),
    )
    return (grad_input.reshape(image_count, length, model_width), grads)


def make_local(n):
    def local(images, routes, w_qkv, w_proj, w_in, w_out, w_router, ln_gain, ln_bias, cotangent):
        shapes = [a.shape for a in (w_qkv, w_proj, w_in, w_out, w_router, ln_gain, ln_bias)]
        weights = gather_weights(w_qkv, w_proj, w_in, w_out, w_router, ln_gain, ln_bias, n)
        field = images.astype(jnp.float32)
        output, record = layer_forward(field, routes[0], weights)
        grad_input, grads = layer_backward(cotangent.astype(jnp.float32), record, weights)
        shards = scatter_grads(grads, n, [(1,) + tuple(s[1:]) for s in shapes])
        return (output, grad_input, *shards)

    return local


def solution(mesh):
    n = mesh.shape["dp"]
    in_specs = (
        P("dp", None, None),
        P(None, "dp", None, None),
        P(None, "dp", None, "mp"),
        P(None, "mp", "dp"),
        P(None, None, "dp", "mp"),
        P(None, None, "mp", "dp"),
        P(None, "dp", None),
        P(None, None, "dp"),
        P(None, None, "dp"),
        P("dp", None, None),
    )
    out_specs = (
        P("dp", None, None),
        P("dp", None, None),
        P(None, "dp", None, "mp"),
        P(None, "mp", "dp"),
        P(None, None, "dp", "mp"),
        P(None, None, "mp", "dp"),
        P(None, "dp", None),
        P(None, None, "dp"),
        P(None, None, "dp"),
    )
    return jax.shard_map(make_local(n), mesh=mesh, in_specs=in_specs, out_specs=out_specs, check_vma=False)
```

```python
import functools

import jax
import jax.numpy as jnp
from jax import lax
from jax.sharding import PartitionSpec as P
from jax.experimental import pallas as pl
from jax.experimental.pallas import tpu as pltpu

MESH = pl.DeviceIdType.MESH
LANES = 128

HD = 64
EXPERTS = 4
TOPK = 2
CAP = 104
EPSILON = 1e-06


def norm_forward(field, gain_row, shift_row):
    mean_value = jnp.mean(field, axis=-1, keepdims=True)
    centered = field - mean_value
    inverse = lax.rsqrt(jnp.mean(centered * centered, axis=-1, keepdims=True) + EPSILON)
    normed = centered * inverse
    return (normed * gain_row + shift_row, normed, inverse)


def norm_backward(grad_out, normed, inverse, gain_row):
    grad_gain = jnp.sum(grad_out * normed, axis=0)
    grad_shift = jnp.sum(grad_out, axis=0)
    scaled = grad_out * gain_row
    grad_in = inverse * (
        scaled
        - jnp.mean(scaled, axis=-1, keepdims=True)
        - normed * jnp.mean(scaled * normed, axis=-1, keepdims=True)
    )
    return (grad_in, grad_gain, grad_shift)


def slot_positions(chosen_ids):
    labels = jnp.arange(EXPERTS, dtype=jnp.int32)
    hit_counts = jnp.sum((chosen_ids[..., None] == labels).astype(jnp.int32), axis=-2)
    before = jnp.cumsum(hit_counts, axis=1) - hit_counts
    return jnp.take_along_axis(before, chosen_ids, axis=-1)


def gelu_slope(inner_pre):
    cumulative = 0.5 * (1.0 + jax.scipy.special.erf(inner_pre * 0.7071067811865476))
    density = jnp.exp(-0.5 * inner_pre * inner_pre) * 0.3989422804014327
    return cumulative + inner_pre * density


def group_of(kind):
    def chips():
        dp, mp = lax.axis_index("dp"), lax.axis_index("mp")
        return dp // 2, lambda i: (2 * i + dp % 2, mp)

    def cores():
        dp, mp = lax.axis_index("dp"), lax.axis_index("mp")
        return dp % 2, lambda i: (2 * (dp // 2) + i, mp)

    def whole():
        dp, mp = lax.axis_index("dp"), lax.axis_index("mp")
        return dp, lambda i: (i, mp)

    def pair():
        dp, mp = lax.axis_index("dp"), lax.axis_index("mp")
        return mp, lambda i: (dp, i)

    return {"chips": chips, "cores": cores, "pair": pair, "all": whole}[kind]


def exchange_kernel(m, pieces, gather, kind, x_ref, out_ref, send_sem, recv_sem, local_sem):
    me, device_of = group_of(kind)()
    step = out_ref.shape[1] // pieces
    barrier = pltpu.get_barrier_semaphore()

    def greet(k, carry):
        pl.semaphore_signal(
            barrier, inc=1, device_id=device_of(lax.rem(me + k, m)), device_id_type=MESH
        )
        return carry

    lax.fori_loop(1, m, greet, 0)
    pl.semaphore_wait(barrier, m - 1)
    own = pltpu.make_async_copy(x_ref if gather else x_ref.at[me], out_ref.at[me], local_sem)
    own.start()

    def describe(t):
        k = 1 + t // pieces
        part = pl.ds(pl.multiple_of((t % pieces) * step, step), step)
        peer = lax.rem(me + k, m)
        return pltpu.make_async_remote_copy(
            src_ref=x_ref.at[part] if gather else x_ref.at[peer, part],
            dst_ref=out_ref.at[me, part],
            send_sem=send_sem.at[t],
            recv_sem=recv_sem.at[t],
            device_id=device_of(peer),
            device_id_type=MESH,
        )

    def start(t, carry):
        describe(t).start()
        return carry

    def finish(t, carry):
        describe(t).wait()
        return carry

    count = (m - 1) * pieces
    lax.fori_loop(0, count, start, 0)
    lax.fori_loop(0, count, finish, 0)
    own.wait()


def exchange(x, m, gather, kind, collective_id, pieces=1):
    block = x.shape if gather else x.shape[1:]
    block_bytes = x.dtype.itemsize
    for d in block:
        block_bytes *= d
    count = (m - 1) * pieces
    return pl.pallas_call(
        functools.partial(exchange_kernel, m, pieces, gather, kind),
        out_shape=jax.ShapeDtypeStruct((m,) + tuple(block), x.dtype),
        in_specs=[pl.BlockSpec(memory_space=pl.ANY)],
        out_specs=pl.BlockSpec(memory_space=pl.ANY),
        scratch_shapes=[
            pltpu.SemaphoreType.DMA((count,)),
            pltpu.SemaphoreType.DMA((count,)),
            pltpu.SemaphoreType.DMA(()),
        ],
        compiler_params=pltpu.CompilerParams(collective_id=collective_id, has_side_effects=True),
        cost_estimate=pl.CostEstimate(flops=0, bytes_accessed=2 * m * block_bytes, transcendentals=0),
    )(x)


def padded_rows(size, dtype_rows=16):
    rows = -(-size // LANES)
    return -(-rows // dtype_rows) * dtype_rows


def shard_sizes(w_qkv, w_proj, w_in, w_out, w_router, ln_gain, ln_bias):
    return [a.size for a in (w_qkv, w_proj, w_in, w_out, w_router, ln_gain, ln_bias)]


def gather_weights(w_qkv, w_proj, w_in, w_out, w_router, ln_gain, ln_bias, n):
    parts = (w_qkv, w_proj, w_in, w_out, w_router, ln_gain, ln_bias)
    flat = jnp.concatenate([a.reshape(-1) for a in parts])
    total = flat.shape[0]
    rows = padded_rows(total)
    flat = jnp.pad(flat, (0, rows * LANES - total)).reshape(rows, LANES)
    full = exchange(flat, n, True, "all", 0).reshape(n, rows * LANES)
    pieces = []
    start = 0
    for a in parts:
        pieces.append(full[:, start:start + a.size].reshape((n,) + a.shape[1:]))
        start += a.size
    q, p, i, o, r, g, b = pieces
    gq = q.reshape((-1,) + w_qkv.shape[2:])
    gr = r.reshape((-1,) + w_router.shape[2:])
    gg = g.transpose(1, 0, 2).reshape(ln_gain.shape[1], -1)
    gb = b.transpose(1, 0, 2).reshape(ln_bias.shape[1], -1)
    return (gq, p, i, o, gr, gg, gb)


def scatter_grads(grads, n, shapes):
    gq, gp, gi, go, gr, gg, gb = grads
    rows = [
        gq.reshape(n, -1),
        gp.reshape(n, -1),
        gi.reshape(n, -1),
        go.reshape(n, -1),
        gr.reshape(n, -1),
        gg.reshape(gg.shape[0], n, -1).transpose(1, 0, 2).reshape(n, -1),
        gb.reshape(gb.shape[0], n, -1).transpose(1, 0, 2).reshape(n, -1),
    ]
    packed = jnp.concatenate(rows, axis=1)
    total = packed.shape[1]
    count = padded_rows(total)
    packed = jnp.pad(packed, ((0, 0), (0, count * LANES - total))).reshape(n, count, LANES)
    received = exchange(packed.astype(jnp.bfloat16), n, False, "all", 1).reshape(n, count * LANES)
    outs = []
    start = 0
    for shape in shapes:
        size = 1
        for d in shape:
            size *= d
        part = received[:, start:start + size].astype(jnp.float32)
        outs.append(jnp.sum(part, axis=0).reshape(shape))
        start += size
    return outs


def layer_forward(field, chosen_ids, weights):
    w_qkv, w_proj, w_in, w_out, w_router, ln_gain, ln_bias = weights
    image_count, length, model_width = field.shape
    row_count = image_count * length
    head_count = w_qkv.shape[2] // HD
    score_scale = HD ** (-0.5)
    gain_rows = ln_gain.astype(jnp.float32)
    shift_rows = ln_bias.astype(jnp.float32)
    flat = field.reshape(row_count, model_width)
    first, normed_one, inverse_one = norm_forward(flat, gain_rows[0], shift_rows[0])
    first = first.astype(jnp.bfloat16)
    projected = jnp.einsum("rd,dcf->rcf", first, w_qkv, preferred_element_type=jnp.float32).astype(
        jnp.bfloat16
    )
    projected = projected.reshape(image_count, length, 3, head_count, HD)
    queries = projected[:, :, 0]
    key_rows = projected[:, :, 1]
    value_rows = projected[:, :, 2]
    scores = (
        jnp.einsum("bqhe,bkhe->bhqk", queries, key_rows, preferred_element_type=jnp.float32)
        * score_scale
    )
    log_total = jax.nn.logsumexp(scores, axis=-1)
    attn_weights = jnp.exp(scores - log_total[..., None]).astype(jnp.bfloat16)
    attended = jnp.einsum(
        "bhqk,bkhe->bqhe", attn_weights, value_rows, preferred_element_type=jnp.float32
    )
    attended = attended.astype(jnp.bfloat16).reshape(row_count, head_count * HD)
    partial_attn = jnp.einsum(
        "rf,jfk->rjk", attended, w_proj, preferred_element_type=jnp.float32
    ).reshape(row_count, model_width)
    hidden = flat + lax.psum(partial_attn, "mp")
    second, normed_two, inverse_two = norm_forward(hidden, gain_rows[1], shift_rows[1])
    second = second.astype(jnp.bfloat16)
    logits = jnp.dot(second, w_router, preferred_element_type=jnp.float32)
    router = jax.nn.softmax(logits, axis=-1)
    labels = jnp.arange(EXPERTS, dtype=jnp.int32)
    ids_flat = chosen_ids.reshape(row_count, TOPK)
    chosen = (ids_flat[:, :, None] == labels).astype(jnp.float32)
    gate_values = jnp.sum(router[:, None, :] * chosen, axis=-1)
    per_image = EXPERTS * CAP
    image_base = (jnp.arange(image_count, dtype=jnp.int32) * per_image)[:, None, None]
    slot_index = (chosen_ids * CAP + slot_positions(chosen_ids) + image_base).reshape(-1)
    owners = (
        jnp.full((image_count * per_image,), row_count, jnp.int32)
        .at[slot_index]
        .set(jnp.repeat(jnp.arange(row_count, dtype=jnp.int32), TOPK))
    )
    slot_gate = (
        jnp.zeros((image_count * per_image,), jnp.float32).at[slot_index].set(gate_values.reshape(-1))
    )
    padded = jnp.concatenate([second, jnp.zeros((1, model_width), jnp.bfloat16)], axis=0)
    slot_rows = jnp.take(padded, owners, axis=0).reshape(image_count, EXPERTS, CAP, model_width)
    slot_split = slot_rows.reshape(slot_rows.shape[:3] + w_in.shape[:1] + w_in.shape[2:3])
    inner_pre = jnp.einsum("becjk,jekf->becf", slot_split, w_in, preferred_element_type=jnp.float32)
    activated = jax.nn.gelu(inner_pre, approximate=False).astype(jnp.bfloat16)
    produced = jnp.einsum("becf,jefk->becjk", activated, w_out, preferred_element_type=jnp.float32)
    produced = produced.reshape(image_count * per_image, model_width)
    picked = jnp.take(produced, slot_index, axis=0).reshape(row_count, TOPK, model_width)
    partial_moe = jnp.sum(gate_values[:, :, None] * picked, axis=1)
    output = hidden + lax.psum(partial_moe.astype(jnp.bfloat16), "mp").astype(jnp.float32)
    record = (
        normed_one, inverse_one, first, projected, log_total, attended, normed_two, inverse_two,
        second, router, chosen, slot_index, owners, slot_gate, slot_rows, inner_pre, activated, picked,
    )
    return (output.reshape(image_count, length, model_width), record)


def layer_backward(grad_field, record, weights):
    w_qkv, w_proj, w_in, w_out, w_router, ln_gain, ln_bias = weights
    (
        normed_one, inverse_one, first, projected, log_total, attended, normed_two, inverse_two,
        second, router, chosen, slot_index, owners, slot_gate, slot_rows, inner_pre, activated, picked,
    ) = record
    image_count, length, model_width = grad_field.shape
    row_count = image_count * length
    head_count = projected.shape[3]
    score_scale = HD ** (-0.5)
    gain_rows = ln_gain.astype(jnp.float32)
    grad_flat = grad_field.reshape(row_count, model_width)
    padded_grad = jnp.concatenate([grad_flat, jnp.zeros((1, model_width), jnp.float32)], axis=0)
    grad_slots = (jnp.take(padded_grad, owners, axis=0) * slot_gate[:, None]).astype(jnp.bfloat16)
    split = (w_out.shape[0], w_out.shape[3])
    grad_slots = grad_slots.reshape((image_count, EXPERTS, CAP) + split)
    slot_split = slot_rows.reshape((image_count, EXPERTS, CAP) + split)
    grad_w_out = jnp.einsum(
        "becf,becjk->jefk", activated, grad_slots, preferred_element_type=jnp.float32
    )
    grad_act = jnp.einsum("becjk,jefk->becf", grad_slots, w_out, preferred_element_type=jnp.float32)
    grad_inner = (grad_act * gelu_slope(inner_pre)).astype(jnp.bfloat16)
    grad_w_in = jnp.einsum(
        "becjk,becf->jekf", slot_split, grad_inner, preferred_element_type=jnp.float32
    )
    grad_slot_rows = jnp.einsum(
        "becf,jekf->becjk", grad_inner, w_in, preferred_element_type=jnp.float32
    )
    grad_slot_rows = grad_slot_rows.reshape(image_count * EXPERTS * CAP, model_width)
    partial_second = jnp.sum(
        jnp.take(grad_slot_rows, slot_index, axis=0).reshape(row_count, TOPK, model_width), axis=1
    )
    partial_gate = jnp.sum(picked * grad_flat[:, None, :], axis=-1)
    grad_second, grad_gate = lax.psum((partial_second, partial_gate), "mp")
    grad_router = jnp.sum(grad_gate[:, :, None] * chosen, axis=1)
    grad_logits = router * (grad_router - jnp.sum(router * grad_router, axis=-1, keepdims=True))
    grad_logits = grad_logits.astype(jnp.bfloat16)
    grad_w_router = jnp.dot(second.T, grad_logits, preferred_element_type=jnp.float32)
    grad_second = grad_second + jnp.dot(grad_logits, w_router.T, preferred_element_type=jnp.float32)
    grad_from_norm, grad_gain_two, grad_shift_two = norm_backward(
        grad_second, normed_two, inverse_two, gain_rows[1]
    )
    grad_hidden = grad_flat + grad_from_norm
    grad_hidden_low = grad_hidden.astype(jnp.bfloat16)
    grad_hidden_split = grad_hidden_low.reshape((row_count,) + split)
    grad_w_proj = jnp.einsum(
        "rf,rjk->jfk", attended, grad_hidden_split, preferred_element_type=jnp.float32
    )
    grad_attended = jnp.einsum(
        "rjk,jfk->rf", grad_hidden_split, w_proj, preferred_element_type=jnp.float32
    ).astype(jnp.bfloat16)
    grad_attended = grad_attended.reshape(image_count, length, head_count, HD)
    queries = projected[:, :, 0]
    key_rows = projected[:, :, 1]
    value_rows = projected[:, :, 2]
    scores = (
        jnp.einsum("bqhe,bkhe->bhqk", queries, key_rows, preferred_element_type=jnp.float32)
        * score_scale
    )
    probs = jnp.exp(scores - log_total[..., None])
    grad_values = jnp.einsum(
        "bhqk,bqhe->bkhe", probs.astype(jnp.bfloat16), grad_attended,
        preferred_element_type=jnp.float32,
    )
    grad_probs = jnp.einsum(
        "bqhe,bkhe->bhqk", grad_attended, value_rows, preferred_element_type=jnp.float32
    )
    grad_scores = (
        probs * (grad_probs - jnp.sum(probs * grad_probs, axis=-1, keepdims=True))
    ).astype(jnp.bfloat16)
    grad_queries = (
        jnp.einsum("bhqk,bkhe->bqhe", grad_scores, key_rows, preferred_element_type=jnp.float32)
        * score_scale
    )
    grad_keys = (
        jnp.einsum("bhqk,bqhe->bkhe", grad_scores, queries, preferred_element_type=jnp.float32)
        * score_scale
    )
    grad_projected = jnp.stack([grad_queries, grad_keys, grad_values], axis=2).astype(jnp.bfloat16)
    grad_projected = grad_projected.reshape(row_count, 3, head_count * HD)
    grad_w_qkv = jnp.einsum(
        "rd,rcf->dcf", first, grad_projected, preferred_element_type=jnp.float32
    )
    partial_first = jnp.einsum(
        "rcf,dcf->rd", grad_projected, w_qkv, preferred_element_type=jnp.float32
    )
    grad_first = lax.psum(partial_first.astype(jnp.bfloat16), "mp").astype(jnp.float32)
    grad_input_norm, grad_gain_one, grad_shift_one = norm_backward(
        grad_first, normed_one, inverse_one, gain_rows[0]
    )
    grad_input = grad_hidden + grad_input_norm
    grads = (
        grad_w_qkv,
        grad_w_proj,
        grad_w_in,
        grad_w_out,
        grad_w_router,
        jnp.stack([grad_gain_one, grad_gain_two]),
        jnp.stack([grad_shift_one, grad_shift_two]),
    )
    return (grad_input.reshape(image_count, length, model_width), grads)


def make_local(n):
    def local(images, routes, w_qkv, w_proj, w_in, w_out, w_router, ln_gain, ln_bias, cotangent):
        shapes = [a.shape for a in (w_qkv, w_proj, w_in, w_out, w_router, ln_gain, ln_bias)]
        weights = gather_weights(w_qkv, w_proj, w_in, w_out, w_router, ln_gain, ln_bias, n)
        field = images.astype(jnp.float32)
        output, record = layer_forward(field, routes[0], weights)
        grad_input, grads = layer_backward(cotangent.astype(jnp.float32), record, weights)
        shards = scatter_grads(grads, n, [(1,) + tuple(s[1:]) for s in shapes])
        return (output, grad_input, *shards)

    return local


def solution(mesh):
    n = mesh.shape["dp"]
    in_specs = (
        P("dp", None, None),
        P(None, "dp", None, None),
        P(None, "dp", None, "mp"),
        P(None, "mp", "dp"),
        P(None, None, "dp", "mp"),
        P(None, None, "mp", "dp"),
        P(None, "dp", None),
        P(None, None, "dp"),
        P(None, None, "dp"),
        P("dp", None, None),
    )
    out_specs = (
        P("dp", None, None),
        P("dp", None, None),
        P(None, "dp", None, "mp"),
        P(None, "mp", "dp"),
        P(None, None, "dp", "mp"),
        P(None, None, "mp", "dp"),
        P(None, "dp", None),
        P(None, None, "dp"),
        P(None, None, "dp"),
    )
    return jax.shard_map(make_local(n), mesh=mesh, in_specs=in_specs, out_specs=out_specs, check_vma=False)
```

```python
import functools

import jax
import jax.numpy as jnp
from jax import lax
from jax.sharding import PartitionSpec as P
from jax.experimental import pallas as pl
from jax.experimental.pallas import tpu as pltpu

MESH = pl.DeviceIdType.MESH
LANES = 128

HD = 64
EXPERTS = 4
TOPK = 2
CAP = 104
EPSILON = 1e-06


def norm_forward(field, gain_row, shift_row):
    mean_value = jnp.mean(field, axis=-1, keepdims=True)
    centered = field - mean_value
    inverse = lax.rsqrt(jnp.mean(centered * centered, axis=-1, keepdims=True) + EPSILON)
    normed = centered * inverse
    return (normed * gain_row + shift_row, normed, inverse)


def norm_backward(grad_out, normed, inverse, gain_row):
    grad_gain = jnp.sum(grad_out * normed, axis=0)
    grad_shift = jnp.sum(grad_out, axis=0)
    scaled = grad_out * gain_row
    grad_in = inverse * (
        scaled
        - jnp.mean(scaled, axis=-1, keepdims=True)
        - normed * jnp.mean(scaled * normed, axis=-1, keepdims=True)
    )
    return (grad_in, grad_gain, grad_shift)


def slot_positions(chosen_ids):
    labels = jnp.arange(EXPERTS, dtype=jnp.int32)
    hit_counts = jnp.sum((chosen_ids[..., None] == labels).astype(jnp.int32), axis=-2)
    before = jnp.cumsum(hit_counts, axis=1) - hit_counts
    return jnp.take_along_axis(before, chosen_ids, axis=-1)


def gelu_slope(inner_pre):
    cumulative = 0.5 * (1.0 + jax.scipy.special.erf(inner_pre * 0.7071067811865476))
    density = jnp.exp(-0.5 * inner_pre * inner_pre) * 0.3989422804014327
    return cumulative + inner_pre * density


def group_of(kind):
    def chips():
        dp, mp = lax.axis_index("dp"), lax.axis_index("mp")
        return dp // 2, lambda i: (2 * i + dp % 2, mp)

    def cores():
        dp, mp = lax.axis_index("dp"), lax.axis_index("mp")
        return dp % 2, lambda i: (2 * (dp // 2) + i, mp)

    def whole():
        dp, mp = lax.axis_index("dp"), lax.axis_index("mp")
        return dp, lambda i: (i, mp)

    def pair():
        dp, mp = lax.axis_index("dp"), lax.axis_index("mp")
        return mp, lambda i: (dp, i)

    return {"chips": chips, "cores": cores, "pair": pair, "all": whole}[kind]


def exchange_kernel(m, pieces, gather, kind, x_ref, out_ref, send_sem, recv_sem, local_sem):
    me, device_of = group_of(kind)()
    step = out_ref.shape[1] // pieces
    barrier = pltpu.get_barrier_semaphore()

    def greet(k, carry):
        pl.semaphore_signal(
            barrier, inc=1, device_id=device_of(lax.rem(me + k, m)), device_id_type=MESH
        )
        return carry

    lax.fori_loop(1, m, greet, 0)
    pl.semaphore_wait(barrier, m - 1)
    own = pltpu.make_async_copy(x_ref if gather else x_ref.at[me], out_ref.at[me], local_sem)
    own.start()

    def describe(t):
        k = 1 + t // pieces
        part = pl.ds(pl.multiple_of((t % pieces) * step, step), step)
        peer = lax.rem(me + k, m)
        return pltpu.make_async_remote_copy(
            src_ref=x_ref.at[part] if gather else x_ref.at[peer, part],
            dst_ref=out_ref.at[me, part],
            send_sem=send_sem.at[t],
            recv_sem=recv_sem.at[t],
            device_id=device_of(peer),
            device_id_type=MESH,
        )

    def start(t, carry):
        describe(t).start()
        return carry

    def finish(t, carry):
        describe(t).wait()
        return carry

    count = (m - 1) * pieces
    lax.fori_loop(0, count, start, 0)
    lax.fori_loop(0, count, finish, 0)
    own.wait()


def exchange(x, m, gather, kind, collective_id, pieces=1):
    block = x.shape if gather else x.shape[1:]
    block_bytes = x.dtype.itemsize
    for d in block:
        block_bytes *= d
    count = (m - 1) * pieces
    return pl.pallas_call(
        functools.partial(exchange_kernel, m, pieces, gather, kind),
        out_shape=jax.ShapeDtypeStruct((m,) + tuple(block), x.dtype),
        in_specs=[pl.BlockSpec(memory_space=pl.ANY)],
        out_specs=pl.BlockSpec(memory_space=pl.ANY),
        scratch_shapes=[
            pltpu.SemaphoreType.DMA((count,)),
            pltpu.SemaphoreType.DMA((count,)),
            pltpu.SemaphoreType.DMA(()),
        ],
        compiler_params=pltpu.CompilerParams(collective_id=collective_id, has_side_effects=True),
        cost_estimate=pl.CostEstimate(flops=0, bytes_accessed=2 * m * block_bytes, transcendentals=0),
    )(x)


def relay_gather_kernel(chips, direct, x_ref, out_ref, sa, ra, sb, rb, sf, rf, sp, rp, sl):
    dp, mp = lax.axis_index("dp"), lax.axis_index("mp")
    n = 2 * chips
    core = dp % 2
    other = 1 - core
    chip = dp // 2
    barrier = pltpu.get_barrier_semaphore()

    def greet(k, carry):
        pl.semaphore_signal(
            barrier, inc=1, device_id=(lax.rem(dp + k, n), mp), device_id_type=MESH
        )
        return carry

    lax.fori_loop(1, n, greet, 0)
    pl.semaphore_wait(barrier, n - 1)
    own = pltpu.make_async_copy(x_ref, out_ref.at[dp], sl)
    own.start()

    def remote(src, dst, send, recv, target):
        return pltpu.make_async_remote_copy(
            src_ref=src, dst_ref=dst, send_sem=send, recv_sem=recv,
            device_id=(target, mp), device_id_type=MESH,
        )

    def same(j):
        return remote(x_ref, out_ref.at[dp], sa.at[j], ra.at[j], 2 * lax.rem(chip + j, chips) + core)

    def cross(j):
        return remote(x_ref, out_ref.at[dp], sb.at[j], rb.at[j], 2 * lax.rem(chip + j, chips) + other)

    def relay(j):
        slot = 2 * lax.rem(chip + chips - j, chips) + core
        return remote(out_ref.at[slot], out_ref.at[slot], sf.at[j], rf.at[j], 2 * chip + other)

    mate = remote(x_ref, out_ref.at[dp], sp, rp, 2 * chip + other)
    forwarded = [j for j in range(1, chips) if j not in direct]
    mate.start()
    for j in forwarded:
        same(j).start()
    for j in direct:
        cross(j).start()
    for j in direct:
        same(j).start()
    for j in forwarded:
        same(j).wait_recv()
        relay(j).start()
    for j in direct:
        same(j).wait_recv()
    for j in range(1, chips):
        same(j).wait_send()
    for j in direct:
        cross(j).wait()
    mate.wait()
    for j in forwarded:
        relay(j).wait()
    own.wait()


def relay_gather(x, n, collective_id):
    chips = n // 2
    direct = tuple(j for j in range(1, chips) if j % 4 == 0)
    block_bytes = x.dtype.itemsize
    for d in x.shape:
        block_bytes *= d
    return pl.pallas_call(
        functools.partial(relay_gather_kernel, chips, direct),
        out_shape=jax.ShapeDtypeStruct((n,) + tuple(x.shape), x.dtype),
        in_specs=[pl.BlockSpec(memory_space=pl.ANY)],
        out_specs=pl.BlockSpec(memory_space=pl.ANY),
        scratch_shapes=[pltpu.SemaphoreType.DMA((chips,))] * 6
        + [pltpu.SemaphoreType.DMA(())] * 3,
        compiler_params=pltpu.CompilerParams(collective_id=collective_id, has_side_effects=True),
        cost_estimate=pl.CostEstimate(flops=0, bytes_accessed=2 * n * block_bytes, transcendentals=0),
    )(x)


def padded_rows(size, dtype_rows=16):
    rows = -(-size // LANES)
    return -(-rows // dtype_rows) * dtype_rows


def shard_sizes(w_qkv, w_proj, w_in, w_out, w_router, ln_gain, ln_bias):
    return [a.size for a in (w_qkv, w_proj, w_in, w_out, w_router, ln_gain, ln_bias)]


def gather_weights(w_qkv, w_proj, w_in, w_out, w_router, ln_gain, ln_bias, n):
    parts = (w_qkv, w_proj, w_in, w_out, w_router, ln_gain, ln_bias)
    flat = jnp.concatenate([a.reshape(-1) for a in parts])
    total = flat.shape[0]
    rows = padded_rows(total)
    flat = jnp.pad(flat, (0, rows * LANES - total)).reshape(rows, LANES)
    full = relay_gather(flat, n, 0).reshape(n, rows * LANES)
    pieces = []
    start = 0
    for a in parts:
        pieces.append(full[:, start:start + a.size].reshape((n,) + a.shape[1:]))
        start += a.size
    q, p, i, o, r, g, b = pieces
    gq = q.reshape((-1,) + w_qkv.shape[2:])
    gr = r.reshape((-1,) + w_router.shape[2:])
    gg = g.transpose(1, 0, 2).reshape(ln_gain.shape[1], -1)
    gb = b.transpose(1, 0, 2).reshape(ln_bias.shape[1], -1)
    return (gq, p, i, o, gr, gg, gb)


def scatter_grads(grads, n, shapes):
    gq, gp, gi, go, gr, gg, gb = grads
    rows = [
        gq.reshape(n, -1),
        gp.reshape(n, -1),
        gi.reshape(n, -1),
        go.reshape(n, -1),
        gr.reshape(n, -1),
        gg.reshape(gg.shape[0], n, -1).transpose(1, 0, 2).reshape(n, -1),
        gb.reshape(gb.shape[0], n, -1).transpose(1, 0, 2).reshape(n, -1),
    ]
    packed = jnp.concatenate(rows, axis=1)
    total = packed.shape[1]
    count = padded_rows(total)
    packed = jnp.pad(packed, ((0, 0), (0, count * LANES - total))).reshape(n, count, LANES)
    received = exchange(packed.astype(jnp.bfloat16), n, False, "all", 1).reshape(n, count * LANES)
    outs = []
    start = 0
    for shape in shapes:
        size = 1
        for d in shape:
            size *= d
        part = received[:, start:start + size].astype(jnp.float32)
        outs.append(jnp.sum(part, axis=0).reshape(shape))
        start += size
    return outs


def layer_forward(field, chosen_ids, weights):
    w_qkv, w_proj, w_in, w_out, w_router, ln_gain, ln_bias = weights
    image_count, length, model_width = field.shape
    row_count = image_count * length
    head_count = w_qkv.shape[2] // HD
    score_scale = HD ** (-0.5)
    gain_rows = ln_gain.astype(jnp.float32)
    shift_rows = ln_bias.astype(jnp.float32)
    flat = field.reshape(row_count, model_width)
    first, normed_one, inverse_one = norm_forward(flat, gain_rows[0], shift_rows[0])
    first = first.astype(jnp.bfloat16)
    projected = jnp.einsum("rd,dcf->rcf", first, w_qkv, preferred_element_type=jnp.float32).astype(
        jnp.bfloat16
    )
    projected = projected.reshape(image_count, length, 3, head_count, HD)
    queries = projected[:, :, 0]
    key_rows = projected[:, :, 1]
    value_rows = projected[:, :, 2]
    scores = (
        jnp.einsum("bqhe,bkhe->bhqk", queries, key_rows, preferred_element_type=jnp.float32)
        * score_scale
    )
    log_total = jax.nn.logsumexp(scores, axis=-1)
    attn_weights = jnp.exp(scores - log_total[..., None]).astype(jnp.bfloat16)
    attended = jnp.einsum(
        "bhqk,bkhe->bqhe", attn_weights, value_rows, preferred_element_type=jnp.float32
    )
    attended = attended.astype(jnp.bfloat16).reshape(row_count, head_count * HD)
    partial_attn = jnp.einsum(
        "rf,jfk->rjk", attended, w_proj, preferred_element_type=jnp.float32
    ).reshape(row_count, model_width)
    hidden = flat + lax.psum(partial_attn, "mp")
    second, normed_two, inverse_two = norm_forward(hidden, gain_rows[1], shift_rows[1])
    second = second.astype(jnp.bfloat16)
    logits = jnp.dot(second, w_router, preferred_element_type=jnp.float32)
    router = jax.nn.softmax(logits, axis=-1)
    labels = jnp.arange(EXPERTS, dtype=jnp.int32)
    ids_flat = chosen_ids.reshape(row_count, TOPK)
    chosen = (ids_flat[:, :, None] == labels).astype(jnp.float32)
    gate_values = jnp.sum(router[:, None, :] * chosen, axis=-1)
    per_image = EXPERTS * CAP
    image_base = (jnp.arange(image_count, dtype=jnp.int32) * per_image)[:, None, None]
    slot_index = (chosen_ids * CAP + slot_positions(chosen_ids) + image_base).reshape(-1)
    owners = (
        jnp.full((image_count * per_image,), row_count, jnp.int32)
        .at[slot_index]
        .set(jnp.repeat(jnp.arange(row_count, dtype=jnp.int32), TOPK))
    )
    slot_gate = (
        jnp.zeros((image_count * per_image,), jnp.float32).at[slot_index].set(gate_values.reshape(-1))
    )
    padded = jnp.concatenate([second, jnp.zeros((1, model_width), jnp.bfloat16)], axis=0)
    slot_rows = jnp.take(padded, owners, axis=0).reshape(image_count, EXPERTS, CAP, model_width)
    slot_split = slot_rows.reshape(slot_rows.shape[:3] + w_in.shape[:1] + w_in.shape[2:3])
    inner_pre = jnp.einsum("becjk,jekf->becf", slot_split, w_in, preferred_element_type=jnp.float32)
    activated = jax.nn.gelu(inner_pre, approximate=False).astype(jnp.bfloat16)
    produced = jnp.einsum("becf,jefk->becjk", activated, w_out, preferred_element_type=jnp.float32)
    produced = produced.reshape(image_count * per_image, model_width)
    picked = jnp.take(produced, slot_index, axis=0).reshape(row_count, TOPK, model_width)
    partial_moe = jnp.sum(gate_values[:, :, None] * picked, axis=1)
    output = hidden + lax.psum(partial_moe.astype(jnp.bfloat16), "mp").astype(jnp.float32)
    record = (
        normed_one, inverse_one, first, projected, log_total, attended, normed_two, inverse_two,
        second, router, chosen, slot_index, owners, slot_gate, slot_rows, inner_pre, activated, picked,
    )
    return (output.reshape(image_count, length, model_width), record)


def layer_backward(grad_field, record, weights):
    w_qkv, w_proj, w_in, w_out, w_router, ln_gain, ln_bias = weights
    (
        normed_one, inverse_one, first, projected, log_total, attended, normed_two, inverse_two,
        second, router, chosen, slot_index, owners, slot_gate, slot_rows, inner_pre, activated, picked,
    ) = record
    image_count, length, model_width = grad_field.shape
    row_count = image_count * length
    head_count = projected.shape[3]
    score_scale = HD ** (-0.5)
    gain_rows = ln_gain.astype(jnp.float32)
    grad_flat = grad_field.reshape(row_count, model_width)
    padded_grad = jnp.concatenate([grad_flat, jnp.zeros((1, model_width), jnp.float32)], axis=0)
    grad_slots = (jnp.take(padded_grad, owners, axis=0) * slot_gate[:, None]).astype(jnp.bfloat16)
    split = (w_out.shape[0], w_out.shape[3])
    grad_slots = grad_slots.reshape((image_count, EXPERTS, CAP) + split)
    slot_split = slot_rows.reshape((image_count, EXPERTS, CAP) + split)
    grad_w_out = jnp.einsum(
        "becf,becjk->jefk", activated, grad_slots, preferred_element_type=jnp.float32
    )
    grad_act = jnp.einsum("becjk,jefk->becf", grad_slots, w_out, preferred_element_type=jnp.float32)
    grad_inner = (grad_act * gelu_slope(inner_pre)).astype(jnp.bfloat16)
    grad_w_in = jnp.einsum(
        "becjk,becf->jekf", slot_split, grad_inner, preferred_element_type=jnp.float32
    )
    grad_slot_rows = jnp.einsum(
        "becf,jekf->becjk", grad_inner, w_in, preferred_element_type=jnp.float32
    )
    grad_slot_rows = grad_slot_rows.reshape(image_count * EXPERTS * CAP, model_width)
    partial_second = jnp.sum(
        jnp.take(grad_slot_rows, slot_index, axis=0).reshape(row_count, TOPK, model_width), axis=1
    )
    partial_gate = jnp.sum(picked * grad_flat[:, None, :], axis=-1)
    grad_second, grad_gate = lax.psum((partial_second, partial_gate), "mp")
    grad_router = jnp.sum(grad_gate[:, :, None] * chosen, axis=1)
    grad_logits = router * (grad_router - jnp.sum(router * grad_router, axis=-1, keepdims=True))
    grad_logits = grad_logits.astype(jnp.bfloat16)
    grad_w_router = jnp.dot(second.T, grad_logits, preferred_element_type=jnp.float32)
    grad_second = grad_second + jnp.dot(grad_logits, w_router.T, preferred_element_type=jnp.float32)
    grad_from_norm, grad_gain_two, grad_shift_two = norm_backward(
        grad_second, normed_two, inverse_two, gain_rows[1]
    )
    grad_hidden = grad_flat + grad_from_norm
    grad_hidden_low = grad_hidden.astype(jnp.bfloat16)
    grad_hidden_split = grad_hidden_low.reshape((row_count,) + split)
    grad_w_proj = jnp.einsum(
        "rf,rjk->jfk", attended, grad_hidden_split, preferred_element_type=jnp.float32
    )
    grad_attended = jnp.einsum(
        "rjk,jfk->rf", grad_hidden_split, w_proj, preferred_element_type=jnp.float32
    ).astype(jnp.bfloat16)
    grad_attended = grad_attended.reshape(image_count, length, head_count, HD)
    queries = projected[:, :, 0]
    key_rows = projected[:, :, 1]
    value_rows = projected[:, :, 2]
    scores = (
        jnp.einsum("bqhe,bkhe->bhqk", queries, key_rows, preferred_element_type=jnp.float32)
        * score_scale
    )
    probs = jnp.exp(scores - log_total[..., None])
    grad_values = jnp.einsum(
        "bhqk,bqhe->bkhe", probs.astype(jnp.bfloat16), grad_attended,
        preferred_element_type=jnp.float32,
    )
    grad_probs = jnp.einsum(
        "bqhe,bkhe->bhqk", grad_attended, value_rows, preferred_element_type=jnp.float32
    )
    grad_scores = (
        probs * (grad_probs - jnp.sum(probs * grad_probs, axis=-1, keepdims=True))
    ).astype(jnp.bfloat16)
    grad_queries = (
        jnp.einsum("bhqk,bkhe->bqhe", grad_scores, key_rows, preferred_element_type=jnp.float32)
        * score_scale
    )
    grad_keys = (
        jnp.einsum("bhqk,bqhe->bkhe", grad_scores, queries, preferred_element_type=jnp.float32)
        * score_scale
    )
    grad_projected = jnp.stack([grad_queries, grad_keys, grad_values], axis=2).astype(jnp.bfloat16)
    grad_projected = grad_projected.reshape(row_count, 3, head_count * HD)
    grad_w_qkv = jnp.einsum(
        "rd,rcf->dcf", first, grad_projected, preferred_element_type=jnp.float32
    )
    partial_first = jnp.einsum(
        "rcf,dcf->rd", grad_projected, w_qkv, preferred_element_type=jnp.float32
    )
    grad_first = lax.psum(partial_first.astype(jnp.bfloat16), "mp").astype(jnp.float32)
    grad_input_norm, grad_gain_one, grad_shift_one = norm_backward(
        grad_first, normed_one, inverse_one, gain_rows[0]
    )
    grad_input = grad_hidden + grad_input_norm
    grads = (
        grad_w_qkv,
        grad_w_proj,
        grad_w_in,
        grad_w_out,
        grad_w_router,
        jnp.stack([grad_gain_one, grad_gain_two]),
        jnp.stack([grad_shift_one, grad_shift_two]),
    )
    return (grad_input.reshape(image_count, length, model_width), grads)


def make_local(n):
    def local(images, routes, w_qkv, w_proj, w_in, w_out, w_router, ln_gain, ln_bias, cotangent):
        shapes = [a.shape for a in (w_qkv, w_proj, w_in, w_out, w_router, ln_gain, ln_bias)]
        weights = gather_weights(w_qkv, w_proj, w_in, w_out, w_router, ln_gain, ln_bias, n)
        field = images.astype(jnp.float32)
        output, record = layer_forward(field, routes[0], weights)
        grad_input, grads = layer_backward(cotangent.astype(jnp.float32), record, weights)
        shards = scatter_grads(grads, n, [(1,) + tuple(s[1:]) for s in shapes])
        return (output, grad_input, *shards)

    return local


def solution(mesh):
    n = mesh.shape["dp"]
    in_specs = (
        P("dp", None, None),
        P(None, "dp", None, None),
        P(None, "dp", None, "mp"),
        P(None, "mp", "dp"),
        P(None, None, "dp", "mp"),
        P(None, None, "mp", "dp"),
        P(None, "dp", None),
        P(None, None, "dp"),
        P(None, None, "dp"),
        P("dp", None, None),
    )
    out_specs = (
        P("dp", None, None),
        P("dp", None, None),
        P(None, "dp", None, "mp"),
        P(None, "mp", "dp"),
        P(None, None, "dp", "mp"),
        P(None, None, "mp", "dp"),
        P(None, "dp", None),
        P(None, None, "dp"),
        P(None, None, "dp"),
    )
    return jax.shard_map(make_local(n), mesh=mesh, in_specs=in_specs, out_specs=out_specs, check_vma=False)
```

```python
import functools

import jax
import jax.numpy as jnp
from jax import lax
from jax.sharding import PartitionSpec as P
from jax.experimental import pallas as pl
from jax.experimental.pallas import tpu as pltpu

MESH = pl.DeviceIdType.MESH
LANES = 128

HD = 64
EXPERTS = 4
TOPK = 2
CAP = 104
EPSILON = 1e-06


def norm_forward(field, gain_row, shift_row):
    mean_value = jnp.mean(field, axis=-1, keepdims=True)
    centered = field - mean_value
    inverse = lax.rsqrt(jnp.mean(centered * centered, axis=-1, keepdims=True) + EPSILON)
    normed = centered * inverse
    return (normed * gain_row + shift_row, normed, inverse)


def norm_backward(grad_out, normed, inverse, gain_row):
    grad_gain = jnp.sum(grad_out * normed, axis=0)
    grad_shift = jnp.sum(grad_out, axis=0)
    scaled = grad_out * gain_row
    grad_in = inverse * (
        scaled
        - jnp.mean(scaled, axis=-1, keepdims=True)
        - normed * jnp.mean(scaled * normed, axis=-1, keepdims=True)
    )
    return (grad_in, grad_gain, grad_shift)


def slot_positions(chosen_ids):
    labels = jnp.arange(EXPERTS, dtype=jnp.int32)
    hit_counts = jnp.sum((chosen_ids[..., None] == labels).astype(jnp.int32), axis=-2)
    before = jnp.cumsum(hit_counts, axis=1) - hit_counts
    return jnp.take_along_axis(before, chosen_ids, axis=-1)


def gelu_slope(inner_pre):
    cumulative = 0.5 * (1.0 + jax.scipy.special.erf(inner_pre * 0.7071067811865476))
    density = jnp.exp(-0.5 * inner_pre * inner_pre) * 0.3989422804014327
    return cumulative + inner_pre * density


def group_of(kind):
    def chips():
        dp, mp = lax.axis_index("dp"), lax.axis_index("mp")
        return dp // 2, lambda i: (2 * i + dp % 2, mp)

    def cores():
        dp, mp = lax.axis_index("dp"), lax.axis_index("mp")
        return dp % 2, lambda i: (2 * (dp // 2) + i, mp)

    def whole():
        dp, mp = lax.axis_index("dp"), lax.axis_index("mp")
        return dp, lambda i: (i, mp)

    def pair():
        dp, mp = lax.axis_index("dp"), lax.axis_index("mp")
        return mp, lambda i: (dp, i)

    return {"chips": chips, "cores": cores, "pair": pair, "all": whole}[kind]


def exchange_kernel(m, pieces, gather, kind, x_ref, out_ref, send_sem, recv_sem, local_sem):
    me, device_of = group_of(kind)()
    step = out_ref.shape[1] // pieces
    barrier = pltpu.get_barrier_semaphore()

    def greet(k, carry):
        pl.semaphore_signal(
            barrier, inc=1, device_id=device_of(lax.rem(me + k, m)), device_id_type=MESH
        )
        return carry

    lax.fori_loop(1, m, greet, 0)
    pl.semaphore_wait(barrier, m - 1)
    own = pltpu.make_async_copy(x_ref if gather else x_ref.at[me], out_ref.at[me], local_sem)
    own.start()

    def describe(t):
        k = 1 + t // pieces
        part = pl.ds(pl.multiple_of((t % pieces) * step, step), step)
        peer = lax.rem(me + k, m)
        return pltpu.make_async_remote_copy(
            src_ref=x_ref.at[part] if gather else x_ref.at[peer, part],
            dst_ref=out_ref.at[me, part],
            send_sem=send_sem.at[t],
            recv_sem=recv_sem.at[t],
            device_id=device_of(peer),
            device_id_type=MESH,
        )

    def start(t, carry):
        describe(t).start()
        return carry

    def finish(t, carry):
        describe(t).wait()
        return carry

    count = (m - 1) * pieces
    lax.fori_loop(0, count, start, 0)
    lax.fori_loop(0, count, finish, 0)
    own.wait()


def exchange(x, m, gather, kind, collective_id, pieces=1):
    block = x.shape if gather else x.shape[1:]
    block_bytes = x.dtype.itemsize
    for d in block:
        block_bytes *= d
    count = (m - 1) * pieces
    return pl.pallas_call(
        functools.partial(exchange_kernel, m, pieces, gather, kind),
        out_shape=jax.ShapeDtypeStruct((m,) + tuple(block), x.dtype),
        in_specs=[pl.BlockSpec(memory_space=pl.ANY)],
        out_specs=pl.BlockSpec(memory_space=pl.ANY),
        scratch_shapes=[
            pltpu.SemaphoreType.DMA((count,)),
            pltpu.SemaphoreType.DMA((count,)),
            pltpu.SemaphoreType.DMA(()),
        ],
        compiler_params=pltpu.CompilerParams(collective_id=collective_id, has_side_effects=True),
        cost_estimate=pl.CostEstimate(flops=0, bytes_accessed=2 * m * block_bytes, transcendentals=0),
    )(x)


def relay_gather_kernel(chips, direct, x_ref, out_ref, sa, ra, sb, rb, sf, rf, sp, rp, sl):
    dp, mp = lax.axis_index("dp"), lax.axis_index("mp")
    n = 2 * chips
    core = dp % 2
    other = 1 - core
    chip = dp // 2
    barrier = pltpu.get_barrier_semaphore()

    def greet(k, carry):
        pl.semaphore_signal(
            barrier, inc=1, device_id=(lax.rem(dp + k, n), mp), device_id_type=MESH
        )
        return carry

    lax.fori_loop(1, n, greet, 0)
    pl.semaphore_wait(barrier, n - 1)
    own = pltpu.make_async_copy(x_ref, out_ref.at[dp], sl)
    own.start()

    def remote(src, dst, send, recv, target):
        return pltpu.make_async_remote_copy(
            src_ref=src, dst_ref=dst, send_sem=send, recv_sem=recv,
            device_id=(target, mp), device_id_type=MESH,
        )

    def same(j):
        return remote(x_ref, out_ref.at[dp], sa.at[j], ra.at[j], 2 * lax.rem(chip + j, chips) + core)

    def cross(j):
        return remote(x_ref, out_ref.at[dp], sb.at[j], rb.at[j], 2 * lax.rem(chip + j, chips) + other)

    def relay(j):
        slot = 2 * lax.rem(chip + chips - j, chips) + core
        return remote(out_ref.at[slot], out_ref.at[slot], sf.at[j], rf.at[j], 2 * chip + other)

    mate = remote(x_ref, out_ref.at[dp], sp, rp, 2 * chip + other)
    forwarded = [j for j in range(1, chips) if j not in direct]
    mate.start()
    for j in forwarded:
        same(j).start()
    for j in direct:
        cross(j).start()
    for j in direct:
        same(j).start()
    for j in forwarded:
        same(j).wait_recv()
        relay(j).start()
    for j in direct:
        same(j).wait_recv()
    for j in range(1, chips):
        same(j).wait_send()
    for j in direct:
        cross(j).wait()
    mate.wait()
    for j in forwarded:
        relay(j).wait()
    own.wait()


def relay_gather(x, n, collective_id):
    chips = n // 2
    direct = tuple(j for j in range(1, chips) if j % 4 == 0)
    block_bytes = x.dtype.itemsize
    for d in x.shape:
        block_bytes *= d
    return pl.pallas_call(
        functools.partial(relay_gather_kernel, chips, direct),
        out_shape=jax.ShapeDtypeStruct((n,) + tuple(x.shape), x.dtype),
        in_specs=[pl.BlockSpec(memory_space=pl.ANY)],
        out_specs=pl.BlockSpec(memory_space=pl.ANY),
        scratch_shapes=[pltpu.SemaphoreType.DMA((chips,))] * 6
        + [pltpu.SemaphoreType.DMA(())] * 3,
        compiler_params=pltpu.CompilerParams(collective_id=collective_id, has_side_effects=True),
        cost_estimate=pl.CostEstimate(flops=0, bytes_accessed=2 * n * block_bytes, transcendentals=0),
    )(x)


def relay_reduce_kernel(chips, direct, y_ref, out_same, out_cross, pin, sbuf, ss, rs, sc, rc, sr, rr, sl):
    dp, mp = lax.axis_index("dp"), lax.axis_index("mp")
    n = 2 * chips
    core = dp % 2
    other = 1 - core
    chip = dp // 2
    mate_id = 2 * chip + other
    barrier = pltpu.get_barrier_semaphore()

    def greet(k, carry):
        pl.semaphore_signal(
            barrier, inc=1, device_id=(lax.rem(dp + k, n), mp), device_id_type=MESH
        )
        return carry

    lax.fori_loop(1, n, greet, 0)
    pl.semaphore_wait(barrier, n - 1)
    own = pltpu.make_async_copy(y_ref.at[dp], out_same.at[0], sl)
    own.start()

    def remote(src, dst, send, recv, target):
        return pltpu.make_async_remote_copy(
            src_ref=src, dst_ref=dst, send_sem=send, recv_sem=recv,
            device_id=(target, mp), device_id_type=MESH,
        )

    def target(j, c):
        return 2 * lax.rem(chip + j, chips) + c

    slot_of = {j: i + 1 for i, j in enumerate(direct)}
    forwarded = [j for j in range(1, chips) if j not in direct]

    def same(j):
        src = y_ref.at[target(j, core)] if j in direct else sbuf.at[j]
        return remote(src, out_same.at[j], ss.at[j], rs.at[j], target(j, core))

    def cross(j):
        i = slot_of[j]
        return remote(y_ref.at[target(j, other)], out_cross.at[i], sc.at[i], rc.at[i], target(j, other))

    def relay(j):
        return remote(y_ref.at[target(j, other)], pin.at[j], sr.at[j], rr.at[j], mate_id)

    mate = remote(y_ref.at[mate_id], out_cross.at[0], sc.at[0], rc.at[0], mate_id)
    for j in forwarded:
        relay(j).start()
    mate.start()
    for j in direct:
        cross(j).start()
        same(j).start()
    for j in forwarded:
        relay(j).wait_recv()
        total = y_ref[target(j, core)].astype(jnp.float32) + pin[j].astype(jnp.float32)
        sbuf[j] = total.astype(sbuf.dtype)
        same(j).start()
    for j in forwarded:
        relay(j).wait_send()
    for j in range(1, chips):
        same(j).wait()
    for j in direct:
        cross(j).wait()
    mate.wait()
    own.wait()


def relay_reduce(y, n, collective_id):
    chips = n // 2
    direct = tuple(j for j in range(1, chips) if j % 4 == 0)
    block = tuple(y.shape[1:])
    block_bytes = y.dtype.itemsize
    for d in block:
        block_bytes *= d
    same, cross = pl.pallas_call(
        functools.partial(relay_reduce_kernel, chips, direct),
        out_shape=(
            jax.ShapeDtypeStruct((chips,) + block, y.dtype),
            jax.ShapeDtypeStruct((len(direct) + 1,) + block, y.dtype),
        ),
        in_specs=[pl.BlockSpec(memory_space=pltpu.VMEM)],
        out_specs=(pl.BlockSpec(memory_space=pl.ANY), pl.BlockSpec(memory_space=pl.ANY)),
        scratch_shapes=[pltpu.VMEM((chips,) + block, y.dtype)] * 2
        + [pltpu.SemaphoreType.DMA((chips,))] * 6
        + [pltpu.SemaphoreType.DMA(())],
        compiler_params=pltpu.CompilerParams(collective_id=collective_id, has_side_effects=True),
        cost_estimate=pl.CostEstimate(flops=0, bytes_accessed=3 * n * block_bytes, transcendentals=0),
    )(y)
    return jnp.sum(same.astype(jnp.float32), axis=0) + jnp.sum(cross.astype(jnp.float32), axis=0)


def padded_rows(size, dtype_rows=16):
    rows = -(-size // LANES)
    return -(-rows // dtype_rows) * dtype_rows


def shard_sizes(w_qkv, w_proj, w_in, w_out, w_router, ln_gain, ln_bias):
    return [a.size for a in (w_qkv, w_proj, w_in, w_out, w_router, ln_gain, ln_bias)]


def gather_weights(w_qkv, w_proj, w_in, w_out, w_router, ln_gain, ln_bias, n):
    parts = (w_qkv, w_proj, w_in, w_out, w_router, ln_gain, ln_bias)
    flat = jnp.concatenate([a.reshape(-1) for a in parts])
    total = flat.shape[0]
    rows = padded_rows(total)
    flat = jnp.pad(flat, (0, rows * LANES - total)).reshape(rows, LANES)
    full = relay_gather(flat, n, 0).reshape(n, rows * LANES)
    pieces = []
    start = 0
    for a in parts:
        pieces.append(full[:, start:start + a.size].reshape((n,) + a.shape[1:]))
        start += a.size
    q, p, i, o, r, g, b = pieces
    gq = q.reshape((-1,) + w_qkv.shape[2:])
    gr = r.reshape((-1,) + w_router.shape[2:])
    gg = g.transpose(1, 0, 2).reshape(ln_gain.shape[1], -1)
    gb = b.transpose(1, 0, 2).reshape(ln_bias.shape[1], -1)
    return (gq, p, i, o, gr, gg, gb)


def scatter_grads(grads, n, shapes):
    gq, gp, gi, go, gr, gg, gb = grads
    rows = [
        gq.reshape(n, -1),
        gp.reshape(n, -1),
        gi.reshape(n, -1),
        go.reshape(n, -1),
        gr.reshape(n, -1),
        gg.reshape(gg.shape[0], n, -1).transpose(1, 0, 2).reshape(n, -1),
        gb.reshape(gb.shape[0], n, -1).transpose(1, 0, 2).reshape(n, -1),
    ]
    packed = jnp.concatenate(rows, axis=1)
    total = packed.shape[1]
    count = padded_rows(total)
    packed = jnp.pad(packed, ((0, 0), (0, count * LANES - total))).reshape(n, count, LANES)
    mine = relay_reduce(packed.astype(jnp.bfloat16), n, 1).reshape(-1)
    outs = []
    start = 0
    for shape in shapes:
        size = 1
        for d in shape:
            size *= d
        outs.append(mine[start:start + size].reshape(shape))
        start += size
    return outs


def layer_forward(field, chosen_ids, weights):
    w_qkv, w_proj, w_in, w_out, w_router, ln_gain, ln_bias = weights
    image_count, length, model_width = field.shape
    row_count = image_count * length
    head_count = w_qkv.shape[2] // HD
    score_scale = HD ** (-0.5)
    gain_rows = ln_gain.astype(jnp.float32)
    shift_rows = ln_bias.astype(jnp.float32)
    flat = field.reshape(row_count, model_width)
    first, normed_one, inverse_one = norm_forward(flat, gain_rows[0], shift_rows[0])
    first = first.astype(jnp.bfloat16)
    projected = jnp.einsum("rd,dcf->rcf", first, w_qkv, preferred_element_type=jnp.float32).astype(
        jnp.bfloat16
    )
    projected = projected.reshape(image_count, length, 3, head_count, HD)
    queries = projected[:, :, 0]
    key_rows = projected[:, :, 1]
    value_rows = projected[:, :, 2]
    scores = (
        jnp.einsum("bqhe,bkhe->bhqk", queries, key_rows, preferred_element_type=jnp.float32)
        * score_scale
    )
    log_total = jax.nn.logsumexp(scores, axis=-1)
    attn_weights = jnp.exp(scores - log_total[..., None]).astype(jnp.bfloat16)
    attended = jnp.einsum(
        "bhqk,bkhe->bqhe", attn_weights, value_rows, preferred_element_type=jnp.float32
    )
    attended = attended.astype(jnp.bfloat16).reshape(row_count, head_count * HD)
    partial_attn = jnp.einsum(
        "rf,jfk->rjk", attended, w_proj, preferred_element_type=jnp.float32
    ).reshape(row_count, model_width)
    hidden = flat + lax.psum(partial_attn, "mp")
    second, normed_two, inverse_two = norm_forward(hidden, gain_rows[1], shift_rows[1])
    second = second.astype(jnp.bfloat16)
    logits = jnp.dot(second, w_router, preferred_element_type=jnp.float32)
    router = jax.nn.softmax(logits, axis=-1)
    labels = jnp.arange(EXPERTS, dtype=jnp.int32)
    ids_flat = chosen_ids.reshape(row_count, TOPK)
    chosen = (ids_flat[:, :, None] == labels).astype(jnp.float32)
    gate_values = jnp.sum(router[:, None, :] * chosen, axis=-1)
    per_image = EXPERTS * CAP
    image_base = (jnp.arange(image_count, dtype=jnp.int32) * per_image)[:, None, None]
    slot_index = (chosen_ids * CAP + slot_positions(chosen_ids) + image_base).reshape(-1)
    owners = (
        jnp.full((image_count * per_image,), row_count, jnp.int32)
        .at[slot_index]
        .set(jnp.repeat(jnp.arange(row_count, dtype=jnp.int32), TOPK))
    )
    slot_gate = (
        jnp.zeros((image_count * per_image,), jnp.float32).at[slot_index].set(gate_values.reshape(-1))
    )
    padded = jnp.concatenate([second, jnp.zeros((1, model_width), jnp.bfloat16)], axis=0)
    slot_rows = jnp.take(padded, owners, axis=0).reshape(image_count, EXPERTS, CAP, model_width)
    slot_split = slot_rows.reshape(slot_rows.shape[:3] + w_in.shape[:1] + w_in.shape[2:3])
    inner_pre = jnp.einsum("becjk,jekf->becf", slot_split, w_in, preferred_element_type=jnp.float32)
    activated = jax.nn.gelu(inner_pre, approximate=False).astype(jnp.bfloat16)
    produced = jnp.einsum("becf,jefk->becjk", activated, w_out, preferred_element_type=jnp.float32)
    produced = produced.reshape(image_count * per_image, model_width)
    picked = jnp.take(produced, slot_index, axis=0).reshape(row_count, TOPK, model_width)
    partial_moe = jnp.sum(gate_values[:, :, None] * picked, axis=1)
    output = hidden + lax.psum(partial_moe.astype(jnp.bfloat16), "mp").astype(jnp.float32)
    record = (
        normed_one, inverse_one, first, projected, log_total, attended, normed_two, inverse_two,
        second, router, chosen, slot_index, owners, slot_gate, slot_rows, inner_pre, activated, picked,
    )
    return (output.reshape(image_count, length, model_width), record)


def layer_backward(grad_field, record, weights):
    w_qkv, w_proj, w_in, w_out, w_router, ln_gain, ln_bias = weights
    (
        normed_one, inverse_one, first, projected, log_total, attended, normed_two, inverse_two,
        second, router, chosen, slot_index, owners, slot_gate, slot_rows, inner_pre, activated, picked,
    ) = record
    image_count, length, model_width = grad_field.shape
    row_count = image_count * length
    head_count = projected.shape[3]
    score_scale = HD ** (-0.5)
    gain_rows = ln_gain.astype(jnp.float32)
    grad_flat = grad_field.reshape(row_count, model_width)
    padded_grad = jnp.concatenate([grad_flat, jnp.zeros((1, model_width), jnp.float32)], axis=0)
    grad_slots = (jnp.take(padded_grad, owners, axis=0) * slot_gate[:, None]).astype(jnp.bfloat16)
    split = (w_out.shape[0], w_out.shape[3])
    grad_slots = grad_slots.reshape((image_count, EXPERTS, CAP) + split)
    slot_split = slot_rows.reshape((image_count, EXPERTS, CAP) + split)
    grad_w_out = jnp.einsum(
        "becf,becjk->jefk", activated, grad_slots, preferred_element_type=jnp.float32
    )
    grad_act = jnp.einsum("becjk,jefk->becf", grad_slots, w_out, preferred_element_type=jnp.float32)
    grad_inner = (grad_act * gelu_slope(inner_pre)).astype(jnp.bfloat16)
    grad_w_in = jnp.einsum(
        "becjk,becf->jekf", slot_split, grad_inner, preferred_element_type=jnp.float32
    )
    grad_slot_rows = jnp.einsum(
        "becf,jekf->becjk", grad_inner, w_in, preferred_element_type=jnp.float32
    )
    grad_slot_rows = grad_slot_rows.reshape(image_count * EXPERTS * CAP, model_width)
    partial_second = jnp.sum(
        jnp.take(grad_slot_rows, slot_index, axis=0).reshape(row_count, TOPK, model_width), axis=1
    )
    partial_gate = jnp.sum(picked * grad_flat[:, None, :], axis=-1)
    grad_second, grad_gate = lax.psum((partial_second, partial_gate), "mp")
    grad_router = jnp.sum(grad_gate[:, :, None] * chosen, axis=1)
    grad_logits = router * (grad_router - jnp.sum(router * grad_router, axis=-1, keepdims=True))
    grad_logits = grad_logits.astype(jnp.bfloat16)
    grad_w_router = jnp.dot(second.T, grad_logits, preferred_element_type=jnp.float32)
    grad_second = grad_second + jnp.dot(grad_logits, w_router.T, preferred_element_type=jnp.float32)
    grad_from_norm, grad_gain_two, grad_shift_two = norm_backward(
        grad_second, normed_two, inverse_two, gain_rows[1]
    )
    grad_hidden = grad_flat + grad_from_norm
    grad_hidden_low = grad_hidden.astype(jnp.bfloat16)
    grad_hidden_split = grad_hidden_low.reshape((row_count,) + split)
    grad_w_proj = jnp.einsum(
        "rf,rjk->jfk", attended, grad_hidden_split, preferred_element_type=jnp.float32
    )
    grad_attended = jnp.einsum(
        "rjk,jfk->rf", grad_hidden_split, w_proj, preferred_element_type=jnp.float32
    ).astype(jnp.bfloat16)
    grad_attended = grad_attended.reshape(image_count, length, head_count, HD)
    queries = projected[:, :, 0]
    key_rows = projected[:, :, 1]
    value_rows = projected[:, :, 2]
    scores = (
        jnp.einsum("bqhe,bkhe->bhqk", queries, key_rows, preferred_element_type=jnp.float32)
        * score_scale
    )
    probs = jnp.exp(scores - log_total[..., None])
    grad_values = jnp.einsum(
        "bhqk,bqhe->bkhe", probs.astype(jnp.bfloat16), grad_attended,
        preferred_element_type=jnp.float32,
    )
    grad_probs = jnp.einsum(
        "bqhe,bkhe->bhqk", grad_attended, value_rows, preferred_element_type=jnp.float32
    )
    grad_scores = (
        probs * (grad_probs - jnp.sum(probs * grad_probs, axis=-1, keepdims=True))
    ).astype(jnp.bfloat16)
    grad_queries = (
        jnp.einsum("bhqk,bkhe->bqhe", grad_scores, key_rows, preferred_element_type=jnp.float32)
        * score_scale
    )
    grad_keys = (
        jnp.einsum("bhqk,bqhe->bkhe", grad_scores, queries, preferred_element_type=jnp.float32)
        * score_scale
    )
    grad_projected = jnp.stack([grad_queries, grad_keys, grad_values], axis=2).astype(jnp.bfloat16)
    grad_projected = grad_projected.reshape(row_count, 3, head_count * HD)
    grad_w_qkv = jnp.einsum(
        "rd,rcf->dcf", first, grad_projected, preferred_element_type=jnp.float32
    )
    partial_first = jnp.einsum(
        "rcf,dcf->rd", grad_projected, w_qkv, preferred_element_type=jnp.float32
    )
    grad_first = lax.psum(partial_first.astype(jnp.bfloat16), "mp").astype(jnp.float32)
    grad_input_norm, grad_gain_one, grad_shift_one = norm_backward(
        grad_first, normed_one, inverse_one, gain_rows[0]
    )
    grad_input = grad_hidden + grad_input_norm
    grads = (
        grad_w_qkv,
        grad_w_proj,
        grad_w_in,
        grad_w_out,
        grad_w_router,
        jnp.stack([grad_gain_one, grad_gain_two]),
        jnp.stack([grad_shift_one, grad_shift_two]),
    )
    return (grad_input.reshape(image_count, length, model_width), grads)


def make_local(n):
    def local(images, routes, w_qkv, w_proj, w_in, w_out, w_router, ln_gain, ln_bias, cotangent):
        shapes = [a.shape for a in (w_qkv, w_proj, w_in, w_out, w_router, ln_gain, ln_bias)]
        weights = gather_weights(w_qkv, w_proj, w_in, w_out, w_router, ln_gain, ln_bias, n)
        field = images.astype(jnp.float32)
        output, record = layer_forward(field, routes[0], weights)
        grad_input, grads = layer_backward(cotangent.astype(jnp.float32), record, weights)
        shards = scatter_grads(grads, n, [(1,) + tuple(s[1:]) for s in shapes])
        return (output, grad_input, *shards)

    return local


def solution(mesh):
    n = mesh.shape["dp"]
    in_specs = (
        P("dp", None, None),
        P(None, "dp", None, None),
        P(None, "dp", None, "mp"),
        P(None, "mp", "dp"),
        P(None, None, "dp", "mp"),
        P(None, None, "mp", "dp"),
        P(None, "dp", None),
        P(None, None, "dp"),
        P(None, None, "dp"),
        P("dp", None, None),
    )
    out_specs = (
        P("dp", None, None),
        P("dp", None, None),
        P(None, "dp", None, "mp"),
        P(None, "mp", "dp"),
        P(None, None, "dp", "mp"),
        P(None, None, "mp", "dp"),
        P(None, "dp", None),
        P(None, None, "dp"),
        P(None, None, "dp"),
    )
    return jax.shard_map(make_local(n), mesh=mesh, in_specs=in_specs, out_specs=out_specs, check_vma=False)
```

```python
import functools

import jax
import jax.numpy as jnp
from jax import lax
from jax.sharding import PartitionSpec as P
from jax.experimental import pallas as pl
from jax.experimental.pallas import tpu as pltpu

MESH = pl.DeviceIdType.MESH
LANES = 128

HD = 64
EXPERTS = 4
TOPK = 2
CAP = 104
EPSILON = 1e-06


def norm_forward(field, gain_row, shift_row):
    mean_value = jnp.mean(field, axis=-1, keepdims=True)
    centered = field - mean_value
    inverse = lax.rsqrt(jnp.mean(centered * centered, axis=-1, keepdims=True) + EPSILON)
    normed = centered * inverse
    return (normed * gain_row + shift_row, normed, inverse)


def norm_backward(grad_out, normed, inverse, gain_row):
    grad_gain = jnp.sum(grad_out * normed, axis=0)
    grad_shift = jnp.sum(grad_out, axis=0)
    scaled = grad_out * gain_row
    grad_in = inverse * (
        scaled
        - jnp.mean(scaled, axis=-1, keepdims=True)
        - normed * jnp.mean(scaled * normed, axis=-1, keepdims=True)
    )
    return (grad_in, grad_gain, grad_shift)


def slot_positions(chosen_ids):
    labels = jnp.arange(EXPERTS, dtype=jnp.int32)
    hit_counts = jnp.sum((chosen_ids[..., None] == labels).astype(jnp.int32), axis=-2)
    before = jnp.cumsum(hit_counts, axis=1) - hit_counts
    return jnp.take_along_axis(before, chosen_ids, axis=-1)


def gelu_slope(inner_pre):
    cumulative = 0.5 * (1.0 + jax.scipy.special.erf(inner_pre * 0.7071067811865476))
    density = jnp.exp(-0.5 * inner_pre * inner_pre) * 0.3989422804014327
    return cumulative + inner_pre * density


def group_of(kind):
    def chips():
        dp, mp = lax.axis_index("dp"), lax.axis_index("mp")
        return dp // 2, lambda i: (2 * i + dp % 2, mp)

    def cores():
        dp, mp = lax.axis_index("dp"), lax.axis_index("mp")
        return dp % 2, lambda i: (2 * (dp // 2) + i, mp)

    def whole():
        dp, mp = lax.axis_index("dp"), lax.axis_index("mp")
        return dp, lambda i: (i, mp)

    def pair():
        dp, mp = lax.axis_index("dp"), lax.axis_index("mp")
        return mp, lambda i: (dp, i)

    return {"chips": chips, "cores": cores, "pair": pair, "all": whole}[kind]


def exchange_kernel(m, pieces, gather, kind, x_ref, out_ref, send_sem, recv_sem, local_sem):
    me, device_of = group_of(kind)()
    step = out_ref.shape[1] // pieces
    barrier = pltpu.get_barrier_semaphore()

    def greet(k, carry):
        pl.semaphore_signal(
            barrier, inc=1, device_id=device_of(lax.rem(me + k, m)), device_id_type=MESH
        )
        return carry

    lax.fori_loop(1, m, greet, 0)
    pl.semaphore_wait(barrier, m - 1)
    own = pltpu.make_async_copy(x_ref if gather else x_ref.at[me], out_ref.at[me], local_sem)
    own.start()

    def describe(t):
        k = 1 + t // pieces
        part = pl.ds(pl.multiple_of((t % pieces) * step, step), step)
        peer = lax.rem(me + k, m)
        return pltpu.make_async_remote_copy(
            src_ref=x_ref.at[part] if gather else x_ref.at[peer, part],
            dst_ref=out_ref.at[me, part],
            send_sem=send_sem.at[t],
            recv_sem=recv_sem.at[t],
            device_id=device_of(peer),
            device_id_type=MESH,
        )

    def start(t, carry):
        describe(t).start()
        return carry

    def finish(t, carry):
        describe(t).wait()
        return carry

    count = (m - 1) * pieces
    lax.fori_loop(0, count, start, 0)
    lax.fori_loop(0, count, finish, 0)
    own.wait()


def exchange(x, m, gather, kind, collective_id, pieces=1):
    block = x.shape if gather else x.shape[1:]
    block_bytes = x.dtype.itemsize
    for d in block:
        block_bytes *= d
    count = (m - 1) * pieces
    return pl.pallas_call(
        functools.partial(exchange_kernel, m, pieces, gather, kind),
        out_shape=jax.ShapeDtypeStruct((m,) + tuple(block), x.dtype),
        in_specs=[pl.BlockSpec(memory_space=pl.ANY)],
        out_specs=pl.BlockSpec(memory_space=pl.ANY),
        scratch_shapes=[
            pltpu.SemaphoreType.DMA((count,)),
            pltpu.SemaphoreType.DMA((count,)),
            pltpu.SemaphoreType.DMA(()),
        ],
        compiler_params=pltpu.CompilerParams(collective_id=collective_id, has_side_effects=True),
        cost_estimate=pl.CostEstimate(flops=0, bytes_accessed=2 * m * block_bytes, transcendentals=0),
    )(x)


def relay_gather_kernel(chips, direct, x_ref, out_ref, sa, ra, sb, rb, sf, rf, sp, rp, sl):
    dp, mp = lax.axis_index("dp"), lax.axis_index("mp")
    n = 2 * chips
    core = dp % 2
    other = 1 - core
    chip = dp // 2
    barrier = pltpu.get_barrier_semaphore()

    def greet(k, carry):
        pl.semaphore_signal(
            barrier, inc=1, device_id=(lax.rem(dp + k, n), mp), device_id_type=MESH
        )
        return carry

    lax.fori_loop(1, n, greet, 0)
    pl.semaphore_wait(barrier, n - 1)
    own = pltpu.make_async_copy(x_ref, out_ref.at[dp], sl)
    own.start()

    def remote(src, dst, send, recv, target):
        return pltpu.make_async_remote_copy(
            src_ref=src, dst_ref=dst, send_sem=send, recv_sem=recv,
            device_id=(target, mp), device_id_type=MESH,
        )

    def same(j):
        return remote(x_ref, out_ref.at[dp], sa.at[j], ra.at[j], 2 * lax.rem(chip + j, chips) + core)

    def cross(j):
        return remote(x_ref, out_ref.at[dp], sb.at[j], rb.at[j], 2 * lax.rem(chip + j, chips) + other)

    def relay(j):
        slot = 2 * lax.rem(chip + chips - j, chips) + core
        return remote(out_ref.at[slot], out_ref.at[slot], sf.at[j], rf.at[j], 2 * chip + other)

    mate = remote(x_ref, out_ref.at[dp], sp, rp, 2 * chip + other)
    forwarded = [j for j in range(1, chips) if j not in direct]
    mate.start()
    for j in forwarded:
        same(j).start()
    for j in direct:
        cross(j).start()
    for j in direct:
        same(j).start()
    for j in forwarded:
        same(j).wait_recv()
        relay(j).start()
    for j in direct:
        same(j).wait_recv()
    for j in range(1, chips):
        same(j).wait_send()
    for j in direct:
        cross(j).wait()
    mate.wait()
    for j in forwarded:
        relay(j).wait()
    own.wait()


def relay_gather(x, n, collective_id):
    chips = n // 2
    direct = tuple(j for j in range(1, chips) if j % 4 == 0)
    block_bytes = x.dtype.itemsize
    for d in x.shape:
        block_bytes *= d
    return pl.pallas_call(
        functools.partial(relay_gather_kernel, chips, direct),
        out_shape=jax.ShapeDtypeStruct((n,) + tuple(x.shape), x.dtype),
        in_specs=[pl.BlockSpec(memory_space=pl.ANY)],
        out_specs=pl.BlockSpec(memory_space=pl.ANY),
        scratch_shapes=[pltpu.SemaphoreType.DMA((chips,))] * 6
        + [pltpu.SemaphoreType.DMA(())] * 3,
        compiler_params=pltpu.CompilerParams(collective_id=collective_id, has_side_effects=True),
        cost_estimate=pl.CostEstimate(flops=0, bytes_accessed=2 * n * block_bytes, transcendentals=0),
    )(x)


def relay_reduce_kernel(chips, direct, y_ref, total_ref, out_same, out_cross, pin, sbuf, ss, rs, sc, rc, sr, rr):
    dp, mp = lax.axis_index("dp"), lax.axis_index("mp")
    n = 2 * chips
    core = dp % 2
    other = 1 - core
    chip = dp // 2
    mate_id = 2 * chip + other
    barrier = pltpu.get_barrier_semaphore()

    def greet(k, carry):
        pl.semaphore_signal(
            barrier, inc=1, device_id=(lax.rem(dp + k, n), mp), device_id_type=MESH
        )
        return carry

    lax.fori_loop(1, n, greet, 0)
    pl.semaphore_wait(barrier, n - 1)

    def remote(src, dst, send, recv, target):
        return pltpu.make_async_remote_copy(
            src_ref=src, dst_ref=dst, send_sem=send, recv_sem=recv,
            device_id=(target, mp), device_id_type=MESH,
        )

    def target(j, c):
        return 2 * lax.rem(chip + j, chips) + c

    slot_of = {j: i + 1 for i, j in enumerate(direct)}
    forwarded = [j for j in range(1, chips) if j not in direct]

    def same(j):
        src = y_ref.at[target(j, core)] if j in direct else sbuf.at[j]
        return remote(src, out_same.at[j], ss.at[j], rs.at[j], target(j, core))

    def cross(j):
        i = slot_of[j]
        return remote(y_ref.at[target(j, other)], out_cross.at[i], sc.at[i], rc.at[i], target(j, other))

    def relay(j):
        return remote(y_ref.at[target(j, other)], pin.at[j], sr.at[j], rr.at[j], mate_id)

    mate = remote(y_ref.at[mate_id], out_cross.at[0], sc.at[0], rc.at[0], mate_id)
    for j in forwarded:
        relay(j).start()
    mate.start()
    for j in direct:
        cross(j).start()
        same(j).start()
    for j in forwarded:
        relay(j).wait_recv()
        total = y_ref[target(j, core)].astype(jnp.float32) + pin[j].astype(jnp.float32)
        sbuf[j] = total.astype(sbuf.dtype)
        same(j).start()
    for j in forwarded:
        relay(j).wait_send()
    for j in range(1, chips):
        same(j).wait()
    for j in direct:
        cross(j).wait()
    mate.wait()
    total = lax.fori_loop(
        1, chips, lambda j, t: t + out_same[j].astype(jnp.float32), y_ref[dp].astype(jnp.float32)
    )
    total = lax.fori_loop(
        0, len(direct) + 1, lambda i, t: t + out_cross[i].astype(jnp.float32), total
    )
    total_ref[...] = total


def relay_reduce(y, n, collective_id):
    chips = n // 2
    direct = tuple(j for j in range(1, chips) if j % 4 == 0)
    block = tuple(y.shape[1:])
    block_bytes = y.dtype.itemsize
    for d in block:
        block_bytes *= d
    return pl.pallas_call(
        functools.partial(relay_reduce_kernel, chips, direct),
        out_shape=jax.ShapeDtypeStruct(block, jnp.float32),
        in_specs=[pl.BlockSpec(memory_space=pltpu.VMEM)],
        out_specs=pl.BlockSpec(memory_space=pltpu.VMEM),
        scratch_shapes=[
            pltpu.VMEM((chips,) + block, y.dtype),
            pltpu.VMEM((len(direct) + 1,) + block, y.dtype),
            pltpu.VMEM((chips,) + block, y.dtype),
            pltpu.VMEM((chips,) + block, y.dtype),
        ]
        + [pltpu.SemaphoreType.DMA((chips,))] * 6,
        compiler_params=pltpu.CompilerParams(collective_id=collective_id, has_side_effects=True),
        cost_estimate=pl.CostEstimate(flops=0, bytes_accessed=3 * n * block_bytes, transcendentals=0),
    )(y)


def pair_sum(parts, collective_id):
    dtype = parts[0].dtype
    flat = jnp.concatenate([p.reshape(-1) for p in parts])
    total = flat.shape[0]
    rows = padded_rows(total, 16 if dtype == jnp.bfloat16 else 8)
    flat = jnp.pad(flat, (0, rows * LANES - total)).reshape(rows, LANES)
    both = exchange(flat, 2, True, "pair", collective_id).astype(jnp.float32)
    summed = (both[0] + both[1]).reshape(-1)
    outs = []
    start = 0
    for p in parts:
        outs.append(summed[start:start + p.size].reshape(p.shape))
        start += p.size
    return outs


def padded_rows(size, dtype_rows=16):
    rows = -(-size // LANES)
    return -(-rows // dtype_rows) * dtype_rows


def shard_sizes(w_qkv, w_proj, w_in, w_out, w_router, ln_gain, ln_bias):
    return [a.size for a in (w_qkv, w_proj, w_in, w_out, w_router, ln_gain, ln_bias)]


def gather_weights(w_qkv, w_proj, w_in, w_out, w_router, ln_gain, ln_bias, n):
    parts = (w_qkv, w_proj, w_in, w_out, w_router, ln_gain, ln_bias)
    flat = jnp.concatenate([a.reshape(-1) for a in parts])
    total = flat.shape[0]
    rows = padded_rows(total)
    flat = jnp.pad(flat, (0, rows * LANES - total)).reshape(rows, LANES)
    full = relay_gather(flat, n, 0).reshape(n, rows * LANES)
    pieces = []
    start = 0
    for a in parts:
        pieces.append(full[:, start:start + a.size].reshape((n,) + a.shape[1:]))
        start += a.size
    q, p, i, o, r, g, b = pieces
    gq = q.reshape((-1,) + w_qkv.shape[2:])
    gr = r.reshape((-1,) + w_router.shape[2:])
    gg = g.transpose(1, 0, 2).reshape(ln_gain.shape[1], -1)
    gb = b.transpose(1, 0, 2).reshape(ln_bias.shape[1], -1)
    return (gq, p, i, o, gr, gg, gb)


def scatter_grads(grads, n, shapes):
    gq, gp, gi, go, gr, gg, gb = grads
    rows = [
        gq.reshape(n, -1),
        gp.reshape(n, -1),
        gi.reshape(n, -1),
        go.reshape(n, -1),
        gr.reshape(n, -1),
        gg.reshape(gg.shape[0], n, -1).transpose(1, 0, 2).reshape(n, -1),
        gb.reshape(gb.shape[0], n, -1).transpose(1, 0, 2).reshape(n, -1),
    ]
    packed = jnp.concatenate(rows, axis=1)
    total = packed.shape[1]
    count = padded_rows(total)
    packed = jnp.pad(packed, ((0, 0), (0, count * LANES - total))).reshape(n, count, LANES)
    mine = relay_reduce(packed.astype(jnp.bfloat16), n, 1).reshape(-1)
    outs = []
    start = 0
    for shape in shapes:
        size = 1
        for d in shape:
            size *= d
        outs.append(mine[start:start + size].reshape(shape))
        start += size
    return outs


def layer_forward(field, chosen_ids, weights):
    w_qkv, w_proj, w_in, w_out, w_router, ln_gain, ln_bias = weights
    image_count, length, model_width = field.shape
    row_count = image_count * length
    head_count = w_qkv.shape[2] // HD
    score_scale = HD ** (-0.5)
    gain_rows = ln_gain.astype(jnp.float32)
    shift_rows = ln_bias.astype(jnp.float32)
    flat = field.reshape(row_count, model_width)
    first, normed_one, inverse_one = norm_forward(flat, gain_rows[0], shift_rows[0])
    first = first.astype(jnp.bfloat16)
    projected = jnp.einsum("rd,dcf->rcf", first, w_qkv, preferred_element_type=jnp.float32).astype(
        jnp.bfloat16
    )
    projected = projected.reshape(image_count, length, 3, head_count, HD)
    queries = projected[:, :, 0]
    key_rows = projected[:, :, 1]
    value_rows = projected[:, :, 2]
    scores = (
        jnp.einsum("bqhe,bkhe->bhqk", queries, key_rows, preferred_element_type=jnp.float32)
        * score_scale
    )
    log_total = jax.nn.logsumexp(scores, axis=-1)
    attn_weights = jnp.exp(scores - log_total[..., None]).astype(jnp.bfloat16)
    attended = jnp.einsum(
        "bhqk,bkhe->bqhe", attn_weights, value_rows, preferred_element_type=jnp.float32
    )
    attended = attended.astype(jnp.bfloat16).reshape(row_count, head_count * HD)
    partial_attn = jnp.einsum(
        "rf,jfk->rjk", attended, w_proj, preferred_element_type=jnp.float32
    ).reshape(row_count, model_width)
    hidden = flat + lax.psum(partial_attn, "mp")
    second, normed_two, inverse_two = norm_forward(hidden, gain_rows[1], shift_rows[1])
    second = second.astype(jnp.bfloat16)
    logits = jnp.dot(second, w_router, preferred_element_type=jnp.float32)
    router = jax.nn.softmax(logits, axis=-1)
    labels = jnp.arange(EXPERTS, dtype=jnp.int32)
    ids_flat = chosen_ids.reshape(row_count, TOPK)
    chosen = (ids_flat[:, :, None] == labels).astype(jnp.float32)
    gate_values = jnp.sum(router[:, None, :] * chosen, axis=-1)
    per_image = EXPERTS * CAP
    image_base = (jnp.arange(image_count, dtype=jnp.int32) * per_image)[:, None, None]
    slot_index = (chosen_ids * CAP + slot_positions(chosen_ids) + image_base).reshape(-1)
    owners = (
        jnp.full((image_count * per_image,), row_count, jnp.int32)
        .at[slot_index]
        .set(jnp.repeat(jnp.arange(row_count, dtype=jnp.int32), TOPK))
    )
    slot_gate = (
        jnp.zeros((image_count * per_image,), jnp.float32).at[slot_index].set(gate_values.reshape(-1))
    )
    padded = jnp.concatenate([second, jnp.zeros((1, model_width), jnp.bfloat16)], axis=0)
    slot_rows = jnp.take(padded, owners, axis=0).reshape(image_count, EXPERTS, CAP, model_width)
    slot_split = slot_rows.reshape(slot_rows.shape[:3] + w_in.shape[:1] + w_in.shape[2:3])
    inner_pre = jnp.einsum("becjk,jekf->becf", slot_split, w_in, preferred_element_type=jnp.float32)
    activated = jax.nn.gelu(inner_pre, approximate=False).astype(jnp.bfloat16)
    produced = jnp.einsum("becf,jefk->becjk", activated, w_out, preferred_element_type=jnp.float32)
    produced = produced.reshape(image_count * per_image, model_width)
    picked = jnp.take(produced, slot_index, axis=0).reshape(row_count, TOPK, model_width)
    partial_moe = jnp.sum(gate_values[:, :, None] * picked, axis=1)
    output = hidden + lax.psum(partial_moe.astype(jnp.bfloat16), "mp").astype(jnp.float32)
    record = (
        normed_one, inverse_one, first, projected, log_total, attended, normed_two, inverse_two,
        second, router, chosen, slot_index, owners, slot_gate, slot_rows, inner_pre, activated, picked,
    )
    return (output.reshape(image_count, length, model_width), record)


def layer_backward(grad_field, record, weights):
    w_qkv, w_proj, w_in, w_out, w_router, ln_gain, ln_bias = weights
    (
        normed_one, inverse_one, first, projected, log_total, attended, normed_two, inverse_two,
        second, router, chosen, slot_index, owners, slot_gate, slot_rows, inner_pre, activated, picked,
    ) = record
    image_count, length, model_width = grad_field.shape
    row_count = image_count * length
    head_count = projected.shape[3]
    score_scale = HD ** (-0.5)
    gain_rows = ln_gain.astype(jnp.float32)
    grad_flat = grad_field.reshape(row_count, model_width)
    padded_grad = jnp.concatenate([grad_flat, jnp.zeros((1, model_width), jnp.float32)], axis=0)
    grad_slots = (jnp.take(padded_grad, owners, axis=0) * slot_gate[:, None]).astype(jnp.bfloat16)
    split = (w_out.shape[0], w_out.shape[3])
    grad_slots = grad_slots.reshape((image_count, EXPERTS, CAP) + split)
    slot_split = slot_rows.reshape((image_count, EXPERTS, CAP) + split)
    grad_w_out = jnp.einsum(
        "becf,becjk->jefk", activated, grad_slots, preferred_element_type=jnp.float32
    )
    grad_act = jnp.einsum("becjk,jefk->becf", grad_slots, w_out, preferred_element_type=jnp.float32)
    grad_inner = (grad_act * gelu_slope(inner_pre)).astype(jnp.bfloat16)
    grad_w_in = jnp.einsum(
        "becjk,becf->jekf", slot_split, grad_inner, preferred_element_type=jnp.float32
    )
    grad_slot_rows = jnp.einsum(
        "becf,jekf->becjk", grad_inner, w_in, preferred_element_type=jnp.float32
    )
    grad_slot_rows = grad_slot_rows.reshape(image_count * EXPERTS * CAP, model_width)
    partial_second = jnp.sum(
        jnp.take(grad_slot_rows, slot_index, axis=0).reshape(row_count, TOPK, model_width), axis=1
    )
    partial_gate = jnp.sum(picked * grad_flat[:, None, :], axis=-1)
    grad_second, grad_gate = pair_sum((partial_second, partial_gate), 2)
    grad_router = jnp.sum(grad_gate[:, :, None] * chosen, axis=1)
    grad_logits = router * (grad_router - jnp.sum(router * grad_router, axis=-1, keepdims=True))
    grad_logits = grad_logits.astype(jnp.bfloat16)
    grad_w_router = jnp.dot(second.T, grad_logits, preferred_element_type=jnp.float32)
    grad_second = grad_second + jnp.dot(grad_logits, w_router.T, preferred_element_type=jnp.float32)
    grad_from_norm, grad_gain_two, grad_shift_two = norm_backward(
        grad_second, normed_two, inverse_two, gain_rows[1]
    )
    grad_hidden = grad_flat + grad_from_norm
    grad_hidden_low = grad_hidden.astype(jnp.bfloat16)
    grad_hidden_split = grad_hidden_low.reshape((row_count,) + split)
    grad_w_proj = jnp.einsum(
        "rf,rjk->jfk", attended, grad_hidden_split, preferred_element_type=jnp.float32
    )
    grad_attended = jnp.einsum(
        "rjk,jfk->rf", grad_hidden_split, w_proj, preferred_element_type=jnp.float32
    ).astype(jnp.bfloat16)
    grad_attended = grad_attended.reshape(image_count, length, head_count, HD)
    queries = projected[:, :, 0]
    key_rows = projected[:, :, 1]
    value_rows = projected[:, :, 2]
    scores = (
        jnp.einsum("bqhe,bkhe->bhqk", queries, key_rows, preferred_element_type=jnp.float32)
        * score_scale
    )
    probs = jnp.exp(scores - log_total[..., None])
    grad_values = jnp.einsum(
        "bhqk,bqhe->bkhe", probs.astype(jnp.bfloat16), grad_attended,
        preferred_element_type=jnp.float32,
    )
    grad_probs = jnp.einsum(
        "bqhe,bkhe->bhqk", grad_attended, value_rows, preferred_element_type=jnp.float32
    )
    grad_scores = (
        probs * (grad_probs - jnp.sum(probs * grad_probs, axis=-1, keepdims=True))
    ).astype(jnp.bfloat16)
    grad_queries = (
        jnp.einsum("bhqk,bkhe->bqhe", grad_scores, key_rows, preferred_element_type=jnp.float32)
        * score_scale
    )
    grad_keys = (
        jnp.einsum("bhqk,bqhe->bkhe", grad_scores, queries, preferred_element_type=jnp.float32)
        * score_scale
    )
    grad_projected = jnp.stack([grad_queries, grad_keys, grad_values], axis=2).astype(jnp.bfloat16)
    grad_projected = grad_projected.reshape(row_count, 3, head_count * HD)
    grad_w_qkv = jnp.einsum(
        "rd,rcf->dcf", first, grad_projected, preferred_element_type=jnp.float32
    )
    partial_first = jnp.einsum(
        "rcf,dcf->rd", grad_projected, w_qkv, preferred_element_type=jnp.float32
    )
    (grad_first,) = pair_sum((partial_first.astype(jnp.bfloat16),), 3)
    grad_first = grad_first.astype(jnp.bfloat16).astype(jnp.float32)
    grad_input_norm, grad_gain_one, grad_shift_one = norm_backward(
        grad_first, normed_one, inverse_one, gain_rows[0]
    )
    grad_input = grad_hidden + grad_input_norm
    grads = (
        grad_w_qkv,
        grad_w_proj,
        grad_w_in,
        grad_w_out,
        grad_w_router,
        jnp.stack([grad_gain_one, grad_gain_two]),
        jnp.stack([grad_shift_one, grad_shift_two]),
    )
    return (grad_input.reshape(image_count, length, model_width), grads)


def make_local(n):
    def local(images, routes, w_qkv, w_proj, w_in, w_out, w_router, ln_gain, ln_bias, cotangent):
        shapes = [a.shape for a in (w_qkv, w_proj, w_in, w_out, w_router, ln_gain, ln_bias)]
        weights = gather_weights(w_qkv, w_proj, w_in, w_out, w_router, ln_gain, ln_bias, n)
        field = images.astype(jnp.float32)
        output, record = layer_forward(field, routes[0], weights)
        grad_input, grads = layer_backward(cotangent.astype(jnp.float32), record, weights)
        shards = scatter_grads(grads, n, [(1,) + tuple(s[1:]) for s in shapes])
        return (output, grad_input, *shards)

    return local


def solution(mesh):
    n = mesh.shape["dp"]
    in_specs = (
        P("dp", None, None),
        P(None, "dp", None, None),
        P(None, "dp", None, "mp"),
        P(None, "mp", "dp"),
        P(None, None, "dp", "mp"),
        P(None, None, "mp", "dp"),
        P(None, "dp", None),
        P(None, None, "dp"),
        P(None, None, "dp"),
        P("dp", None, None),
    )
    out_specs = (
        P("dp", None, None),
        P("dp", None, None),
        P(None, "dp", None, "mp"),
        P(None, "mp", "dp"),
        P(None, None, "dp", "mp"),
        P(None, None, "mp", "dp"),
        P(None, "dp", None),
        P(None, None, "dp"),
        P(None, None, "dp"),
    )
    return jax.shard_map(make_local(n), mesh=mesh, in_specs=in_specs, out_specs=out_specs, check_vma=False)
```

```python
import functools

import jax
import jax.numpy as jnp
from jax import lax
from jax.sharding import PartitionSpec as P
from jax.experimental import pallas as pl
from jax.experimental.pallas import tpu as pltpu

MESH = pl.DeviceIdType.MESH
LANES = 128

HD = 64
EXPERTS = 4
TOPK = 2
CAP = 104
EPSILON = 1e-06


def norm_forward(field, gain_row, shift_row):
    mean_value = jnp.mean(field, axis=-1, keepdims=True)
    centered = field - mean_value
    inverse = lax.rsqrt(jnp.mean(centered * centered, axis=-1, keepdims=True) + EPSILON)
    normed = centered * inverse
    return (normed * gain_row + shift_row, normed, inverse)


def norm_backward(grad_out, normed, inverse, gain_row):
    grad_gain = jnp.sum(grad_out * normed, axis=0)
    grad_shift = jnp.sum(grad_out, axis=0)
    scaled = grad_out * gain_row
    grad_in = inverse * (
        scaled
        - jnp.mean(scaled, axis=-1, keepdims=True)
        - normed * jnp.mean(scaled * normed, axis=-1, keepdims=True)
    )
    return (grad_in, grad_gain, grad_shift)


def slot_positions(chosen_ids):
    labels = jnp.arange(EXPERTS, dtype=jnp.int32)
    hit_counts = jnp.sum((chosen_ids[..., None] == labels).astype(jnp.int32), axis=-2)
    before = jnp.cumsum(hit_counts, axis=1) - hit_counts
    return jnp.take_along_axis(before, chosen_ids, axis=-1)


def gelu_slope(inner_pre):
    cumulative = 0.5 * (1.0 + jax.scipy.special.erf(inner_pre * 0.7071067811865476))
    density = jnp.exp(-0.5 * inner_pre * inner_pre) * 0.3989422804014327
    return cumulative + inner_pre * density


def group_of(kind):
    def chips():
        dp, mp = lax.axis_index("dp"), lax.axis_index("mp")
        return dp // 2, lambda i: (2 * i + dp % 2, mp)

    def cores():
        dp, mp = lax.axis_index("dp"), lax.axis_index("mp")
        return dp % 2, lambda i: (2 * (dp // 2) + i, mp)

    def whole():
        dp, mp = lax.axis_index("dp"), lax.axis_index("mp")
        return dp, lambda i: (i, mp)

    def pair():
        dp, mp = lax.axis_index("dp"), lax.axis_index("mp")
        return mp, lambda i: (dp, i)

    return {"chips": chips, "cores": cores, "pair": pair, "all": whole}[kind]


def exchange_kernel(m, pieces, gather, kind, x_ref, out_ref, send_sem, recv_sem, local_sem):
    me, device_of = group_of(kind)()
    step = out_ref.shape[1] // pieces
    barrier = pltpu.get_barrier_semaphore()

    def greet(k, carry):
        pl.semaphore_signal(
            barrier, inc=1, device_id=device_of(lax.rem(me + k, m)), device_id_type=MESH
        )
        return carry

    lax.fori_loop(1, m, greet, 0)
    pl.semaphore_wait(barrier, m - 1)
    own = pltpu.make_async_copy(x_ref if gather else x_ref.at[me], out_ref.at[me], local_sem)
    own.start()

    def describe(t):
        k = 1 + t // pieces
        part = pl.ds(pl.multiple_of((t % pieces) * step, step), step)
        peer = lax.rem(me + k, m)
        return pltpu.make_async_remote_copy(
            src_ref=x_ref.at[part] if gather else x_ref.at[peer, part],
            dst_ref=out_ref.at[me, part],
            send_sem=send_sem.at[t],
            recv_sem=recv_sem.at[t],
            device_id=device_of(peer),
            device_id_type=MESH,
        )

    def start(t, carry):
        describe(t).start()
        return carry

    def finish(t, carry):
        describe(t).wait()
        return carry

    count = (m - 1) * pieces
    lax.fori_loop(0, count, start, 0)
    lax.fori_loop(0, count, finish, 0)
    own.wait()


def exchange(x, m, gather, kind, collective_id, pieces=1):
    block = x.shape if gather else x.shape[1:]
    block_bytes = x.dtype.itemsize
    for d in block:
        block_bytes *= d
    count = (m - 1) * pieces
    return pl.pallas_call(
        functools.partial(exchange_kernel, m, pieces, gather, kind),
        out_shape=jax.ShapeDtypeStruct((m,) + tuple(block), x.dtype),
        in_specs=[pl.BlockSpec(memory_space=pl.ANY)],
        out_specs=pl.BlockSpec(memory_space=pl.ANY),
        scratch_shapes=[
            pltpu.SemaphoreType.DMA((count,)),
            pltpu.SemaphoreType.DMA((count,)),
            pltpu.SemaphoreType.DMA(()),
        ],
        compiler_params=pltpu.CompilerParams(collective_id=collective_id, has_side_effects=True),
        cost_estimate=pl.CostEstimate(flops=0, bytes_accessed=2 * m * block_bytes, transcendentals=0),
    )(x)


def relay_gather_kernel(chips, direct, x_ref, out_ref, sa, ra, sb, rb, sf, rf, sp, rp, sl):
    dp, mp = lax.axis_index("dp"), lax.axis_index("mp")
    n = 2 * chips
    core = dp % 2
    other = 1 - core
    chip = dp // 2
    barrier = pltpu.get_barrier_semaphore()

    def greet(k, carry):
        pl.semaphore_signal(
            barrier, inc=1, device_id=(lax.rem(dp + k, n), mp), device_id_type=MESH
        )
        return carry

    lax.fori_loop(1, n, greet, 0)
    pl.semaphore_wait(barrier, n - 1)
    own = pltpu.make_async_copy(x_ref, out_ref.at[dp], sl)
    own.start()

    def remote(src, dst, send, recv, target):
        return pltpu.make_async_remote_copy(
            src_ref=src, dst_ref=dst, send_sem=send, recv_sem=recv,
            device_id=(target, mp), device_id_type=MESH,
        )

    def same(j):
        return remote(x_ref, out_ref.at[dp], sa.at[j], ra.at[j], 2 * lax.rem(chip + j, chips) + core)

    def cross(j):
        return remote(x_ref, out_ref.at[dp], sb.at[j], rb.at[j], 2 * lax.rem(chip + j, chips) + other)

    def relay(j):
        slot = 2 * lax.rem(chip + chips - j, chips) + core
        return remote(out_ref.at[slot], out_ref.at[slot], sf.at[j], rf.at[j], 2 * chip + other)

    mate = remote(x_ref, out_ref.at[dp], sp, rp, 2 * chip + other)
    forwarded = [j for j in range(1, chips) if j not in direct]
    mate.start()
    for j in forwarded:
        same(j).start()
    for j in direct:
        cross(j).start()
    for j in direct:
        same(j).start()
    for j in forwarded:
        same(j).wait_recv()
        relay(j).start()
    for j in direct:
        same(j).wait_recv()
    for j in range(1, chips):
        same(j).wait_send()
    for j in direct:
        cross(j).wait()
    mate.wait()
    for j in forwarded:
        relay(j).wait()
    own.wait()


def relay_gather(x, n, collective_id):
    chips = n // 2
    direct = tuple(j for j in range(1, chips) if j % 4 == 0)
    block_bytes = x.dtype.itemsize
    for d in x.shape:
        block_bytes *= d
    return pl.pallas_call(
        functools.partial(relay_gather_kernel, chips, direct),
        out_shape=jax.ShapeDtypeStruct((n,) + tuple(x.shape), x.dtype),
        in_specs=[pl.BlockSpec(memory_space=pl.ANY)],
        out_specs=pl.BlockSpec(memory_space=pl.ANY),
        scratch_shapes=[pltpu.SemaphoreType.DMA((chips,))] * 6
        + [pltpu.SemaphoreType.DMA(())] * 3,
        compiler_params=pltpu.CompilerParams(collective_id=collective_id, has_side_effects=True),
        cost_estimate=pl.CostEstimate(flops=0, bytes_accessed=2 * n * block_bytes, transcendentals=0),
    )(x)


def relay_reduce_kernel(chips, direct, y_ref, out_same, out_cross, pin, sbuf, ss, rs, sc, rc, sr, rr, sl):
    dp, mp = lax.axis_index("dp"), lax.axis_index("mp")
    n = 2 * chips
    core = dp % 2
    other = 1 - core
    chip = dp // 2
    mate_id = 2 * chip + other
    barrier = pltpu.get_barrier_semaphore()

    def greet(k, carry):
        pl.semaphore_signal(
            barrier, inc=1, device_id=(lax.rem(dp + k, n), mp), device_id_type=MESH
        )
        return carry

    lax.fori_loop(1, n, greet, 0)
    pl.semaphore_wait(barrier, n - 1)
    own = pltpu.make_async_copy(y_ref.at[dp], out_same.at[0], sl)
    own.start()

    def remote(src, dst, send, recv, target):
        return pltpu.make_async_remote_copy(
            src_ref=src, dst_ref=dst, send_sem=send, recv_sem=recv,
            device_id=(target, mp), device_id_type=MESH,
        )

    def target(j, c):
        return 2 * lax.rem(chip + j, chips) + c

    slot_of = {j: i + 1 for i, j in enumerate(direct)}
    forwarded = [j for j in range(1, chips) if j not in direct]

    def same(j):
        src = y_ref.at[target(j, core)] if j in direct else sbuf.at[j]
        return remote(src, out_same.at[j], ss.at[j], rs.at[j], target(j, core))

    def cross(j):
        i = slot_of[j]
        return remote(y_ref.at[target(j, other)], out_cross.at[i], sc.at[i], rc.at[i], target(j, other))

    def relay(j):
        return remote(y_ref.at[target(j, other)], pin.at[j], sr.at[j], rr.at[j], mate_id)

    mate = remote(y_ref.at[mate_id], out_cross.at[0], sc.at[0], rc.at[0], mate_id)
    for j in forwarded:
        relay(j).start()
    mate.start()
    for j in direct:
        cross(j).start()
        same(j).start()
    for j in forwarded:
        relay(j).wait_recv()
        total = y_ref[target(j, core)].astype(jnp.float32) + pin[j].astype(jnp.float32)
        sbuf[j] = total.astype(sbuf.dtype)
        same(j).start()
    for j in forwarded:
        relay(j).wait_send()
    for j in range(1, chips):
        same(j).wait()
    for j in direct:
        cross(j).wait()
    mate.wait()
    own.wait()


def relay_reduce(y, n, collective_id):
    chips = n // 2
    direct = tuple(j for j in range(1, chips) if j % 4 == 0)
    block = tuple(y.shape[1:])
    block_bytes = y.dtype.itemsize
    for d in block:
        block_bytes *= d
    same, cross = pl.pallas_call(
        functools.partial(relay_reduce_kernel, chips, direct),
        out_shape=(
            jax.ShapeDtypeStruct((chips,) + block, y.dtype),
            jax.ShapeDtypeStruct((len(direct) + 1,) + block, y.dtype),
        ),
        in_specs=[pl.BlockSpec(memory_space=pltpu.VMEM)],
        out_specs=(pl.BlockSpec(memory_space=pl.ANY), pl.BlockSpec(memory_space=pl.ANY)),
        scratch_shapes=[pltpu.VMEM((chips,) + block, y.dtype)] * 2
        + [pltpu.SemaphoreType.DMA((chips,))] * 6
        + [pltpu.SemaphoreType.DMA(())],
        compiler_params=pltpu.CompilerParams(collective_id=collective_id, has_side_effects=True),
        cost_estimate=pl.CostEstimate(flops=0, bytes_accessed=3 * n * block_bytes, transcendentals=0),
    )(y)
    return jnp.sum(same.astype(jnp.float32), axis=0) + jnp.sum(cross.astype(jnp.float32), axis=0)


def padded_rows(size, dtype_rows=16):
    rows = -(-size // LANES)
    return -(-rows // dtype_rows) * dtype_rows


def shard_sizes(w_qkv, w_proj, w_in, w_out, w_router, ln_gain, ln_bias):
    return [a.size for a in (w_qkv, w_proj, w_in, w_out, w_router, ln_gain, ln_bias)]


def gather_weights(w_qkv, w_proj, w_in, w_out, w_router, ln_gain, ln_bias, n):
    parts = (w_qkv, w_proj, w_in, w_out, w_router, ln_gain, ln_bias)
    flat = jnp.concatenate([a.reshape(-1) for a in parts])
    total = flat.shape[0]
    rows = padded_rows(total)
    flat = jnp.pad(flat, (0, rows * LANES - total)).reshape(rows, LANES)
    full = relay_gather(flat, n, 0).reshape(n, rows * LANES)
    pieces = []
    start = 0
    for a in parts:
        pieces.append(full[:, start:start + a.size].reshape((n,) + a.shape[1:]))
        start += a.size
    q, p, i, o, r, g, b = pieces
    gq = q.reshape((-1,) + w_qkv.shape[2:])
    gr = r.reshape((-1,) + w_router.shape[2:])
    gg = g.transpose(1, 0, 2).reshape(ln_gain.shape[1], -1)
    gb = b.transpose(1, 0, 2).reshape(ln_bias.shape[1], -1)
    return (gq, p, i, o, gr, gg, gb)


def scatter_grads(grads, n, shapes):
    gq, gp, gi, go, gr, gg, gb = grads
    rows = [
        gq.reshape(n, -1),
        gp.reshape(n, -1),
        gi.reshape(n, -1),
        go.reshape(n, -1),
        gr.reshape(n, -1),
        gg.reshape(gg.shape[0], n, -1).transpose(1, 0, 2).reshape(n, -1),
        gb.reshape(gb.shape[0], n, -1).transpose(1, 0, 2).reshape(n, -1),
    ]
    packed = jnp.concatenate(rows, axis=1)
    total = packed.shape[1]
    count = padded_rows(total)
    packed = jnp.pad(packed, ((0, 0), (0, count * LANES - total))).reshape(n, count, LANES)
    mine = relay_reduce(packed.astype(jnp.bfloat16), n, 1).reshape(-1)
    outs = []
    start = 0
    for shape in shapes:
        size = 1
        for d in shape:
            size *= d
        outs.append(mine[start:start + size].reshape(shape))
        start += size
    return outs


def layer_forward(field, chosen_ids, weights):
    w_qkv, w_proj, w_in, w_out, w_router, ln_gain, ln_bias = weights
    image_count, length, model_width = field.shape
    row_count = image_count * length
    head_count = w_qkv.shape[2] // HD
    score_scale = HD ** (-0.5)
    gain_rows = ln_gain.astype(jnp.float32)
    shift_rows = ln_bias.astype(jnp.float32)
    flat = field.reshape(row_count, model_width)
    first, normed_one, inverse_one = norm_forward(flat, gain_rows[0], shift_rows[0])
    first = first.astype(jnp.bfloat16)
    projected = jnp.einsum("rd,dcf->rcf", first, w_qkv, preferred_element_type=jnp.float32).astype(
        jnp.bfloat16
    )
    projected = projected.reshape(image_count, length, 3, head_count, HD)
    queries = projected[:, :, 0]
    key_rows = projected[:, :, 1]
    value_rows = projected[:, :, 2]
    scores = (
        jnp.einsum("bqhe,bkhe->bhqk", queries, key_rows, preferred_element_type=jnp.float32)
        * score_scale
    )
    log_total = jax.nn.logsumexp(scores, axis=-1)
    attn_weights = jnp.exp(scores - log_total[..., None]).astype(jnp.bfloat16)
    attended = jnp.einsum(
        "bhqk,bkhe->bqhe", attn_weights, value_rows, preferred_element_type=jnp.float32
    )
    attended = attended.astype(jnp.bfloat16).reshape(row_count, head_count * HD)
    partial_attn = jnp.einsum(
        "rf,jfk->rjk", attended, w_proj, preferred_element_type=jnp.float32
    ).reshape(row_count, model_width)
    hidden = flat + lax.psum(partial_attn, "mp")
    second, normed_two, inverse_two = norm_forward(hidden, gain_rows[1], shift_rows[1])
    second = second.astype(jnp.bfloat16)
    logits = jnp.dot(second, w_router, preferred_element_type=jnp.float32)
    router = jax.nn.softmax(logits, axis=-1)
    labels = jnp.arange(EXPERTS, dtype=jnp.int32)
    ids_flat = chosen_ids.reshape(row_count, TOPK)
    chosen = (ids_flat[:, :, None] == labels).astype(jnp.float32)
    gate_values = jnp.sum(router[:, None, :] * chosen, axis=-1)
    per_image = EXPERTS * CAP
    image_base = (jnp.arange(image_count, dtype=jnp.int32) * per_image)[:, None, None]
    slot_index = (chosen_ids * CAP + slot_positions(chosen_ids) + image_base).reshape(-1)
    owners = (
        jnp.full((image_count * per_image,), row_count, jnp.int32)
        .at[slot_index]
        .set(jnp.repeat(jnp.arange(row_count, dtype=jnp.int32), TOPK))
    )
    slot_gate = (
        jnp.zeros((image_count * per_image,), jnp.float32).at[slot_index].set(gate_values.reshape(-1))
    )
    padded = jnp.concatenate([second, jnp.zeros((1, model_width), jnp.bfloat16)], axis=0)
    slot_rows = jnp.take(padded, owners, axis=0).reshape(image_count, EXPERTS, CAP, model_width)
    slot_split = slot_rows.reshape(slot_rows.shape[:3] + w_in.shape[:1] + w_in.shape[2:3])
    inner_pre = jnp.einsum("becjk,jekf->becf", slot_split, w_in, preferred_element_type=jnp.float32)
    activated = jax.nn.gelu(inner_pre, approximate=False).astype(jnp.bfloat16)
    produced = jnp.einsum("becf,jefk->becjk", activated, w_out, preferred_element_type=jnp.float32)
    produced = produced.reshape(image_count * per_image, model_width)
    picked = jnp.take(produced, slot_index, axis=0).reshape(row_count, TOPK, model_width)
    partial_moe = jnp.sum(gate_values[:, :, None] * picked, axis=1)
    output = hidden + lax.psum(partial_moe.astype(jnp.bfloat16), "mp").astype(jnp.float32)
    record = (
        normed_one, inverse_one, first, projected, log_total, attended, normed_two, inverse_two,
        second, router, chosen, slot_index, owners, slot_gate, slot_rows, inner_pre, activated, picked,
    )
    return (output.reshape(image_count, length, model_width), record)


def layer_backward(grad_field, record, weights):
    w_qkv, w_proj, w_in, w_out, w_router, ln_gain, ln_bias = weights
    (
        normed_one, inverse_one, first, projected, log_total, attended, normed_two, inverse_two,
        second, router, chosen, slot_index, owners, slot_gate, slot_rows, inner_pre, activated, picked,
    ) = record
    image_count, length, model_width = grad_field.shape
    row_count = image_count * length
    head_count = projected.shape[3]
    score_scale = HD ** (-0.5)
    gain_rows = ln_gain.astype(jnp.float32)
    grad_flat = grad_field.reshape(row_count, model_width)
    padded_grad = jnp.concatenate([grad_flat, jnp.zeros((1, model_width), jnp.float32)], axis=0)
    grad_slots = (jnp.take(padded_grad, owners, axis=0) * slot_gate[:, None]).astype(jnp.bfloat16)
    split = (w_out.shape[0], w_out.shape[3])
    grad_slots = grad_slots.reshape((image_count, EXPERTS, CAP) + split)
    slot_split = slot_rows.reshape((image_count, EXPERTS, CAP) + split)
    grad_w_out = jnp.einsum(
        "becf,becjk->jefk", activated, grad_slots, preferred_element_type=jnp.float32
    )
    grad_act = jnp.einsum("becjk,jefk->becf", grad_slots, w_out, preferred_element_type=jnp.float32)
    grad_inner = (grad_act * gelu_slope(inner_pre)).astype(jnp.bfloat16)
    grad_w_in = jnp.einsum(
        "becjk,becf->jekf", slot_split, grad_inner, preferred_element_type=jnp.float32
    )
    grad_slot_rows = jnp.einsum(
        "becf,jekf->becjk", grad_inner, w_in, preferred_element_type=jnp.float32
    )
    grad_slot_rows = grad_slot_rows.reshape(image_count * EXPERTS * CAP, model_width)
    partial_second = jnp.sum(
        jnp.take(grad_slot_rows, slot_index, axis=0).reshape(row_count, TOPK, model_width), axis=1
    )
    partial_gate = jnp.sum(picked * grad_flat[:, None, :], axis=-1)
    grad_second, grad_gate = lax.psum((partial_second, partial_gate), "mp")
    grad_router = jnp.sum(grad_gate[:, :, None] * chosen, axis=1)
    grad_logits = router * (grad_router - jnp.sum(router * grad_router, axis=-1, keepdims=True))
    grad_logits = grad_logits.astype(jnp.bfloat16)
    grad_w_router = jnp.dot(second.T, grad_logits, preferred_element_type=jnp.float32)
    grad_second = grad_second + jnp.dot(grad_logits, w_router.T, preferred_element_type=jnp.float32)
    grad_from_norm, grad_gain_two, grad_shift_two = norm_backward(
        grad_second, normed_two, inverse_two, gain_rows[1]
    )
    grad_hidden = grad_flat + grad_from_norm
    grad_hidden_low = grad_hidden.astype(jnp.bfloat16)
    grad_hidden_split = grad_hidden_low.reshape((row_count,) + split)
    grad_w_proj = jnp.einsum(
        "rf,rjk->jfk", attended, grad_hidden_split, preferred_element_type=jnp.float32
    )
    grad_attended = jnp.einsum(
        "rjk,jfk->rf", grad_hidden_split, w_proj, preferred_element_type=jnp.float32
    ).astype(jnp.bfloat16)
    grad_attended = grad_attended.reshape(image_count, length, head_count, HD)
    queries = projected[:, :, 0]
    key_rows = projected[:, :, 1]
    value_rows = projected[:, :, 2]
    scores = (
        jnp.einsum("bqhe,bkhe->bhqk", queries, key_rows, preferred_element_type=jnp.float32)
        * score_scale
    )
    probs = jnp.exp(scores - log_total[..., None])
    grad_values = jnp.einsum(
        "bhqk,bqhe->bkhe", probs.astype(jnp.bfloat16), grad_attended,
        preferred_element_type=jnp.float32,
    )
    grad_probs = jnp.einsum(
        "bqhe,bkhe->bhqk", grad_attended, value_rows, preferred_element_type=jnp.float32
    )
    grad_scores = (
        probs * (grad_probs - jnp.sum(probs * grad_probs, axis=-1, keepdims=True))
    ).astype(jnp.bfloat16)
    grad_queries = (
        jnp.einsum("bhqk,bkhe->bqhe", grad_scores, key_rows, preferred_element_type=jnp.float32)
        * score_scale
    )
    grad_keys = (
        jnp.einsum("bhqk,bqhe->bkhe", grad_scores, queries, preferred_element_type=jnp.float32)
        * score_scale
    )
    grad_projected = jnp.stack([grad_queries, grad_keys, grad_values], axis=2).astype(jnp.bfloat16)
    grad_projected = grad_projected.reshape(row_count, 3, head_count * HD)
    grad_w_qkv = jnp.einsum(
        "rd,rcf->dcf", first, grad_projected, preferred_element_type=jnp.float32
    )
    partial_first = jnp.einsum(
        "rcf,dcf->rd", grad_projected, w_qkv, preferred_element_type=jnp.float32
    )
    both = exchange(partial_first.astype(jnp.bfloat16), 2, True, "pair", 2).astype(jnp.float32)
    grad_first = (both[0] + both[1]).astype(jnp.bfloat16).astype(jnp.float32)
    grad_input_norm, grad_gain_one, grad_shift_one = norm_backward(
        grad_first, normed_one, inverse_one, gain_rows[0]
    )
    grad_input = grad_hidden + grad_input_norm
    grads = (
        grad_w_qkv,
        grad_w_proj,
        grad_w_in,
        grad_w_out,
        grad_w_router,
        jnp.stack([grad_gain_one, grad_gain_two]),
        jnp.stack([grad_shift_one, grad_shift_two]),
    )
    return (grad_input.reshape(image_count, length, model_width), grads)


def make_local(n):
    def local(images, routes, w_qkv, w_proj, w_in, w_out, w_router, ln_gain, ln_bias, cotangent):
        shapes = [a.shape for a in (w_qkv, w_proj, w_in, w_out, w_router, ln_gain, ln_bias)]
        weights = gather_weights(w_qkv, w_proj, w_in, w_out, w_router, ln_gain, ln_bias, n)
        field = images.astype(jnp.float32)
        output, record = layer_forward(field, routes[0], weights)
        grad_input, grads = layer_backward(cotangent.astype(jnp.float32), record, weights)
        shards = scatter_grads(grads, n, [(1,) + tuple(s[1:]) for s in shapes])
        return (output, grad_input, *shards)

    return local


def solution(mesh):
    n = mesh.shape["dp"]
    in_specs = (
        P("dp", None, None),
        P(None, "dp", None, None),
        P(None, "dp", None, "mp"),
        P(None, "mp", "dp"),
        P(None, None, "dp", "mp"),
        P(None, None, "mp", "dp"),
        P(None, "dp", None),
        P(None, None, "dp"),
        P(None, None, "dp"),
        P("dp", None, None),
    )
    out_specs = (
        P("dp", None, None),
        P("dp", None, None),
        P(None, "dp", None, "mp"),
        P(None, "mp", "dp"),
        P(None, None, "dp", "mp"),
        P(None, None, "mp", "dp"),
        P(None, "dp", None),
        P(None, None, "dp"),
        P(None, None, "dp"),
    )
    return jax.shard_map(make_local(n), mesh=mesh, in_specs=in_specs, out_specs=out_specs, check_vma=False)
```

```python
import functools

import jax
import jax.numpy as jnp
from jax import lax
from jax.sharding import PartitionSpec as P
from jax.experimental import pallas as pl
from jax.experimental.pallas import tpu as pltpu

MESH = pl.DeviceIdType.MESH
LANES = 128

HD = 64
EXPERTS = 4
TOPK = 2
CAP = 104
EPSILON = 1e-06


def norm_forward(field, gain_row, shift_row):
    mean_value = jnp.mean(field, axis=-1, keepdims=True)
    centered = field - mean_value
    inverse = lax.rsqrt(jnp.mean(centered * centered, axis=-1, keepdims=True) + EPSILON)
    normed = centered * inverse
    return (normed * gain_row + shift_row, normed, inverse)


def norm_backward(grad_out, normed, inverse, gain_row):
    grad_gain = jnp.sum(grad_out * normed, axis=0)
    grad_shift = jnp.sum(grad_out, axis=0)
    scaled = grad_out * gain_row
    grad_in = inverse * (
        scaled
        - jnp.mean(scaled, axis=-1, keepdims=True)
        - normed * jnp.mean(scaled * normed, axis=-1, keepdims=True)
    )
    return (grad_in, grad_gain, grad_shift)


def slot_positions(chosen_ids):
    labels = jnp.arange(EXPERTS, dtype=jnp.int32)
    hit_counts = jnp.sum((chosen_ids[..., None] == labels).astype(jnp.int32), axis=-2)
    before = jnp.cumsum(hit_counts, axis=1) - hit_counts
    return jnp.take_along_axis(before, chosen_ids, axis=-1)


def gelu_slope(inner_pre):
    cumulative = 0.5 * (1.0 + jax.scipy.special.erf(inner_pre * 0.7071067811865476))
    density = jnp.exp(-0.5 * inner_pre * inner_pre) * 0.3989422804014327
    return cumulative + inner_pre * density


def group_of(kind):
    def chips():
        dp, mp = lax.axis_index("dp"), lax.axis_index("mp")
        return dp // 2, lambda i: (2 * i + dp % 2, mp)

    def cores():
        dp, mp = lax.axis_index("dp"), lax.axis_index("mp")
        return dp % 2, lambda i: (2 * (dp // 2) + i, mp)

    def whole():
        dp, mp = lax.axis_index("dp"), lax.axis_index("mp")
        return dp, lambda i: (i, mp)

    def pair():
        dp, mp = lax.axis_index("dp"), lax.axis_index("mp")
        return mp, lambda i: (dp, i)

    return {"chips": chips, "cores": cores, "pair": pair, "all": whole}[kind]


def exchange_kernel(m, pieces, gather, kind, x_ref, out_ref, send_sem, recv_sem, local_sem):
    me, device_of = group_of(kind)()
    step = out_ref.shape[1] // pieces
    barrier = pltpu.get_barrier_semaphore()

    def greet(k, carry):
        pl.semaphore_signal(
            barrier, inc=1, device_id=device_of(lax.rem(me + k, m)), device_id_type=MESH
        )
        return carry

    lax.fori_loop(1, m, greet, 0)
    pl.semaphore_wait(barrier, m - 1)
    own = pltpu.make_async_copy(x_ref if gather else x_ref.at[me], out_ref.at[me], local_sem)
    own.start()

    def describe(t):
        k = 1 + t // pieces
        part = pl.ds(pl.multiple_of((t % pieces) * step, step), step)
        peer = lax.rem(me + k, m)
        return pltpu.make_async_remote_copy(
            src_ref=x_ref.at[part] if gather else x_ref.at[peer, part],
            dst_ref=out_ref.at[me, part],
            send_sem=send_sem.at[t],
            recv_sem=recv_sem.at[t],
            device_id=device_of(peer),
            device_id_type=MESH,
        )

    def start(t, carry):
        describe(t).start()
        return carry

    def finish(t, carry):
        describe(t).wait()
        return carry

    count = (m - 1) * pieces
    lax.fori_loop(0, count, start, 0)
    lax.fori_loop(0, count, finish, 0)
    own.wait()


def exchange(x, m, gather, kind, collective_id, pieces=1):
    block = x.shape if gather else x.shape[1:]
    block_bytes = x.dtype.itemsize
    for d in block:
        block_bytes *= d
    count = (m - 1) * pieces
    return pl.pallas_call(
        functools.partial(exchange_kernel, m, pieces, gather, kind),
        out_shape=jax.ShapeDtypeStruct((m,) + tuple(block), x.dtype),
        in_specs=[pl.BlockSpec(memory_space=pl.ANY)],
        out_specs=pl.BlockSpec(memory_space=pl.ANY),
        scratch_shapes=[
            pltpu.SemaphoreType.DMA((count,)),
            pltpu.SemaphoreType.DMA((count,)),
            pltpu.SemaphoreType.DMA(()),
        ],
        compiler_params=pltpu.CompilerParams(collective_id=collective_id, has_side_effects=True),
        cost_estimate=pl.CostEstimate(flops=0, bytes_accessed=2 * m * block_bytes, transcendentals=0),
    )(x)


def relay_gather_kernel(chips, direct, x_ref, out_ref, sa, ra, sb, rb, sf, rf, sp, rp, sl):
    dp, mp = lax.axis_index("dp"), lax.axis_index("mp")
    n = 2 * chips
    core = dp % 2
    other = 1 - core
    chip = dp // 2
    barrier = pltpu.get_barrier_semaphore()

    def greet(k, carry):
        pl.semaphore_signal(
            barrier, inc=1, device_id=(lax.rem(dp + k, n), mp), device_id_type=MESH
        )
        return carry

    lax.fori_loop(1, n, greet, 0)
    pl.semaphore_wait(barrier, n - 1)
    own = pltpu.make_async_copy(x_ref, out_ref.at[dp], sl)
    own.start()

    def remote(src, dst, send, recv, target):
        return pltpu.make_async_remote_copy(
            src_ref=src, dst_ref=dst, send_sem=send, recv_sem=recv,
            device_id=(target, mp), device_id_type=MESH,
        )

    def same(j):
        return remote(x_ref, out_ref.at[dp], sa.at[j], ra.at[j], 2 * lax.rem(chip + j, chips) + core)

    def cross(j):
        return remote(x_ref, out_ref.at[dp], sb.at[j], rb.at[j], 2 * lax.rem(chip + j, chips) + other)

    def relay(j):
        slot = 2 * lax.rem(chip + chips - j, chips) + core
        return remote(out_ref.at[slot], out_ref.at[slot], sf.at[j], rf.at[j], 2 * chip + other)

    mate = remote(x_ref, out_ref.at[dp], sp, rp, 2 * chip + other)
    forwarded = [j for j in range(1, chips) if j not in direct]
    mate.start()
    for j in forwarded:
        same(j).start()
    for j in direct:
        cross(j).start()
    for j in direct:
        same(j).start()
    for j in forwarded:
        same(j).wait_recv()
        relay(j).start()
    for j in direct:
        same(j).wait_recv()
    for j in range(1, chips):
        same(j).wait_send()
    for j in direct:
        cross(j).wait()
    mate.wait()
    for j in forwarded:
        relay(j).wait()
    own.wait()


def relay_gather(x, n, collective_id):
    chips = n // 2
    direct = tuple(j for j in range(1, chips) if j % 4 == 0)
    block_bytes = x.dtype.itemsize
    for d in x.shape:
        block_bytes *= d
    return pl.pallas_call(
        functools.partial(relay_gather_kernel, chips, direct),
        out_shape=jax.ShapeDtypeStruct((n,) + tuple(x.shape), x.dtype),
        in_specs=[pl.BlockSpec(memory_space=pl.ANY)],
        out_specs=pl.BlockSpec(memory_space=pl.ANY),
        scratch_shapes=[pltpu.SemaphoreType.DMA((chips,))] * 6
        + [pltpu.SemaphoreType.DMA(())] * 3,
        compiler_params=pltpu.CompilerParams(collective_id=collective_id, has_side_effects=True),
        cost_estimate=pl.CostEstimate(flops=0, bytes_accessed=2 * n * block_bytes, transcendentals=0),
    )(x)


def relay_reduce_kernel(chips, direct, y_ref, out_same, out_cross, pin, sbuf, ss, rs, sc, rc, sr, rr, sl):
    dp, mp = lax.axis_index("dp"), lax.axis_index("mp")
    n = 2 * chips
    core = dp % 2
    other = 1 - core
    chip = dp // 2
    mate_id = 2 * chip + other
    barrier = pltpu.get_barrier_semaphore()

    def greet(k, carry):
        pl.semaphore_signal(
            barrier, inc=1, device_id=(lax.rem(dp + k, n), mp), device_id_type=MESH
        )
        return carry

    lax.fori_loop(1, n, greet, 0)
    pl.semaphore_wait(barrier, n - 1)
    own = pltpu.make_async_copy(y_ref.at[dp], out_same.at[0], sl)
    own.start()

    def remote(src, dst, send, recv, target):
        return pltpu.make_async_remote_copy(
            src_ref=src, dst_ref=dst, send_sem=send, recv_sem=recv,
            device_id=(target, mp), device_id_type=MESH,
        )

    def target(j, c):
        return 2 * lax.rem(chip + j, chips) + c

    slot_of = {j: i + 1 for i, j in enumerate(direct)}
    forwarded = [j for j in range(1, chips) if j not in direct]

    def same(j):
        src = y_ref.at[target(j, core)] if j in direct else sbuf.at[j]
        return remote(src, out_same.at[j], ss.at[j], rs.at[j], target(j, core))

    def cross(j):
        i = slot_of[j]
        return remote(y_ref.at[target(j, other)], out_cross.at[i], sc.at[i], rc.at[i], target(j, other))

    def relay(j):
        return remote(y_ref.at[target(j, other)], pin.at[j], sr.at[j], rr.at[j], mate_id)

    mate = remote(y_ref.at[mate_id], out_cross.at[0], sc.at[0], rc.at[0], mate_id)
    for j in forwarded:
        relay(j).start()
    mate.start()
    for j in direct:
        cross(j).start()
        same(j).start()
    for j in forwarded:
        relay(j).wait_recv()
        total = y_ref[target(j, core)].astype(jnp.float32) + pin[j].astype(jnp.float32)
        sbuf[j] = total.astype(sbuf.dtype)
        same(j).start()
    for j in forwarded:
        relay(j).wait_send()
    for j in range(1, chips):
        same(j).wait()
    for j in direct:
        cross(j).wait()
    mate.wait()
    own.wait()


def relay_reduce(y, n, collective_id):
    chips = n // 2
    direct = tuple(j for j in range(1, chips) if j % 4 == 0)
    block = tuple(y.shape[1:])
    block_bytes = y.dtype.itemsize
    for d in block:
        block_bytes *= d
    same, cross = pl.pallas_call(
        functools.partial(relay_reduce_kernel, chips, direct),
        out_shape=(
            jax.ShapeDtypeStruct((chips,) + block, y.dtype),
            jax.ShapeDtypeStruct((len(direct) + 1,) + block, y.dtype),
        ),
        in_specs=[pl.BlockSpec(memory_space=pltpu.VMEM)],
        out_specs=(pl.BlockSpec(memory_space=pl.ANY), pl.BlockSpec(memory_space=pl.ANY)),
        scratch_shapes=[pltpu.VMEM((chips,) + block, y.dtype)] * 2
        + [pltpu.SemaphoreType.DMA((chips,))] * 6
        + [pltpu.SemaphoreType.DMA(())],
        compiler_params=pltpu.CompilerParams(collective_id=collective_id, has_side_effects=True),
        cost_estimate=pl.CostEstimate(flops=0, bytes_accessed=3 * n * block_bytes, transcendentals=0),
    )(y)
    return jnp.sum(same.astype(jnp.float32), axis=0) + jnp.sum(cross.astype(jnp.float32), axis=0)


def padded_rows(size, dtype_rows=16):
    rows = -(-size // LANES)
    return -(-rows // dtype_rows) * dtype_rows


def shard_sizes(w_qkv, w_proj, w_in, w_out, w_router, ln_gain, ln_bias):
    return [a.size for a in (w_qkv, w_proj, w_in, w_out, w_router, ln_gain, ln_bias)]


def gather_weights(w_qkv, w_proj, w_in, w_out, w_router, ln_gain, ln_bias, n):
    parts = (w_qkv, w_proj, w_in, w_out, w_router, ln_gain, ln_bias)
    flat = jnp.concatenate([a.reshape(-1) for a in parts])
    total = flat.shape[0]
    rows = padded_rows(total)
    flat = jnp.pad(flat, (0, rows * LANES - total)).reshape(rows, LANES)
    full = relay_gather(flat, n, 0).reshape(n, rows * LANES)
    pieces = []
    start = 0
    for a in parts:
        pieces.append(full[:, start:start + a.size].reshape((n,) + a.shape[1:]))
        start += a.size
    q, p, i, o, r, g, b = pieces
    gq = q.reshape((-1,) + w_qkv.shape[2:])
    gr = r.reshape((-1,) + w_router.shape[2:])
    gg = g.transpose(1, 0, 2).reshape(ln_gain.shape[1], -1)
    gb = b.transpose(1, 0, 2).reshape(ln_bias.shape[1], -1)
    return (gq, p, i, o, gr, gg, gb)


def scatter_grads(grads, n, shapes):
    gq, gp, gi, go, gr, gg, gb = grads
    rows = [
        gq.reshape(n, -1),
        gp.reshape(n, -1),
        gi.reshape(n, -1),
        go.reshape(n, -1),
        gr.reshape(n, -1),
        gg.reshape(gg.shape[0], n, -1).transpose(1, 0, 2).reshape(n, -1),
        gb.reshape(gb.shape[0], n, -1).transpose(1, 0, 2).reshape(n, -1),
    ]
    packed = jnp.concatenate(rows, axis=1)
    total = packed.shape[1]
    count = padded_rows(total)
    packed = jnp.pad(packed, ((0, 0), (0, count * LANES - total))).reshape(n, count, LANES)
    mine = relay_reduce(packed.astype(jnp.bfloat16), n, 1).reshape(-1)
    outs = []
    start = 0
    for shape in shapes:
        size = 1
        for d in shape:
            size *= d
        outs.append(mine[start:start + size].reshape(shape))
        start += size
    return outs


def layer_forward(field, chosen_ids, weights):
    w_qkv, w_proj, w_in, w_out, w_router, ln_gain, ln_bias = weights
    image_count, length, model_width = field.shape
    row_count = image_count * length
    head_count = w_qkv.shape[2] // HD
    score_scale = HD ** (-0.5)
    gain_rows = ln_gain.astype(jnp.float32)
    shift_rows = ln_bias.astype(jnp.float32)
    flat = field.reshape(row_count, model_width)
    first, normed_one, inverse_one = norm_forward(flat, gain_rows[0], shift_rows[0])
    first = first.astype(jnp.bfloat16)
    projected = jnp.einsum("rd,dcf->rcf", first, w_qkv, preferred_element_type=jnp.float32).astype(
        jnp.bfloat16
    )
    projected = projected.reshape(image_count, length, 3, head_count, HD)
    queries = projected[:, :, 0]
    key_rows = projected[:, :, 1]
    value_rows = projected[:, :, 2]
    scores = (
        jnp.einsum("bqhe,bkhe->bhqk", queries, key_rows, preferred_element_type=jnp.float32)
        * score_scale
    )
    log_total = jax.nn.logsumexp(scores, axis=-1)
    attn_weights = jnp.exp(scores - log_total[..., None]).astype(jnp.bfloat16)
    attended = jnp.einsum(
        "bhqk,bkhe->bqhe", attn_weights, value_rows, preferred_element_type=jnp.float32
    )
    attended = attended.astype(jnp.bfloat16).reshape(row_count, head_count * HD)
    partial_attn = jnp.einsum(
        "rf,jfk->rjk", attended, w_proj, preferred_element_type=jnp.float32
    ).reshape(row_count, model_width)
    hidden = flat + lax.psum(partial_attn, "mp")
    second, normed_two, inverse_two = norm_forward(hidden, gain_rows[1], shift_rows[1])
    second = second.astype(jnp.bfloat16)
    logits = jnp.dot(second, w_router, preferred_element_type=jnp.float32)
    router = jax.nn.softmax(logits, axis=-1)
    labels = jnp.arange(EXPERTS, dtype=jnp.int32)
    ids_flat = chosen_ids.reshape(row_count, TOPK)
    chosen = (ids_flat[:, :, None] == labels).astype(jnp.float32)
    gate_values = jnp.sum(router[:, None, :] * chosen, axis=-1)
    per_image = EXPERTS * CAP
    image_base = (jnp.arange(image_count, dtype=jnp.int32) * per_image)[:, None, None]
    slot_index = (chosen_ids * CAP + slot_positions(chosen_ids) + image_base).reshape(-1)
    owners = (
        jnp.full((image_count * per_image,), row_count, jnp.int32)
        .at[slot_index]
        .set(jnp.repeat(jnp.arange(row_count, dtype=jnp.int32), TOPK))
    )
    slot_gate = (
        jnp.zeros((image_count * per_image,), jnp.float32).at[slot_index].set(gate_values.reshape(-1))
    )
    padded = jnp.concatenate([second, jnp.zeros((1, model_width), jnp.bfloat16)], axis=0)
    slot_rows = jnp.take(padded, owners, axis=0).reshape(image_count, EXPERTS, CAP, model_width)
    slot_split = slot_rows.reshape(slot_rows.shape[:3] + w_in.shape[:1] + w_in.shape[2:3])
    inner_pre = jnp.einsum("becjk,jekf->becf", slot_split, w_in, preferred_element_type=jnp.float32)
    activated = jax.nn.gelu(inner_pre, approximate=False).astype(jnp.bfloat16)
    produced = jnp.einsum("becf,jefk->becjk", activated, w_out, preferred_element_type=jnp.float32)
    produced = produced.reshape(image_count * per_image, model_width)
    picked = jnp.take(produced, slot_index, axis=0).reshape(row_count, TOPK, model_width)
    partial_moe = jnp.sum(gate_values[:, :, None] * picked, axis=1)
    both = exchange(partial_moe.astype(jnp.bfloat16), 2, True, "pair", 3).astype(jnp.float32)
    output = hidden + (both[0] + both[1]).astype(jnp.bfloat16).astype(jnp.float32)
    record = (
        normed_one, inverse_one, first, projected, log_total, attended, normed_two, inverse_two,
        second, router, chosen, slot_index, owners, slot_gate, slot_rows, inner_pre, activated, picked,
    )
    return (output.reshape(image_count, length, model_width), record)


def layer_backward(grad_field, record, weights):
    w_qkv, w_proj, w_in, w_out, w_router, ln_gain, ln_bias = weights
    (
        normed_one, inverse_one, first, projected, log_total, attended, normed_two, inverse_two,
        second, router, chosen, slot_index, owners, slot_gate, slot_rows, inner_pre, activated, picked,
    ) = record
    image_count, length, model_width = grad_field.shape
    row_count = image_count * length
    head_count = projected.shape[3]
    score_scale = HD ** (-0.5)
    gain_rows = ln_gain.astype(jnp.float32)
    grad_flat = grad_field.reshape(row_count, model_width)
    padded_grad = jnp.concatenate([grad_flat, jnp.zeros((1, model_width), jnp.float32)], axis=0)
    grad_slots = (jnp.take(padded_grad, owners, axis=0) * slot_gate[:, None]).astype(jnp.bfloat16)
    split = (w_out.shape[0], w_out.shape[3])
    grad_slots = grad_slots.reshape((image_count, EXPERTS, CAP) + split)
    slot_split = slot_rows.reshape((image_count, EXPERTS, CAP) + split)
    grad_w_out = jnp.einsum(
        "becf,becjk->jefk", activated, grad_slots, preferred_element_type=jnp.float32
    )
    grad_act = jnp.einsum("becjk,jefk->becf", grad_slots, w_out, preferred_element_type=jnp.float32)
    grad_inner = (grad_act * gelu_slope(inner_pre)).astype(jnp.bfloat16)
    grad_w_in = jnp.einsum(
        "becjk,becf->jekf", slot_split, grad_inner, preferred_element_type=jnp.float32
    )
    grad_slot_rows = jnp.einsum(
        "becf,jekf->becjk", grad_inner, w_in, preferred_element_type=jnp.float32
    )
    grad_slot_rows = grad_slot_rows.reshape(image_count * EXPERTS * CAP, model_width)
    partial_second = jnp.sum(
        jnp.take(grad_slot_rows, slot_index, axis=0).reshape(row_count, TOPK, model_width), axis=1
    )
    partial_gate = jnp.sum(picked * grad_flat[:, None, :], axis=-1)
    joined = lax.psum(jnp.concatenate([partial_second, partial_gate], axis=1), "mp")
    grad_second, grad_gate = joined[:, :model_width], joined[:, model_width:]
    grad_router = jnp.sum(grad_gate[:, :, None] * chosen, axis=1)
    grad_logits = router * (grad_router - jnp.sum(router * grad_router, axis=-1, keepdims=True))
    grad_logits = grad_logits.astype(jnp.bfloat16)
    grad_w_router = jnp.dot(second.T, grad_logits, preferred_element_type=jnp.float32)
    grad_second = grad_second + jnp.dot(grad_logits, w_router.T, preferred_element_type=jnp.float32)
    grad_from_norm, grad_gain_two, grad_shift_two = norm_backward(
        grad_second, normed_two, inverse_two, gain_rows[1]
    )
    grad_hidden = grad_flat + grad_from_norm
    grad_hidden_low = grad_hidden.astype(jnp.bfloat16)
    grad_hidden_split = grad_hidden_low.reshape((row_count,) + split)
    grad_w_proj = jnp.einsum(
        "rf,rjk->jfk", attended, grad_hidden_split, preferred_element_type=jnp.float32
    )
    grad_attended = jnp.einsum(
        "rjk,jfk->rf", grad_hidden_split, w_proj, preferred_element_type=jnp.float32
    ).astype(jnp.bfloat16)
    grad_attended = grad_attended.reshape(image_count, length, head_count, HD)
    queries = projected[:, :, 0]
    key_rows = projected[:, :, 1]
    value_rows = projected[:, :, 2]
    scores = (
        jnp.einsum("bqhe,bkhe->bhqk", queries, key_rows, preferred_element_type=jnp.float32)
        * score_scale
    )
    probs = jnp.exp(scores - log_total[..., None])
    grad_values = jnp.einsum(
        "bhqk,bqhe->bkhe", probs.astype(jnp.bfloat16), grad_attended,
        preferred_element_type=jnp.float32,
    )
    grad_probs = jnp.einsum(
        "bqhe,bkhe->bhqk", grad_attended, value_rows, preferred_element_type=jnp.float32
    )
    grad_scores = (
        probs * (grad_probs - jnp.sum(probs * grad_probs, axis=-1, keepdims=True))
    ).astype(jnp.bfloat16)
    grad_queries = (
        jnp.einsum("bhqk,bkhe->bqhe", grad_scores, key_rows, preferred_element_type=jnp.float32)
        * score_scale
    )
    grad_keys = (
        jnp.einsum("bhqk,bqhe->bkhe", grad_scores, queries, preferred_element_type=jnp.float32)
        * score_scale
    )
    grad_projected = jnp.stack([grad_queries, grad_keys, grad_values], axis=2).astype(jnp.bfloat16)
    grad_projected = grad_projected.reshape(row_count, 3, head_count * HD)
    grad_w_qkv = jnp.einsum(
        "rd,rcf->dcf", first, grad_projected, preferred_element_type=jnp.float32
    )
    partial_first = jnp.einsum(
        "rcf,dcf->rd", grad_projected, w_qkv, preferred_element_type=jnp.float32
    )
    both = exchange(partial_first.astype(jnp.bfloat16), 2, True, "pair", 2).astype(jnp.float32)
    grad_first = (both[0] + both[1]).astype(jnp.bfloat16).astype(jnp.float32)
    grad_input_norm, grad_gain_one, grad_shift_one = norm_backward(
        grad_first, normed_one, inverse_one, gain_rows[0]
    )
    grad_input = grad_hidden + grad_input_norm
    grads = (
        grad_w_qkv,
        grad_w_proj,
        grad_w_in,
        grad_w_out,
        grad_w_router,
        jnp.stack([grad_gain_one, grad_gain_two]),
        jnp.stack([grad_shift_one, grad_shift_two]),
    )
    return (grad_input.reshape(image_count, length, model_width), grads)


def make_local(n):
    def local(images, routes, w_qkv, w_proj, w_in, w_out, w_router, ln_gain, ln_bias, cotangent):
        shapes = [a.shape for a in (w_qkv, w_proj, w_in, w_out, w_router, ln_gain, ln_bias)]
        weights = gather_weights(w_qkv, w_proj, w_in, w_out, w_router, ln_gain, ln_bias, n)
        field = images.astype(jnp.float32)
        output, record = layer_forward(field, routes[0], weights)
        grad_input, grads = layer_backward(cotangent.astype(jnp.float32), record, weights)
        shards = scatter_grads(grads, n, [(1,) + tuple(s[1:]) for s in shapes])
        return (output, grad_input, *shards)

    return local


def solution(mesh):
    n = mesh.shape["dp"]
    in_specs = (
        P("dp", None, None),
        P(None, "dp", None, None),
        P(None, "dp", None, "mp"),
        P(None, "mp", "dp"),
        P(None, None, "dp", "mp"),
        P(None, None, "mp", "dp"),
        P(None, "dp", None),
        P(None, None, "dp"),
        P(None, None, "dp"),
        P("dp", None, None),
    )
    out_specs = (
        P("dp", None, None),
        P("dp", None, None),
        P(None, "dp", None, "mp"),
        P(None, "mp", "dp"),
        P(None, None, "dp", "mp"),
        P(None, None, "mp", "dp"),
        P(None, "dp", None),
        P(None, None, "dp"),
        P(None, None, "dp"),
    )
    return jax.shard_map(make_local(n), mesh=mesh, in_specs=in_specs, out_specs=out_specs, check_vma=False)
```

```python
import functools

import jax
import jax.numpy as jnp
from jax import lax
from jax.sharding import PartitionSpec as P
from jax.experimental import pallas as pl
from jax.experimental.pallas import tpu as pltpu

MESH = pl.DeviceIdType.MESH
LANES = 128

HD = 64
EXPERTS = 4
TOPK = 2
CAP = 104
EPSILON = 1e-06


def norm_forward(field, gain_row, shift_row):
    mean_value = jnp.mean(field, axis=-1, keepdims=True)
    centered = field - mean_value
    inverse = lax.rsqrt(jnp.mean(centered * centered, axis=-1, keepdims=True) + EPSILON)
    normed = centered * inverse
    return (normed * gain_row + shift_row, normed, inverse)


def norm_backward(grad_out, normed, inverse, gain_row):
    grad_gain = jnp.sum(grad_out * normed, axis=0)
    grad_shift = jnp.sum(grad_out, axis=0)
    scaled = grad_out * gain_row
    grad_in = inverse * (
        scaled
        - jnp.mean(scaled, axis=-1, keepdims=True)
        - normed * jnp.mean(scaled * normed, axis=-1, keepdims=True)
    )
    return (grad_in, grad_gain, grad_shift)


def slot_positions(chosen_ids):
    labels = jnp.arange(EXPERTS, dtype=jnp.int32)
    hit_counts = jnp.sum((chosen_ids[..., None] == labels).astype(jnp.int32), axis=-2)
    before = jnp.cumsum(hit_counts, axis=1) - hit_counts
    picked = chosen_ids[..., None] == labels
    return jnp.sum(jnp.where(picked, before[..., None, :], 0), axis=-1)


def gelu_slope(inner_pre):
    cumulative = 0.5 * (1.0 + jax.scipy.special.erf(inner_pre * 0.7071067811865476))
    density = jnp.exp(-0.5 * inner_pre * inner_pre) * 0.3989422804014327
    return cumulative + inner_pre * density


def group_of(kind):
    def chips():
        dp, mp = lax.axis_index("dp"), lax.axis_index("mp")
        return dp // 2, lambda i: (2 * i + dp % 2, mp)

    def cores():
        dp, mp = lax.axis_index("dp"), lax.axis_index("mp")
        return dp % 2, lambda i: (2 * (dp // 2) + i, mp)

    def whole():
        dp, mp = lax.axis_index("dp"), lax.axis_index("mp")
        return dp, lambda i: (i, mp)

    def pair():
        dp, mp = lax.axis_index("dp"), lax.axis_index("mp")
        return mp, lambda i: (dp, i)

    return {"chips": chips, "cores": cores, "pair": pair, "all": whole}[kind]


def exchange_kernel(m, pieces, gather, kind, x_ref, out_ref, send_sem, recv_sem, local_sem):
    me, device_of = group_of(kind)()
    step = out_ref.shape[1] // pieces
    barrier = pltpu.get_barrier_semaphore()

    def greet(k, carry):
        pl.semaphore_signal(
            barrier, inc=1, device_id=device_of(lax.rem(me + k, m)), device_id_type=MESH
        )
        return carry

    lax.fori_loop(1, m, greet, 0)
    pl.semaphore_wait(barrier, m - 1)
    own = pltpu.make_async_copy(x_ref if gather else x_ref.at[me], out_ref.at[me], local_sem)
    own.start()

    def describe(t):
        k = 1 + t // pieces
        part = pl.ds(pl.multiple_of((t % pieces) * step, step), step)
        peer = lax.rem(me + k, m)
        return pltpu.make_async_remote_copy(
            src_ref=x_ref.at[part] if gather else x_ref.at[peer, part],
            dst_ref=out_ref.at[me, part],
            send_sem=send_sem.at[t],
            recv_sem=recv_sem.at[t],
            device_id=device_of(peer),
            device_id_type=MESH,
        )

    def start(t, carry):
        describe(t).start()
        return carry

    def finish(t, carry):
        describe(t).wait()
        return carry

    count = (m - 1) * pieces
    lax.fori_loop(0, count, start, 0)
    lax.fori_loop(0, count, finish, 0)
    own.wait()


def exchange(x, m, gather, kind, collective_id, pieces=1):
    block = x.shape if gather else x.shape[1:]
    block_bytes = x.dtype.itemsize
    for d in block:
        block_bytes *= d
    count = (m - 1) * pieces
    return pl.pallas_call(
        functools.partial(exchange_kernel, m, pieces, gather, kind),
        out_shape=jax.ShapeDtypeStruct((m,) + tuple(block), x.dtype),
        in_specs=[pl.BlockSpec(memory_space=pl.ANY)],
        out_specs=pl.BlockSpec(memory_space=pl.ANY),
        scratch_shapes=[
            pltpu.SemaphoreType.DMA((count,)),
            pltpu.SemaphoreType.DMA((count,)),
            pltpu.SemaphoreType.DMA(()),
        ],
        compiler_params=pltpu.CompilerParams(collective_id=collective_id, has_side_effects=True),
        cost_estimate=pl.CostEstimate(flops=0, bytes_accessed=2 * m * block_bytes, transcendentals=0),
    )(x)


def relay_gather_kernel(chips, direct, x_ref, out_ref, sa, ra, sb, rb, sf, rf, sp, rp, sl):
    dp, mp = lax.axis_index("dp"), lax.axis_index("mp")
    n = 2 * chips
    core = dp % 2
    other = 1 - core
    chip = dp // 2
    barrier = pltpu.get_barrier_semaphore()

    def greet(k, carry):
        pl.semaphore_signal(
            barrier, inc=1, device_id=(lax.rem(dp + k, n), mp), device_id_type=MESH
        )
        return carry

    lax.fori_loop(1, n, greet, 0)
    pl.semaphore_wait(barrier, n - 1)
    own = pltpu.make_async_copy(x_ref, out_ref.at[dp], sl)
    own.start()

    def remote(src, dst, send, recv, target):
        return pltpu.make_async_remote_copy(
            src_ref=src, dst_ref=dst, send_sem=send, recv_sem=recv,
            device_id=(target, mp), device_id_type=MESH,
        )

    def same(j):
        return remote(x_ref, out_ref.at[dp], sa.at[j], ra.at[j], 2 * lax.rem(chip + j, chips) + core)

    def cross(j):
        return remote(x_ref, out_ref.at[dp], sb.at[j], rb.at[j], 2 * lax.rem(chip + j, chips) + other)

    def relay(j):
        slot = 2 * lax.rem(chip + chips - j, chips) + core
        return remote(out_ref.at[slot], out_ref.at[slot], sf.at[j], rf.at[j], 2 * chip + other)

    mate = remote(x_ref, out_ref.at[dp], sp, rp, 2 * chip + other)
    forwarded = [j for j in range(1, chips) if j not in direct]
    mate.start()
    for j in forwarded:
        same(j).start()
    for j in direct:
        cross(j).start()
    for j in direct:
        same(j).start()
    for j in forwarded:
        same(j).wait_recv()
        relay(j).start()
    for j in direct:
        same(j).wait_recv()
    for j in range(1, chips):
        same(j).wait_send()
    for j in direct:
        cross(j).wait()
    mate.wait()
    for j in forwarded:
        relay(j).wait()
    own.wait()


def relay_gather(x, n, collective_id):
    chips = n // 2
    direct = tuple(j for j in range(1, chips) if j % 4 == 0)
    block_bytes = x.dtype.itemsize
    for d in x.shape:
        block_bytes *= d
    return pl.pallas_call(
        functools.partial(relay_gather_kernel, chips, direct),
        out_shape=jax.ShapeDtypeStruct((n,) + tuple(x.shape), x.dtype),
        in_specs=[pl.BlockSpec(memory_space=pl.ANY)],
        out_specs=pl.BlockSpec(memory_space=pl.ANY),
        scratch_shapes=[pltpu.SemaphoreType.DMA((chips,))] * 6
        + [pltpu.SemaphoreType.DMA(())] * 3,
        compiler_params=pltpu.CompilerParams(collective_id=collective_id, has_side_effects=True),
        cost_estimate=pl.CostEstimate(flops=0, bytes_accessed=2 * n * block_bytes, transcendentals=0),
    )(x)


def relay_reduce_kernel(chips, direct, y_ref, out_same, out_cross, pin, sbuf, ss, rs, sc, rc, sr, rr, sl):
    dp, mp = lax.axis_index("dp"), lax.axis_index("mp")
    n = 2 * chips
    core = dp % 2
    other = 1 - core
    chip = dp // 2
    mate_id = 2 * chip + other
    barrier = pltpu.get_barrier_semaphore()

    def greet(k, carry):
        pl.semaphore_signal(
            barrier, inc=1, device_id=(lax.rem(dp + k, n), mp), device_id_type=MESH
        )
        return carry

    lax.fori_loop(1, n, greet, 0)
    pl.semaphore_wait(barrier, n - 1)
    own = pltpu.make_async_copy(y_ref.at[dp], out_same.at[0], sl)
    own.start()

    def remote(src, dst, send, recv, target):
        return pltpu.make_async_remote_copy(
            src_ref=src, dst_ref=dst, send_sem=send, recv_sem=recv,
            device_id=(target, mp), device_id_type=MESH,
        )

    def target(j, c):
        return 2 * lax.rem(chip + j, chips) + c

    slot_of = {j: i + 1 for i, j in enumerate(direct)}
    forwarded = [j for j in range(1, chips) if j not in direct]

    def same(j):
        src = y_ref.at[target(j, core)] if j in direct else sbuf.at[j]
        return remote(src, out_same.at[j], ss.at[j], rs.at[j], target(j, core))

    def cross(j):
        i = slot_of[j]
        return remote(y_ref.at[target(j, other)], out_cross.at[i], sc.at[i], rc.at[i], target(j, other))

    def relay(j):
        return remote(y_ref.at[target(j, other)], pin.at[j], sr.at[j], rr.at[j], mate_id)

    mate = remote(y_ref.at[mate_id], out_cross.at[0], sc.at[0], rc.at[0], mate_id)
    for j in forwarded:
        relay(j).start()
    mate.start()
    for j in direct:
        cross(j).start()
        same(j).start()
    for j in forwarded:
        relay(j).wait_recv()
        total = y_ref[target(j, core)].astype(jnp.float32) + pin[j].astype(jnp.float32)
        sbuf[j] = total.astype(sbuf.dtype)
        same(j).start()
    for j in forwarded:
        relay(j).wait_send()
    for j in range(1, chips):
        same(j).wait()
    for j in direct:
        cross(j).wait()
    mate.wait()
    own.wait()


def relay_reduce(y, n, collective_id):
    chips = n // 2
    direct = tuple(j for j in range(1, chips) if j % 4 == 0)
    block = tuple(y.shape[1:])
    block_bytes = y.dtype.itemsize
    for d in block:
        block_bytes *= d
    same, cross = pl.pallas_call(
        functools.partial(relay_reduce_kernel, chips, direct),
        out_shape=(
            jax.ShapeDtypeStruct((chips,) + block, y.dtype),
            jax.ShapeDtypeStruct((len(direct) + 1,) + block, y.dtype),
        ),
        in_specs=[pl.BlockSpec(memory_space=pltpu.VMEM)],
        out_specs=(pl.BlockSpec(memory_space=pl.ANY), pl.BlockSpec(memory_space=pl.ANY)),
        scratch_shapes=[pltpu.VMEM((chips,) + block, y.dtype)] * 2
        + [pltpu.SemaphoreType.DMA((chips,))] * 6
        + [pltpu.SemaphoreType.DMA(())],
        compiler_params=pltpu.CompilerParams(collective_id=collective_id, has_side_effects=True),
        cost_estimate=pl.CostEstimate(flops=0, bytes_accessed=3 * n * block_bytes, transcendentals=0),
    )(y)
    return jnp.sum(same.astype(jnp.float32), axis=0) + jnp.sum(cross.astype(jnp.float32), axis=0)


def padded_rows(size, dtype_rows=16):
    rows = -(-size // LANES)
    return -(-rows // dtype_rows) * dtype_rows


def shard_sizes(w_qkv, w_proj, w_in, w_out, w_router, ln_gain, ln_bias):
    return [a.size for a in (w_qkv, w_proj, w_in, w_out, w_router, ln_gain, ln_bias)]


def gather_weights(w_qkv, w_proj, w_in, w_out, w_router, ln_gain, ln_bias, n):
    parts = (w_qkv, w_proj, w_in, w_out, w_router, ln_gain, ln_bias)
    flat = jnp.concatenate([a.reshape(-1) for a in parts])
    total = flat.shape[0]
    rows = padded_rows(total)
    flat = jnp.pad(flat, (0, rows * LANES - total)).reshape(rows, LANES)
    full = relay_gather(flat, n, 0).reshape(n, rows * LANES)
    pieces = []
    start = 0
    for a in parts:
        pieces.append(full[:, start:start + a.size].reshape((n,) + a.shape[1:]))
        start += a.size
    q, p, i, o, r, g, b = pieces
    gq = q.reshape((-1,) + w_qkv.shape[2:])
    gr = r.reshape((-1,) + w_router.shape[2:])
    gg = g.transpose(1, 0, 2).reshape(ln_gain.shape[1], -1)
    gb = b.transpose(1, 0, 2).reshape(ln_bias.shape[1], -1)
    return (gq, p, i, o, gr, gg, gb)


def scatter_grads(grads, n, shapes):
    gq, gp, gi, go, gr, gg, gb = grads
    rows = [
        gq.reshape(n, -1),
        gp.reshape(n, -1),
        gi.reshape(n, -1),
        go.reshape(n, -1),
        gr.reshape(n, -1),
        gg.reshape(gg.shape[0], n, -1).transpose(1, 0, 2).reshape(n, -1),
        gb.reshape(gb.shape[0], n, -1).transpose(1, 0, 2).reshape(n, -1),
    ]
    packed = jnp.concatenate(rows, axis=1)
    total = packed.shape[1]
    count = padded_rows(total)
    packed = jnp.pad(packed, ((0, 0), (0, count * LANES - total))).reshape(n, count, LANES)
    mine = relay_reduce(packed.astype(jnp.bfloat16), n, 1).reshape(-1)
    outs = []
    start = 0
    for shape in shapes:
        size = 1
        for d in shape:
            size *= d
        outs.append(mine[start:start + size].reshape(shape))
        start += size
    return outs


def layer_forward(field, chosen_ids, weights):
    w_qkv, w_proj, w_in, w_out, w_router, ln_gain, ln_bias = weights
    image_count, length, model_width = field.shape
    row_count = image_count * length
    head_count = w_qkv.shape[2] // HD
    score_scale = HD ** (-0.5)
    gain_rows = ln_gain.astype(jnp.float32)
    shift_rows = ln_bias.astype(jnp.float32)
    flat = field.reshape(row_count, model_width)
    first, normed_one, inverse_one = norm_forward(flat, gain_rows[0], shift_rows[0])
    first = first.astype(jnp.bfloat16)
    projected = jnp.einsum("rd,dcf->rcf", first, w_qkv, preferred_element_type=jnp.float32).astype(
        jnp.bfloat16
    )
    projected = projected.reshape(image_count, length, 3, head_count, HD)
    queries = projected[:, :, 0]
    key_rows = projected[:, :, 1]
    value_rows = projected[:, :, 2]
    scores = (
        jnp.einsum("bqhe,bkhe->bhqk", queries, key_rows, preferred_element_type=jnp.float32)
        * score_scale
    )
    log_total = jax.nn.logsumexp(scores, axis=-1)
    attn_weights = jnp.exp(scores - log_total[..., None]).astype(jnp.bfloat16)
    attended = jnp.einsum(
        "bhqk,bkhe->bqhe", attn_weights, value_rows, preferred_element_type=jnp.float32
    )
    attended = attended.astype(jnp.bfloat16).reshape(row_count, head_count * HD)
    partial_attn = jnp.einsum(
        "rf,jfk->rjk", attended, w_proj, preferred_element_type=jnp.float32
    ).reshape(row_count, model_width)
    hidden = flat + lax.psum(partial_attn, "mp")
    second, normed_two, inverse_two = norm_forward(hidden, gain_rows[1], shift_rows[1])
    second = second.astype(jnp.bfloat16)
    logits = jnp.dot(second, w_router, preferred_element_type=jnp.float32)
    router = jax.nn.softmax(logits, axis=-1)
    labels = jnp.arange(EXPERTS, dtype=jnp.int32)
    ids_flat = chosen_ids.reshape(row_count, TOPK)
    chosen = (ids_flat[:, :, None] == labels).astype(jnp.float32)
    gate_values = jnp.sum(router[:, None, :] * chosen, axis=-1)
    per_image = EXPERTS * CAP
    image_base = (jnp.arange(image_count, dtype=jnp.int32) * per_image)[:, None, None]
    slot_index = (chosen_ids * CAP + slot_positions(chosen_ids) + image_base).reshape(-1)
    owners = (
        jnp.full((image_count * per_image,), row_count, jnp.int32)
        .at[slot_index]
        .set(jnp.repeat(jnp.arange(row_count, dtype=jnp.int32), TOPK))
    )
    slot_gate = (
        jnp.zeros((image_count * per_image,), jnp.float32).at[slot_index].set(gate_values.reshape(-1))
    )
    padded = jnp.concatenate([second, jnp.zeros((1, model_width), jnp.bfloat16)], axis=0)
    slot_rows = jnp.take(padded, owners, axis=0).reshape(image_count, EXPERTS, CAP, model_width)
    slot_split = slot_rows.reshape(slot_rows.shape[:3] + w_in.shape[:1] + w_in.shape[2:3])
    inner_pre = jnp.einsum("becjk,jekf->becf", slot_split, w_in, preferred_element_type=jnp.float32)
    activated = jax.nn.gelu(inner_pre, approximate=False).astype(jnp.bfloat16)
    produced = jnp.einsum("becf,jefk->becjk", activated, w_out, preferred_element_type=jnp.float32)
    produced = produced.reshape(image_count * per_image, model_width)
    picked = jnp.take(produced, slot_index, axis=0).reshape(row_count, TOPK, model_width)
    partial_moe = jnp.sum(gate_values[:, :, None] * picked, axis=1)
    both = exchange(partial_moe.astype(jnp.bfloat16), 2, True, "pair", 3).astype(jnp.float32)
    output = hidden + (both[0] + both[1]).astype(jnp.bfloat16).astype(jnp.float32)
    record = (
        normed_one, inverse_one, first, projected, log_total, attended, normed_two, inverse_two,
        second, router, chosen, slot_index, owners, slot_gate, slot_rows, inner_pre, activated, picked,
    )
    return (output.reshape(image_count, length, model_width), record)


def layer_backward(grad_field, record, weights):
    w_qkv, w_proj, w_in, w_out, w_router, ln_gain, ln_bias = weights
    (
        normed_one, inverse_one, first, projected, log_total, attended, normed_two, inverse_two,
        second, router, chosen, slot_index, owners, slot_gate, slot_rows, inner_pre, activated, picked,
    ) = record
    image_count, length, model_width = grad_field.shape
    row_count = image_count * length
    head_count = projected.shape[3]
    score_scale = HD ** (-0.5)
    gain_rows = ln_gain.astype(jnp.float32)
    grad_flat = grad_field.reshape(row_count, model_width)
    padded_grad = jnp.concatenate([grad_flat, jnp.zeros((1, model_width), jnp.float32)], axis=0)
    grad_slots = (jnp.take(padded_grad, owners, axis=0) * slot_gate[:, None]).astype(jnp.bfloat16)
    split = (w_out.shape[0], w_out.shape[3])
    grad_slots = grad_slots.reshape((image_count, EXPERTS, CAP) + split)
    slot_split = slot_rows.reshape((image_count, EXPERTS, CAP) + split)
    grad_w_out = jnp.einsum(
        "becf,becjk->jefk", activated, grad_slots, preferred_element_type=jnp.float32
    )
    grad_act = jnp.einsum("becjk,jefk->becf", grad_slots, w_out, preferred_element_type=jnp.float32)
    grad_inner = (grad_act * gelu_slope(inner_pre)).astype(jnp.bfloat16)
    grad_w_in = jnp.einsum(
        "becjk,becf->jekf", slot_split, grad_inner, preferred_element_type=jnp.float32
    )
    grad_slot_rows = jnp.einsum(
        "becf,jekf->becjk", grad_inner, w_in, preferred_element_type=jnp.float32
    )
    grad_slot_rows = grad_slot_rows.reshape(image_count * EXPERTS * CAP, model_width)
    partial_second = jnp.sum(
        jnp.take(grad_slot_rows, slot_index, axis=0).reshape(row_count, TOPK, model_width), axis=1
    )
    partial_gate = jnp.sum(picked * grad_flat[:, None, :], axis=-1)
    joined = lax.psum(jnp.concatenate([partial_second, partial_gate], axis=1), "mp")
    grad_second, grad_gate = joined[:, :model_width], joined[:, model_width:]
    grad_router = jnp.sum(grad_gate[:, :, None] * chosen, axis=1)
    grad_logits = router * (grad_router - jnp.sum(router * grad_router, axis=-1, keepdims=True))
    grad_logits = grad_logits.astype(jnp.bfloat16)
    grad_w_router = jnp.dot(second.T, grad_logits, preferred_element_type=jnp.float32)
    grad_second = grad_second + jnp.dot(grad_logits, w_router.T, preferred_element_type=jnp.float32)
    grad_from_norm, grad_gain_two, grad_shift_two = norm_backward(
        grad_second, normed_two, inverse_two, gain_rows[1]
    )
    grad_hidden = grad_flat + grad_from_norm
    grad_hidden_low = grad_hidden.astype(jnp.bfloat16)
    grad_hidden_split = grad_hidden_low.reshape((row_count,) + split)
    grad_w_proj = jnp.einsum(
        "rf,rjk->jfk", attended, grad_hidden_split, preferred_element_type=jnp.float32
    )
    grad_attended = jnp.einsum(
        "rjk,jfk->rf", grad_hidden_split, w_proj, preferred_element_type=jnp.float32
    ).astype(jnp.bfloat16)
    grad_attended = grad_attended.reshape(image_count, length, head_count, HD)
    queries = projected[:, :, 0]
    key_rows = projected[:, :, 1]
    value_rows = projected[:, :, 2]
    scores = (
        jnp.einsum("bqhe,bkhe->bhqk", queries, key_rows, preferred_element_type=jnp.float32)
        * score_scale
    )
    probs = jnp.exp(scores - log_total[..., None])
    grad_values = jnp.einsum(
        "bhqk,bqhe->bkhe", probs.astype(jnp.bfloat16), grad_attended,
        preferred_element_type=jnp.float32,
    )
    grad_probs = jnp.einsum(
        "bqhe,bkhe->bhqk", grad_attended, value_rows, preferred_element_type=jnp.float32
    )
    grad_scores = (
        probs * (grad_probs - jnp.sum(probs * grad_probs, axis=-1, keepdims=True))
    ).astype(jnp.bfloat16)
    grad_queries = (
        jnp.einsum("bhqk,bkhe->bqhe", grad_scores, key_rows, preferred_element_type=jnp.float32)
        * score_scale
    )
    grad_keys = (
        jnp.einsum("bhqk,bqhe->bkhe", grad_scores, queries, preferred_element_type=jnp.float32)
        * score_scale
    )
    grad_projected = jnp.stack([grad_queries, grad_keys, grad_values], axis=2).astype(jnp.bfloat16)
    grad_projected = grad_projected.reshape(row_count, 3, head_count * HD)
    grad_w_qkv = jnp.einsum(
        "rd,rcf->dcf", first, grad_projected, preferred_element_type=jnp.float32
    )
    partial_first = jnp.einsum(
        "rcf,dcf->rd", grad_projected, w_qkv, preferred_element_type=jnp.float32
    )
    both = exchange(partial_first.astype(jnp.bfloat16), 2, True, "pair", 2).astype(jnp.float32)
    grad_first = (both[0] + both[1]).astype(jnp.bfloat16).astype(jnp.float32)
    grad_input_norm, grad_gain_one, grad_shift_one = norm_backward(
        grad_first, normed_one, inverse_one, gain_rows[0]
    )
    grad_input = grad_hidden + grad_input_norm
    grads = (
        grad_w_qkv,
        grad_w_proj,
        grad_w_in,
        grad_w_out,
        grad_w_router,
        jnp.stack([grad_gain_one, grad_gain_two]),
        jnp.stack([grad_shift_one, grad_shift_two]),
    )
    return (grad_input.reshape(image_count, length, model_width), grads)


def make_local(n):
    def local(images, routes, w_qkv, w_proj, w_in, w_out, w_router, ln_gain, ln_bias, cotangent):
        shapes = [a.shape for a in (w_qkv, w_proj, w_in, w_out, w_router, ln_gain, ln_bias)]
        weights = gather_weights(w_qkv, w_proj, w_in, w_out, w_router, ln_gain, ln_bias, n)
        field = images.astype(jnp.float32)
        output, record = layer_forward(field, routes[0], weights)
        grad_input, grads = layer_backward(cotangent.astype(jnp.float32), record, weights)
        shards = scatter_grads(grads, n, [(1,) + tuple(s[1:]) for s in shapes])
        return (output, grad_input, *shards)

    return local


def solution(mesh):
    n = mesh.shape["dp"]
    in_specs = (
        P("dp", None, None),
        P(None, "dp", None, None),
        P(None, "dp", None, "mp"),
        P(None, "mp", "dp"),
        P(None, None, "dp", "mp"),
        P(None, None, "mp", "dp"),
        P(None, "dp", None),
        P(None, None, "dp"),
        P(None, None, "dp"),
        P("dp", None, None),
    )
    out_specs = (
        P("dp", None, None),
        P("dp", None, None),
        P(None, "dp", None, "mp"),
        P(None, "mp", "dp"),
        P(None, None, "dp", "mp"),
        P(None, None, "mp", "dp"),
        P(None, "dp", None),
        P(None, None, "dp"),
        P(None, None, "dp"),
    )
    return jax.shard_map(make_local(n), mesh=mesh, in_specs=in_specs, out_specs=out_specs, check_vma=False)
```

```python
import functools

import jax
import jax.numpy as jnp
from jax import lax
from jax.sharding import PartitionSpec as P
from jax.experimental import pallas as pl
from jax.experimental.pallas import tpu as pltpu

MESH = pl.DeviceIdType.MESH
LANES = 128

HD = 64
EXPERTS = 4
TOPK = 2
CAP = 104
EPSILON = 1e-06


def norm_forward(field, gain_row, shift_row):
    mean_value = jnp.mean(field, axis=-1, keepdims=True)
    centered = field - mean_value
    inverse = lax.rsqrt(jnp.mean(centered * centered, axis=-1, keepdims=True) + EPSILON)
    normed = centered * inverse
    return (normed * gain_row + shift_row, normed, inverse)


def norm_backward(grad_out, normed, inverse, gain_row):
    grad_gain = jnp.sum(grad_out * normed, axis=0)
    grad_shift = jnp.sum(grad_out, axis=0)
    scaled = grad_out * gain_row
    grad_in = inverse * (
        scaled
        - jnp.mean(scaled, axis=-1, keepdims=True)
        - normed * jnp.mean(scaled * normed, axis=-1, keepdims=True)
    )
    return (grad_in, grad_gain, grad_shift)


def slot_positions(chosen_ids):
    labels = jnp.arange(EXPERTS, dtype=jnp.int32)
    hit_counts = jnp.sum((chosen_ids[..., None] == labels).astype(jnp.int32), axis=-2)
    before = jnp.cumsum(hit_counts, axis=1) - hit_counts
    picked = chosen_ids[..., None] == labels
    return jnp.sum(jnp.where(picked, before[..., None, :], 0), axis=-1)


def gelu_slope(inner_pre):
    cumulative = 0.5 * (1.0 + jax.scipy.special.erf(inner_pre * 0.7071067811865476))
    density = jnp.exp(-0.5 * inner_pre * inner_pre) * 0.3989422804014327
    return cumulative + inner_pre * density


def group_of(kind):
    def chips():
        dp, mp = lax.axis_index("dp"), lax.axis_index("mp")
        return dp // 2, lambda i: (2 * i + dp % 2, mp)

    def cores():
        dp, mp = lax.axis_index("dp"), lax.axis_index("mp")
        return dp % 2, lambda i: (2 * (dp // 2) + i, mp)

    def whole():
        dp, mp = lax.axis_index("dp"), lax.axis_index("mp")
        return dp, lambda i: (i, mp)

    def pair():
        dp, mp = lax.axis_index("dp"), lax.axis_index("mp")
        return mp, lambda i: (dp, i)

    return {"chips": chips, "cores": cores, "pair": pair, "all": whole}[kind]


def exchange_kernel(m, pieces, gather, kind, x_ref, out_ref, send_sem, recv_sem, local_sem):
    me, device_of = group_of(kind)()
    step = out_ref.shape[1] // pieces
    barrier = pltpu.get_barrier_semaphore()

    def greet(k, carry):
        pl.semaphore_signal(
            barrier, inc=1, device_id=device_of(lax.rem(me + k, m)), device_id_type=MESH
        )
        return carry

    lax.fori_loop(1, m, greet, 0)
    pl.semaphore_wait(barrier, m - 1)
    own = pltpu.make_async_copy(x_ref if gather else x_ref.at[me], out_ref.at[me], local_sem)
    own.start()

    def describe(t):
        k = 1 + t // pieces
        part = pl.ds(pl.multiple_of((t % pieces) * step, step), step)
        peer = lax.rem(me + k, m)
        return pltpu.make_async_remote_copy(
            src_ref=x_ref.at[part] if gather else x_ref.at[peer, part],
            dst_ref=out_ref.at[me, part],
            send_sem=send_sem.at[t],
            recv_sem=recv_sem.at[t],
            device_id=device_of(peer),
            device_id_type=MESH,
        )

    def start(t, carry):
        describe(t).start()
        return carry

    def finish(t, carry):
        describe(t).wait()
        return carry

    count = (m - 1) * pieces
    lax.fori_loop(0, count, start, 0)
    lax.fori_loop(0, count, finish, 0)
    own.wait()


def exchange(x, m, gather, kind, collective_id, pieces=1):
    block = x.shape if gather else x.shape[1:]
    block_bytes = x.dtype.itemsize
    for d in block:
        block_bytes *= d
    count = (m - 1) * pieces
    return pl.pallas_call(
        functools.partial(exchange_kernel, m, pieces, gather, kind),
        out_shape=jax.ShapeDtypeStruct((m,) + tuple(block), x.dtype),
        in_specs=[pl.BlockSpec(memory_space=pl.ANY)],
        out_specs=pl.BlockSpec(memory_space=pl.ANY),
        scratch_shapes=[
            pltpu.SemaphoreType.DMA((count,)),
            pltpu.SemaphoreType.DMA((count,)),
            pltpu.SemaphoreType.DMA(()),
        ],
        compiler_params=pltpu.CompilerParams(collective_id=collective_id, has_side_effects=True),
        cost_estimate=pl.CostEstimate(flops=0, bytes_accessed=2 * m * block_bytes, transcendentals=0),
    )(x)


def relay_gather_kernel(chips, direct, x_ref, out_ref, sa, ra, sb, rb, sf, rf, sp, rp, sl):
    dp, mp = lax.axis_index("dp"), lax.axis_index("mp")
    n = 2 * chips
    core = dp % 2
    other = 1 - core
    chip = dp // 2
    barrier = pltpu.get_barrier_semaphore()

    def greet(k, carry):
        pl.semaphore_signal(
            barrier, inc=1, device_id=(lax.rem(dp + k, n), mp), device_id_type=MESH
        )
        return carry

    lax.fori_loop(1, n, greet, 0)
    pl.semaphore_wait(barrier, n - 1)
    own = pltpu.make_async_copy(x_ref, out_ref.at[dp], sl)
    own.start()

    def remote(src, dst, send, recv, target):
        return pltpu.make_async_remote_copy(
            src_ref=src, dst_ref=dst, send_sem=send, recv_sem=recv,
            device_id=(target, mp), device_id_type=MESH,
        )

    def same(j):
        return remote(x_ref, out_ref.at[dp], sa.at[j], ra.at[j], 2 * lax.rem(chip + j, chips) + core)

    def cross(j):
        return remote(x_ref, out_ref.at[dp], sb.at[j], rb.at[j], 2 * lax.rem(chip + j, chips) + other)

    def relay(j):
        slot = 2 * lax.rem(chip + chips - j, chips) + core
        return remote(out_ref.at[slot], out_ref.at[slot], sf.at[j], rf.at[j], 2 * chip + other)

    mate = remote(x_ref, out_ref.at[dp], sp, rp, 2 * chip + other)
    forwarded = [j for j in range(1, chips) if j not in direct]
    mate.start()
    for j in forwarded:
        same(j).start()
    for j in direct:
        cross(j).start()
    for j in direct:
        same(j).start()
    for j in forwarded:
        same(j).wait_recv()
        relay(j).start()
    for j in direct:
        same(j).wait_recv()
    for j in range(1, chips):
        same(j).wait_send()
    for j in direct:
        cross(j).wait()
    mate.wait()
    for j in forwarded:
        relay(j).wait()
    own.wait()


def relay_gather(x, n, collective_id):
    chips = n // 2
    direct = tuple(j for j in range(1, chips) if j % 4 == 0 or j in (1, chips - 1))
    block_bytes = x.dtype.itemsize
    for d in x.shape:
        block_bytes *= d
    return pl.pallas_call(
        functools.partial(relay_gather_kernel, chips, direct),
        out_shape=jax.ShapeDtypeStruct((n,) + tuple(x.shape), x.dtype),
        in_specs=[pl.BlockSpec(memory_space=pl.ANY)],
        out_specs=pl.BlockSpec(memory_space=pl.ANY),
        scratch_shapes=[pltpu.SemaphoreType.DMA((chips,))] * 6
        + [pltpu.SemaphoreType.DMA(())] * 3,
        compiler_params=pltpu.CompilerParams(collective_id=collective_id, has_side_effects=True),
        cost_estimate=pl.CostEstimate(flops=0, bytes_accessed=2 * n * block_bytes, transcendentals=0),
    )(x)


def relay_reduce_kernel(chips, direct, y_ref, out_same, out_cross, pin, sbuf, ss, rs, sc, rc, sr, rr, sl):
    dp, mp = lax.axis_index("dp"), lax.axis_index("mp")
    n = 2 * chips
    core = dp % 2
    other = 1 - core
    chip = dp // 2
    mate_id = 2 * chip + other
    barrier = pltpu.get_barrier_semaphore()

    def greet(k, carry):
        pl.semaphore_signal(
            barrier, inc=1, device_id=(lax.rem(dp + k, n), mp), device_id_type=MESH
        )
        return carry

    lax.fori_loop(1, n, greet, 0)
    pl.semaphore_wait(barrier, n - 1)
    own = pltpu.make_async_copy(y_ref.at[dp], out_same.at[0], sl)
    own.start()

    def remote(src, dst, send, recv, target):
        return pltpu.make_async_remote_copy(
            src_ref=src, dst_ref=dst, send_sem=send, recv_sem=recv,
            device_id=(target, mp), device_id_type=MESH,
        )

    def target(j, c):
        return 2 * lax.rem(chip + j, chips) + c

    slot_of = {j: i + 1 for i, j in enumerate(direct)}
    forwarded = [j for j in range(1, chips) if j not in direct]

    def same(j):
        src = y_ref.at[target(j, core)] if j in direct else sbuf.at[j]
        return remote(src, out_same.at[j], ss.at[j], rs.at[j], target(j, core))

    def cross(j):
        i = slot_of[j]
        return remote(y_ref.at[target(j, other)], out_cross.at[i], sc.at[i], rc.at[i], target(j, other))

    def relay(j):
        return remote(y_ref.at[target(j, other)], pin.at[j], sr.at[j], rr.at[j], mate_id)

    mate = remote(y_ref.at[mate_id], out_cross.at[0], sc.at[0], rc.at[0], mate_id)
    for j in forwarded:
        relay(j).start()
    mate.start()
    for j in direct:
        cross(j).start()
        same(j).start()
    for j in forwarded:
        relay(j).wait_recv()
        total = y_ref[target(j, core)].astype(jnp.float32) + pin[j].astype(jnp.float32)
        sbuf[j] = total.astype(sbuf.dtype)
        same(j).start()
    for j in forwarded:
        relay(j).wait_send()
    for j in range(1, chips):
        same(j).wait()
    for j in direct:
        cross(j).wait()
    mate.wait()
    own.wait()


def relay_reduce(y, n, collective_id):
    chips = n // 2
    direct = tuple(j for j in range(1, chips) if j % 4 == 0 or j in (1, chips - 1))
    block = tuple(y.shape[1:])
    block_bytes = y.dtype.itemsize
    for d in block:
        block_bytes *= d
    same, cross = pl.pallas_call(
        functools.partial(relay_reduce_kernel, chips, direct),
        out_shape=(
            jax.ShapeDtypeStruct((chips,) + block, y.dtype),
            jax.ShapeDtypeStruct((len(direct) + 1,) + block, y.dtype),
        ),
        in_specs=[pl.BlockSpec(memory_space=pltpu.VMEM)],
        out_specs=(pl.BlockSpec(memory_space=pl.ANY), pl.BlockSpec(memory_space=pl.ANY)),
        scratch_shapes=[pltpu.VMEM((chips,) + block, y.dtype)] * 2
        + [pltpu.SemaphoreType.DMA((chips,))] * 6
        + [pltpu.SemaphoreType.DMA(())],
        compiler_params=pltpu.CompilerParams(collective_id=collective_id, has_side_effects=True),
        cost_estimate=pl.CostEstimate(flops=0, bytes_accessed=3 * n * block_bytes, transcendentals=0),
    )(y)
    return jnp.sum(same.astype(jnp.float32), axis=0) + jnp.sum(cross.astype(jnp.float32), axis=0)


def padded_rows(size, dtype_rows=16):
    rows = -(-size // LANES)
    return -(-rows // dtype_rows) * dtype_rows


def shard_sizes(w_qkv, w_proj, w_in, w_out, w_router, ln_gain, ln_bias):
    return [a.size for a in (w_qkv, w_proj, w_in, w_out, w_router, ln_gain, ln_bias)]


def gather_weights(w_qkv, w_proj, w_in, w_out, w_router, ln_gain, ln_bias, n):
    parts = (w_qkv, w_proj, w_in, w_out, w_router, ln_gain, ln_bias)
    flat = jnp.concatenate([a.reshape(-1) for a in parts])
    total = flat.shape[0]
    rows = padded_rows(total)
    flat = jnp.pad(flat, (0, rows * LANES - total)).reshape(rows, LANES)
    full = relay_gather(flat, n, 0).reshape(n, rows * LANES)
    pieces = []
    start = 0
    for a in parts:
        pieces.append(full[:, start:start + a.size].reshape((n,) + a.shape[1:]))
        start += a.size
    q, p, i, o, r, g, b = pieces
    gq = q.reshape((-1,) + w_qkv.shape[2:])
    gr = r.reshape((-1,) + w_router.shape[2:])
    gg = g.transpose(1, 0, 2).reshape(ln_gain.shape[1], -1)
    gb = b.transpose(1, 0, 2).reshape(ln_bias.shape[1], -1)
    return (gq, p, i, o, gr, gg, gb)


def scatter_grads(grads, n, shapes):
    gq, gp, gi, go, gr, gg, gb = grads
    rows = [
        gq.reshape(n, -1),
        gp.reshape(n, -1),
        gi.reshape(n, -1),
        go.reshape(n, -1),
        gr.reshape(n, -1),
        gg.reshape(gg.shape[0], n, -1).transpose(1, 0, 2).reshape(n, -1),
        gb.reshape(gb.shape[0], n, -1).transpose(1, 0, 2).reshape(n, -1),
    ]
    packed = jnp.concatenate(rows, axis=1)
    total = packed.shape[1]
    count = padded_rows(total)
    packed = jnp.pad(packed, ((0, 0), (0, count * LANES - total))).reshape(n, count, LANES)
    mine = relay_reduce(packed.astype(jnp.bfloat16), n, 1).reshape(-1)
    outs = []
    start = 0
    for shape in shapes:
        size = 1
        for d in shape:
            size *= d
        outs.append(mine[start:start + size].reshape(shape))
        start += size
    return outs


def layer_forward(field, chosen_ids, weights):
    w_qkv, w_proj, w_in, w_out, w_router, ln_gain, ln_bias = weights
    image_count, length, model_width = field.shape
    row_count = image_count * length
    head_count = w_qkv.shape[2] // HD
    score_scale = HD ** (-0.5)
    gain_rows = ln_gain.astype(jnp.float32)
    shift_rows = ln_bias.astype(jnp.float32)
    flat = field.reshape(row_count, model_width)
    first, normed_one, inverse_one = norm_forward(flat, gain_rows[0], shift_rows[0])
    first = first.astype(jnp.bfloat16)
    projected = jnp.einsum("rd,dcf->rcf", first, w_qkv, preferred_element_type=jnp.float32).astype(
        jnp.bfloat16
    )
    projected = projected.reshape(image_count, length, 3, head_count, HD)
    queries = projected[:, :, 0]
    key_rows = projected[:, :, 1]
    value_rows = projected[:, :, 2]
    scores = (
        jnp.einsum("bqhe,bkhe->bhqk", queries, key_rows, preferred_element_type=jnp.float32)
        * score_scale
    )
    log_total = jax.nn.logsumexp(scores, axis=-1)
    attn_weights = jnp.exp(scores - log_total[..., None]).astype(jnp.bfloat16)
    attended = jnp.einsum(
        "bhqk,bkhe->bqhe", attn_weights, value_rows, preferred_element_type=jnp.float32
    )
    attended = attended.astype(jnp.bfloat16).reshape(row_count, head_count * HD)
    partial_attn = jnp.einsum(
        "rf,jfk->rjk", attended, w_proj, preferred_element_type=jnp.float32
    ).reshape(row_count, model_width)
    hidden = flat + lax.psum(partial_attn, "mp")
    second, normed_two, inverse_two = norm_forward(hidden, gain_rows[1], shift_rows[1])
    second = second.astype(jnp.bfloat16)
    logits = jnp.dot(second, w_router, preferred_element_type=jnp.float32)
    router = jax.nn.softmax(logits, axis=-1)
    labels = jnp.arange(EXPERTS, dtype=jnp.int32)
    ids_flat = chosen_ids.reshape(row_count, TOPK)
    chosen = (ids_flat[:, :, None] == labels).astype(jnp.float32)
    gate_values = jnp.sum(router[:, None, :] * chosen, axis=-1)
    per_image = EXPERTS * CAP
    image_base = (jnp.arange(image_count, dtype=jnp.int32) * per_image)[:, None, None]
    slot_index = (chosen_ids * CAP + slot_positions(chosen_ids) + image_base).reshape(-1)
    owners = (
        jnp.full((image_count * per_image,), row_count, jnp.int32)
        .at[slot_index]
        .set(jnp.repeat(jnp.arange(row_count, dtype=jnp.int32), TOPK))
    )
    slot_gate = (
        jnp.zeros((image_count * per_image,), jnp.float32).at[slot_index].set(gate_values.reshape(-1))
    )
    padded = jnp.concatenate([second, jnp.zeros((1, model_width), jnp.bfloat16)], axis=0)
    slot_rows = jnp.take(padded, owners, axis=0).reshape(image_count, EXPERTS, CAP, model_width)
    slot_split = slot_rows.reshape(slot_rows.shape[:3] + w_in.shape[:1] + w_in.shape[2:3])
    inner_pre = jnp.einsum("becjk,jekf->becf", slot_split, w_in, preferred_element_type=jnp.float32)
    activated = jax.nn.gelu(inner_pre, approximate=False).astype(jnp.bfloat16)
    produced = jnp.einsum("becf,jefk->becjk", activated, w_out, preferred_element_type=jnp.float32)
    produced = produced.reshape(image_count * per_image, model_width)
    picked = jnp.take(produced, slot_index, axis=0).reshape(row_count, TOPK, model_width)
    partial_moe = jnp.sum(gate_values[:, :, None] * picked, axis=1)
    both = exchange(partial_moe.astype(jnp.bfloat16), 2, True, "pair", 3).astype(jnp.float32)
    output = hidden + (both[0] + both[1]).astype(jnp.bfloat16).astype(jnp.float32)
    record = (
        normed_one, inverse_one, first, projected, log_total, attended, normed_two, inverse_two,
        second, router, chosen, slot_index, owners, slot_gate, slot_rows, inner_pre, activated, picked,
    )
    return (output.reshape(image_count, length, model_width), record)


def layer_backward(grad_field, record, weights):
    w_qkv, w_proj, w_in, w_out, w_router, ln_gain, ln_bias = weights
    (
        normed_one, inverse_one, first, projected, log_total, attended, normed_two, inverse_two,
        second, router, chosen, slot_index, owners, slot_gate, slot_rows, inner_pre, activated, picked,
    ) = record
    image_count, length, model_width = grad_field.shape
    row_count = image_count * length
    head_count = projected.shape[3]
    score_scale = HD ** (-0.5)
    gain_rows = ln_gain.astype(jnp.float32)
    grad_flat = grad_field.reshape(row_count, model_width)
    padded_grad = jnp.concatenate([grad_flat, jnp.zeros((1, model_width), jnp.float32)], axis=0)
    grad_slots = (jnp.take(padded_grad, owners, axis=0) * slot_gate[:, None]).astype(jnp.bfloat16)
    split = (w_out.shape[0], w_out.shape[3])
    grad_slots = grad_slots.reshape((image_count, EXPERTS, CAP) + split)
    slot_split = slot_rows.reshape((image_count, EXPERTS, CAP) + split)
    grad_w_out = jnp.einsum(
        "becf,becjk->jefk", activated, grad_slots, preferred_element_type=jnp.float32
    )
    grad_act = jnp.einsum("becjk,jefk->becf", grad_slots, w_out, preferred_element_type=jnp.float32)
    grad_inner = (grad_act * gelu_slope(inner_pre)).astype(jnp.bfloat16)
    grad_w_in = jnp.einsum(
        "becjk,becf->jekf", slot_split, grad_inner, preferred_element_type=jnp.float32
    )
    grad_slot_rows = jnp.einsum(
        "becf,jekf->becjk", grad_inner, w_in, preferred_element_type=jnp.float32
    )
    grad_slot_rows = grad_slot_rows.reshape(image_count * EXPERTS * CAP, model_width)
    partial_second = jnp.sum(
        jnp.take(grad_slot_rows, slot_index, axis=0).reshape(row_count, TOPK, model_width), axis=1
    )
    partial_gate = jnp.sum(picked * grad_flat[:, None, :], axis=-1)
    joined = lax.psum(jnp.concatenate([partial_second, partial_gate], axis=1), "mp")
    grad_second, grad_gate = joined[:, :model_width], joined[:, model_width:]
    grad_router = jnp.sum(grad_gate[:, :, None] * chosen, axis=1)
    grad_logits = router * (grad_router - jnp.sum(router * grad_router, axis=-1, keepdims=True))
    grad_logits = grad_logits.astype(jnp.bfloat16)
    grad_w_router = jnp.dot(second.T, grad_logits, preferred_element_type=jnp.float32)
    grad_second = grad_second + jnp.dot(grad_logits, w_router.T, preferred_element_type=jnp.float32)
    grad_from_norm, grad_gain_two, grad_shift_two = norm_backward(
        grad_second, normed_two, inverse_two, gain_rows[1]
    )
    grad_hidden = grad_flat + grad_from_norm
    grad_hidden_low = grad_hidden.astype(jnp.bfloat16)
    grad_hidden_split = grad_hidden_low.reshape((row_count,) + split)
    grad_w_proj = jnp.einsum(
        "rf,rjk->jfk", attended, grad_hidden_split, preferred_element_type=jnp.float32
    )
    grad_attended = jnp.einsum(
        "rjk,jfk->rf", grad_hidden_split, w_proj, preferred_element_type=jnp.float32
    ).astype(jnp.bfloat16)
    grad_attended = grad_attended.reshape(image_count, length, head_count, HD)
    queries = projected[:, :, 0]
    key_rows = projected[:, :, 1]
    value_rows = projected[:, :, 2]
    scores = (
        jnp.einsum("bqhe,bkhe->bhqk", queries, key_rows, preferred_element_type=jnp.float32)
        * score_scale
    )
    probs = jnp.exp(scores - log_total[..., None])
    grad_values = jnp.einsum(
        "bhqk,bqhe->bkhe", probs.astype(jnp.bfloat16), grad_attended,
        preferred_element_type=jnp.float32,
    )
    grad_probs = jnp.einsum(
        "bqhe,bkhe->bhqk", grad_attended, value_rows, preferred_element_type=jnp.float32
    )
    grad_scores = (
        probs * (grad_probs - jnp.sum(probs * grad_probs, axis=-1, keepdims=True))
    ).astype(jnp.bfloat16)
    grad_queries = (
        jnp.einsum("bhqk,bkhe->bqhe", grad_scores, key_rows, preferred_element_type=jnp.float32)
        * score_scale
    )
    grad_keys = (
        jnp.einsum("bhqk,bqhe->bkhe", grad_scores, queries, preferred_element_type=jnp.float32)
        * score_scale
    )
    grad_projected = jnp.stack([grad_queries, grad_keys, grad_values], axis=2).astype(jnp.bfloat16)
    grad_projected = grad_projected.reshape(row_count, 3, head_count * HD)
    grad_w_qkv = jnp.einsum(
        "rd,rcf->dcf", first, grad_projected, preferred_element_type=jnp.float32
    )
    partial_first = jnp.einsum(
        "rcf,dcf->rd", grad_projected, w_qkv, preferred_element_type=jnp.float32
    )
    both = exchange(partial_first.astype(jnp.bfloat16), 2, True, "pair", 2).astype(jnp.float32)
    grad_first = (both[0] + both[1]).astype(jnp.bfloat16).astype(jnp.float32)
    grad_input_norm, grad_gain_one, grad_shift_one = norm_backward(
        grad_first, normed_one, inverse_one, gain_rows[0]
    )
    grad_input = grad_hidden + grad_input_norm
    grads = (
        grad_w_qkv,
        grad_w_proj,
        grad_w_in,
        grad_w_out,
        grad_w_router,
        jnp.stack([grad_gain_one, grad_gain_two]),
        jnp.stack([grad_shift_one, grad_shift_two]),
    )
    return (grad_input.reshape(image_count, length, model_width), grads)


def make_local(n):
    def local(images, routes, w_qkv, w_proj, w_in, w_out, w_router, ln_gain, ln_bias, cotangent):
        shapes = [a.shape for a in (w_qkv, w_proj, w_in, w_out, w_router, ln_gain, ln_bias)]
        weights = gather_weights(w_qkv, w_proj, w_in, w_out, w_router, ln_gain, ln_bias, n)
        field = images.astype(jnp.float32)
        output, record = layer_forward(field, routes[0], weights)
        grad_input, grads = layer_backward(cotangent.astype(jnp.float32), record, weights)
        shards = scatter_grads(grads, n, [(1,) + tuple(s[1:]) for s in shapes])
        return (output, grad_input, *shards)

    return local


def solution(mesh):
    n = mesh.shape["dp"]
    in_specs = (
        P("dp", None, None),
        P(None, "dp", None, None),
        P(None, "dp", None, "mp"),
        P(None, "mp", "dp"),
        P(None, None, "dp", "mp"),
        P(None, None, "mp", "dp"),
        P(None, "dp", None),
        P(None, None, "dp"),
        P(None, None, "dp"),
        P("dp", None, None),
    )
    out_specs = (
        P("dp", None, None),
        P("dp", None, None),
        P(None, "dp", None, "mp"),
        P(None, "mp", "dp"),
        P(None, None, "dp", "mp"),
        P(None, None, "mp", "dp"),
        P(None, "dp", None),
        P(None, None, "dp"),
        P(None, None, "dp"),
    )
    return jax.shard_map(make_local(n), mesh=mesh, in_specs=in_specs, out_specs=out_specs, check_vma=False)
```

```python
import functools

import jax
import jax.numpy as jnp
from jax import lax
from jax.sharding import PartitionSpec as P
from jax.experimental import pallas as pl
from jax.experimental.pallas import tpu as pltpu

MESH = pl.DeviceIdType.MESH
LANES = 128

HD = 64
EXPERTS = 4
TOPK = 2
CAP = 104
EPSILON = 1e-06


def norm_forward(field, gain_row, shift_row):
    mean_value = jnp.mean(field, axis=-1, keepdims=True)
    centered = field - mean_value
    inverse = lax.rsqrt(jnp.mean(centered * centered, axis=-1, keepdims=True) + EPSILON)
    normed = centered * inverse
    return (normed * gain_row + shift_row, normed, inverse)


def norm_backward(grad_out, normed, inverse, gain_row):
    grad_gain = jnp.sum(grad_out * normed, axis=0)
    grad_shift = jnp.sum(grad_out, axis=0)
    scaled = grad_out * gain_row
    grad_in = inverse * (
        scaled
        - jnp.mean(scaled, axis=-1, keepdims=True)
        - normed * jnp.mean(scaled * normed, axis=-1, keepdims=True)
    )
    return (grad_in, grad_gain, grad_shift)


def slot_positions(chosen_ids):
    labels = jnp.arange(EXPERTS, dtype=jnp.int32)
    hit_counts = jnp.sum((chosen_ids[..., None] == labels).astype(jnp.int32), axis=-2)
    before = jnp.cumsum(hit_counts, axis=1) - hit_counts
    picked = chosen_ids[..., None] == labels
    return jnp.sum(jnp.where(picked, before[..., None, :], 0), axis=-1)


def gelu_slope(inner_pre):
    cumulative = 0.5 * (1.0 + jax.scipy.special.erf(inner_pre * 0.7071067811865476))
    density = jnp.exp(-0.5 * inner_pre * inner_pre) * 0.3989422804014327
    return cumulative + inner_pre * density


def group_of(kind):
    def chips():
        dp, mp = lax.axis_index("dp"), lax.axis_index("mp")
        return dp // 2, lambda i: (2 * i + dp % 2, mp)

    def cores():
        dp, mp = lax.axis_index("dp"), lax.axis_index("mp")
        return dp % 2, lambda i: (2 * (dp // 2) + i, mp)

    def whole():
        dp, mp = lax.axis_index("dp"), lax.axis_index("mp")
        return dp, lambda i: (i, mp)

    def pair():
        dp, mp = lax.axis_index("dp"), lax.axis_index("mp")
        return mp, lambda i: (dp, i)

    return {"chips": chips, "cores": cores, "pair": pair, "all": whole}[kind]


def exchange_kernel(m, pieces, gather, kind, x_ref, out_ref, send_sem, recv_sem, local_sem):
    me, device_of = group_of(kind)()
    step = out_ref.shape[1] // pieces
    barrier = pltpu.get_barrier_semaphore()

    def greet(k, carry):
        pl.semaphore_signal(
            barrier, inc=1, device_id=device_of(lax.rem(me + k, m)), device_id_type=MESH
        )
        return carry

    lax.fori_loop(1, m, greet, 0)
    pl.semaphore_wait(barrier, m - 1)
    own = pltpu.make_async_copy(x_ref if gather else x_ref.at[me], out_ref.at[me], local_sem)
    own.start()

    def describe(t):
        k = 1 + t // pieces
        part = pl.ds(pl.multiple_of((t % pieces) * step, step), step)
        peer = lax.rem(me + k, m)
        return pltpu.make_async_remote_copy(
            src_ref=x_ref.at[part] if gather else x_ref.at[peer, part],
            dst_ref=out_ref.at[me, part],
            send_sem=send_sem.at[t],
            recv_sem=recv_sem.at[t],
            device_id=device_of(peer),
            device_id_type=MESH,
        )

    def start(t, carry):
        describe(t).start()
        return carry

    def finish(t, carry):
        describe(t).wait()
        return carry

    count = (m - 1) * pieces
    lax.fori_loop(0, count, start, 0)
    lax.fori_loop(0, count, finish, 0)
    own.wait()


def exchange(x, m, gather, kind, collective_id, pieces=1):
    block = x.shape if gather else x.shape[1:]
    block_bytes = x.dtype.itemsize
    for d in block:
        block_bytes *= d
    count = (m - 1) * pieces
    return pl.pallas_call(
        functools.partial(exchange_kernel, m, pieces, gather, kind),
        out_shape=jax.ShapeDtypeStruct((m,) + tuple(block), x.dtype),
        in_specs=[pl.BlockSpec(memory_space=pl.ANY)],
        out_specs=pl.BlockSpec(memory_space=pl.ANY),
        scratch_shapes=[
            pltpu.SemaphoreType.DMA((count,)),
            pltpu.SemaphoreType.DMA((count,)),
            pltpu.SemaphoreType.DMA(()),
        ],
        compiler_params=pltpu.CompilerParams(collective_id=collective_id, has_side_effects=True),
        cost_estimate=pl.CostEstimate(flops=0, bytes_accessed=2 * m * block_bytes, transcendentals=0),
    )(x)


def relay_gather_kernel(chips, direct, x_ref, out_ref, sa, ra, sb, rb, sf, rf, sp, rp, sl):
    dp, mp = lax.axis_index("dp"), lax.axis_index("mp")
    n = 2 * chips
    core = dp % 2
    other = 1 - core
    chip = dp // 2
    barrier = pltpu.get_barrier_semaphore()

    def greet(k, carry):
        pl.semaphore_signal(
            barrier, inc=1, device_id=(lax.rem(dp + k, n), mp), device_id_type=MESH
        )
        return carry

    lax.fori_loop(1, n, greet, 0)
    pl.semaphore_wait(barrier, n - 1)
    own = pltpu.make_async_copy(x_ref, out_ref.at[dp], sl)
    own.start()

    def remote(src, dst, send, recv, target):
        return pltpu.make_async_remote_copy(
            src_ref=src, dst_ref=dst, send_sem=send, recv_sem=recv,
            device_id=(target, mp), device_id_type=MESH,
        )

    def same(j):
        return remote(x_ref, out_ref.at[dp], sa.at[j], ra.at[j], 2 * lax.rem(chip + j, chips) + core)

    def cross(j):
        return remote(x_ref, out_ref.at[dp], sb.at[j], rb.at[j], 2 * lax.rem(chip + j, chips) + other)

    def relay(j):
        slot = 2 * lax.rem(chip + chips - j, chips) + core
        return remote(out_ref.at[slot], out_ref.at[slot], sf.at[j], rf.at[j], 2 * chip + other)

    mate = remote(x_ref, out_ref.at[dp], sp, rp, 2 * chip + other)
    forwarded = [j for j in range(1, chips) if j not in direct]
    mate.start()
    for j in forwarded:
        same(j).start()
    for j in direct:
        cross(j).start()
    for j in direct:
        same(j).start()
    for j in forwarded:
        same(j).wait_recv()
        relay(j).start()
    for j in direct:
        same(j).wait_recv()
    for j in range(1, chips):
        same(j).wait_send()
    for j in direct:
        cross(j).wait()
    mate.wait()
    for j in forwarded:
        relay(j).wait()
    own.wait()


def relay_gather(x, n, collective_id):
    chips = n // 2
    direct = tuple(j for j in range(1, chips) if j % 4 == 0)
    block_bytes = x.dtype.itemsize
    for d in x.shape:
        block_bytes *= d
    return pl.pallas_call(
        functools.partial(relay_gather_kernel, chips, direct),
        out_shape=jax.ShapeDtypeStruct((n,) + tuple(x.shape), x.dtype),
        in_specs=[pl.BlockSpec(memory_space=pl.ANY)],
        out_specs=pl.BlockSpec(memory_space=pl.ANY),
        scratch_shapes=[pltpu.SemaphoreType.DMA((chips,))] * 6
        + [pltpu.SemaphoreType.DMA(())] * 3,
        compiler_params=pltpu.CompilerParams(collective_id=collective_id, has_side_effects=True),
        cost_estimate=pl.CostEstimate(flops=0, bytes_accessed=2 * n * block_bytes, transcendentals=0),
    )(x)


def relay_reduce_kernel(chips, direct, y_ref, received, pin, sbuf, ss, rs, sc, rc, sr, rr, sl):
    dp, mp = lax.axis_index("dp"), lax.axis_index("mp")
    n = 2 * chips
    core = dp % 2
    other = 1 - core
    chip = dp // 2
    mate_id = 2 * chip + other
    barrier = pltpu.get_barrier_semaphore()

    def greet(k, carry):
        pl.semaphore_signal(
            barrier, inc=1, device_id=(lax.rem(dp + k, n), mp), device_id_type=MESH
        )
        return carry

    lax.fori_loop(1, n, greet, 0)
    pl.semaphore_wait(barrier, n - 1)
    own = pltpu.make_async_copy(y_ref.at[dp], received.at[0], sl)
    own.start()

    def remote(src, dst, send, recv, target):
        return pltpu.make_async_remote_copy(
            src_ref=src, dst_ref=dst, send_sem=send, recv_sem=recv,
            device_id=(target, mp), device_id_type=MESH,
        )

    def target(j, c):
        return 2 * lax.rem(chip + j, chips) + c

    slot_of = {j: i + 1 for i, j in enumerate(direct)}
    forwarded = [j for j in range(1, chips) if j not in direct]

    def same(j):
        src = y_ref.at[target(j, core)] if j in direct else sbuf.at[j]
        return remote(src, received.at[j], ss.at[j], rs.at[j], target(j, core))

    def cross(j):
        i = slot_of[j]
        return remote(y_ref.at[target(j, other)], received.at[chips + i], sc.at[i], rc.at[i], target(j, other))

    def relay(j):
        return remote(y_ref.at[target(j, other)], pin.at[j], sr.at[j], rr.at[j], mate_id)

    mate = remote(y_ref.at[mate_id], received.at[chips], sc.at[0], rc.at[0], mate_id)
    for j in forwarded:
        relay(j).start()
    mate.start()
    for j in direct:
        cross(j).start()
        same(j).start()
    for j in forwarded:
        relay(j).wait_recv()
        total = y_ref[target(j, core)].astype(jnp.float32) + pin[j].astype(jnp.float32)
        sbuf[j] = total.astype(sbuf.dtype)
        same(j).start()
    for j in forwarded:
        relay(j).wait_send()
    for j in range(1, chips):
        same(j).wait()
    for j in direct:
        cross(j).wait()
    mate.wait()
    own.wait()


def relay_reduce(y, n, collective_id):
    chips = n // 2
    direct = tuple(j for j in range(1, chips) if j % 4 == 0)
    block = tuple(y.shape[1:])
    block_bytes = y.dtype.itemsize
    for d in block:
        block_bytes *= d
    received = pl.pallas_call(
        functools.partial(relay_reduce_kernel, chips, direct),
        out_shape=jax.ShapeDtypeStruct((chips + len(direct) + 1,) + block, y.dtype),
        in_specs=[pl.BlockSpec(memory_space=pltpu.VMEM)],
        out_specs=pl.BlockSpec(memory_space=pl.ANY),
        scratch_shapes=[pltpu.VMEM((chips,) + block, y.dtype)] * 2
        + [pltpu.SemaphoreType.DMA((chips,))] * 6
        + [pltpu.SemaphoreType.DMA(())],
        compiler_params=pltpu.CompilerParams(collective_id=collective_id, has_side_effects=True),
        cost_estimate=pl.CostEstimate(flops=0, bytes_accessed=3 * n * block_bytes, transcendentals=0),
    )(y)
    return jnp.sum(received.astype(jnp.float32), axis=0)


def padded_rows(size, dtype_rows=16):
    rows = -(-size // LANES)
    return -(-rows // dtype_rows) * dtype_rows


def shard_sizes(w_qkv, w_proj, w_in, w_out, w_router, ln_gain, ln_bias):
    return [a.size for a in (w_qkv, w_proj, w_in, w_out, w_router, ln_gain, ln_bias)]


def gather_weights(w_qkv, w_proj, w_in, w_out, w_router, ln_gain, ln_bias, n):
    parts = (w_qkv, w_proj, w_in, w_out, w_router, ln_gain, ln_bias)
    flat = jnp.concatenate([a.reshape(-1) for a in parts])
    total = flat.shape[0]
    rows = padded_rows(total)
    flat = jnp.pad(flat, (0, rows * LANES - total)).reshape(rows, LANES)
    full = relay_gather(flat, n, 0).reshape(n, rows * LANES)
    pieces = []
    start = 0
    for a in parts:
        pieces.append(full[:, start:start + a.size].reshape((n,) + a.shape[1:]))
        start += a.size
    q, p, i, o, r, g, b = pieces
    gq = q.reshape((-1,) + w_qkv.shape[2:])
    gr = r.reshape((-1,) + w_router.shape[2:])
    gg = g.transpose(1, 0, 2).reshape(ln_gain.shape[1], -1)
    gb = b.transpose(1, 0, 2).reshape(ln_bias.shape[1], -1)
    return (gq, p, i, o, gr, gg, gb)


def scatter_grads(grads, n, shapes):
    gq, gp, gi, go, gr, gg, gb = grads
    rows = [
        gq.reshape(n, -1),
        gp.reshape(n, -1),
        gi.reshape(n, -1),
        go.reshape(n, -1),
        gr.reshape(n, -1),
        gg.reshape(gg.shape[0], n, -1).transpose(1, 0, 2).reshape(n, -1),
        gb.reshape(gb.shape[0], n, -1).transpose(1, 0, 2).reshape(n, -1),
    ]
    packed = jnp.concatenate(rows, axis=1)
    total = packed.shape[1]
    count = padded_rows(total)
    packed = jnp.pad(packed, ((0, 0), (0, count * LANES - total))).reshape(n, count, LANES)
    mine = relay_reduce(packed.astype(jnp.bfloat16), n, 1).reshape(-1)
    outs = []
    start = 0
    for shape in shapes:
        size = 1
        for d in shape:
            size *= d
        outs.append(mine[start:start + size].reshape(shape))
        start += size
    return outs


def layer_forward(field, chosen_ids, weights):
    w_qkv, w_proj, w_in, w_out, w_router, ln_gain, ln_bias = weights
    image_count, length, model_width = field.shape
    row_count = image_count * length
    head_count = w_qkv.shape[2] // HD
    score_scale = HD ** (-0.5)
    gain_rows = ln_gain.astype(jnp.float32)
    shift_rows = ln_bias.astype(jnp.float32)
    flat = field.reshape(row_count, model_width)
    first, normed_one, inverse_one = norm_forward(flat, gain_rows[0], shift_rows[0])
    first = first.astype(jnp.bfloat16)
    projected = jnp.einsum("rd,dcf->rcf", first, w_qkv, preferred_element_type=jnp.float32).astype(
        jnp.bfloat16
    )
    projected = projected.reshape(image_count, length, 3, head_count, HD)
    queries = projected[:, :, 0]
    key_rows = projected[:, :, 1]
    value_rows = projected[:, :, 2]
    scores = (
        jnp.einsum("bqhe,bkhe->bhqk", queries, key_rows, preferred_element_type=jnp.float32)
        * score_scale
    )
    log_total = jax.nn.logsumexp(scores, axis=-1)
    attn_weights = jnp.exp(scores - log_total[..., None]).astype(jnp.bfloat16)
    attended = jnp.einsum(
        "bhqk,bkhe->bqhe", attn_weights, value_rows, preferred_element_type=jnp.float32
    )
    attended = attended.astype(jnp.bfloat16).reshape(row_count, head_count * HD)
    partial_attn = jnp.einsum(
        "rf,jfk->rjk", attended, w_proj, preferred_element_type=jnp.float32
    ).reshape(row_count, model_width)
    hidden = flat + lax.psum(partial_attn, "mp")
    second, normed_two, inverse_two = norm_forward(hidden, gain_rows[1], shift_rows[1])
    second = second.astype(jnp.bfloat16)
    logits = jnp.dot(second, w_router, preferred_element_type=jnp.float32)
    router = jax.nn.softmax(logits, axis=-1)
    labels = jnp.arange(EXPERTS, dtype=jnp.int32)
    ids_flat = chosen_ids.reshape(row_count, TOPK)
    chosen = (ids_flat[:, :, None] == labels).astype(jnp.float32)
    gate_values = jnp.sum(router[:, None, :] * chosen, axis=-1)
    per_image = EXPERTS * CAP
    image_base = (jnp.arange(image_count, dtype=jnp.int32) * per_image)[:, None, None]
    slot_index = (chosen_ids * CAP + slot_positions(chosen_ids) + image_base).reshape(-1)
    owners = (
        jnp.full((image_count * per_image,), row_count, jnp.int32)
        .at[slot_index]
        .set(jnp.repeat(jnp.arange(row_count, dtype=jnp.int32), TOPK))
    )
    slot_gate = (
        jnp.zeros((image_count * per_image,), jnp.float32).at[slot_index].set(gate_values.reshape(-1))
    )
    padded = jnp.concatenate([second, jnp.zeros((1, model_width), jnp.bfloat16)], axis=0)
    slot_rows = jnp.take(padded, owners, axis=0).reshape(image_count, EXPERTS, CAP, model_width)
    slot_split = slot_rows.reshape(slot_rows.shape[:3] + w_in.shape[:1] + w_in.shape[2:3])
    inner_pre = jnp.einsum("becjk,jekf->becf", slot_split, w_in, preferred_element_type=jnp.float32)
    activated = jax.nn.gelu(inner_pre, approximate=False).astype(jnp.bfloat16)
    produced = jnp.einsum("becf,jefk->becjk", activated, w_out, preferred_element_type=jnp.float32)
    produced = produced.reshape(image_count * per_image, model_width)
    picked = jnp.take(produced, slot_index, axis=0).reshape(row_count, TOPK, model_width)
    partial_moe = jnp.sum(gate_values[:, :, None] * picked, axis=1)
    both = exchange(partial_moe.astype(jnp.bfloat16), 2, True, "pair", 3).astype(jnp.float32)
    output = hidden + (both[0] + both[1]).astype(jnp.bfloat16).astype(jnp.float32)
    record = (
        normed_one, inverse_one, first, projected, log_total, attended, normed_two, inverse_two,
        second, router, chosen, slot_index, owners, slot_gate, slot_rows, inner_pre, activated, picked,
    )
    return (output.reshape(image_count, length, model_width), record)


def layer_backward(grad_field, record, weights):
    w_qkv, w_proj, w_in, w_out, w_router, ln_gain, ln_bias = weights
    (
        normed_one, inverse_one, first, projected, log_total, attended, normed_two, inverse_two,
        second, router, chosen, slot_index, owners, slot_gate, slot_rows, inner_pre, activated, picked,
    ) = record
    image_count, length, model_width = grad_field.shape
    row_count = image_count * length
    head_count = projected.shape[3]
    score_scale = HD ** (-0.5)
    gain_rows = ln_gain.astype(jnp.float32)
    grad_flat = grad_field.reshape(row_count, model_width)
    padded_grad = jnp.concatenate([grad_flat, jnp.zeros((1, model_width), jnp.float32)], axis=0)
    grad_slots = (jnp.take(padded_grad, owners, axis=0) * slot_gate[:, None]).astype(jnp.bfloat16)
    split = (w_out.shape[0], w_out.shape[3])
    grad_slots = grad_slots.reshape((image_count, EXPERTS, CAP) + split)
    slot_split = slot_rows.reshape((image_count, EXPERTS, CAP) + split)
    grad_w_out = jnp.einsum(
        "becf,becjk->jefk", activated, grad_slots, preferred_element_type=jnp.float32
    )
    grad_act = jnp.einsum("becjk,jefk->becf", grad_slots, w_out, preferred_element_type=jnp.float32)
    grad_inner = (grad_act * gelu_slope(inner_pre)).astype(jnp.bfloat16)
    grad_w_in = jnp.einsum(
        "becjk,becf->jekf", slot_split, grad_inner, preferred_element_type=jnp.float32
    )
    grad_slot_rows = jnp.einsum(
        "becf,jekf->becjk", grad_inner, w_in, preferred_element_type=jnp.float32
    )
    grad_slot_rows = grad_slot_rows.reshape(image_count * EXPERTS * CAP, model_width)
    partial_second = jnp.sum(
        jnp.take(grad_slot_rows, slot_index, axis=0).reshape(row_count, TOPK, model_width), axis=1
    )
    partial_gate = jnp.sum(picked * grad_flat[:, None, :], axis=-1)
    joined = lax.psum(jnp.concatenate([partial_second, partial_gate], axis=1), "mp")
    grad_second, grad_gate = joined[:, :model_width], joined[:, model_width:]
    grad_router = jnp.sum(grad_gate[:, :, None] * chosen, axis=1)
    grad_logits = router * (grad_router - jnp.sum(router * grad_router, axis=-1, keepdims=True))
    grad_logits = grad_logits.astype(jnp.bfloat16)
    grad_w_router = jnp.dot(second.T, grad_logits, preferred_element_type=jnp.float32)
    grad_second = grad_second + jnp.dot(grad_logits, w_router.T, preferred_element_type=jnp.float32)
    grad_from_norm, grad_gain_two, grad_shift_two = norm_backward(
        grad_second, normed_two, inverse_two, gain_rows[1]
    )
    grad_hidden = grad_flat + grad_from_norm
    grad_hidden_low = grad_hidden.astype(jnp.bfloat16)
    grad_hidden_split = grad_hidden_low.reshape((row_count,) + split)
    grad_w_proj = jnp.einsum(
        "rf,rjk->jfk", attended, grad_hidden_split, preferred_element_type=jnp.float32
    )
    grad_attended = jnp.einsum(
        "rjk,jfk->rf", grad_hidden_split, w_proj, preferred_element_type=jnp.float32
    ).astype(jnp.bfloat16)
    grad_attended = grad_attended.reshape(image_count, length, head_count, HD)
    queries = projected[:, :, 0]
    key_rows = projected[:, :, 1]
    value_rows = projected[:, :, 2]
    scores = (
        jnp.einsum("bqhe,bkhe->bhqk", queries, key_rows, preferred_element_type=jnp.float32)
        * score_scale
    )
    probs = jnp.exp(scores - log_total[..., None])
    grad_values = jnp.einsum(
        "bhqk,bqhe->bkhe", probs.astype(jnp.bfloat16), grad_attended,
        preferred_element_type=jnp.float32,
    )
    grad_probs = jnp.einsum(
        "bqhe,bkhe->bhqk", grad_attended, value_rows, preferred_element_type=jnp.float32
    )
    grad_scores = (
        probs * (grad_probs - jnp.sum(probs * grad_probs, axis=-1, keepdims=True))
    ).astype(jnp.bfloat16)
    grad_queries = (
        jnp.einsum("bhqk,bkhe->bqhe", grad_scores, key_rows, preferred_element_type=jnp.float32)
        * score_scale
    )
    grad_keys = (
        jnp.einsum("bhqk,bqhe->bkhe", grad_scores, queries, preferred_element_type=jnp.float32)
        * score_scale
    )
    grad_projected = jnp.stack([grad_queries, grad_keys, grad_values], axis=2).astype(jnp.bfloat16)
    grad_projected = grad_projected.reshape(row_count, 3, head_count * HD)
    grad_w_qkv = jnp.einsum(
        "rd,rcf->dcf", first, grad_projected, preferred_element_type=jnp.float32
    )
    partial_first = jnp.einsum(
        "rcf,dcf->rd", grad_projected, w_qkv, preferred_element_type=jnp.float32
    )
    both = exchange(partial_first.astype(jnp.bfloat16), 2, True, "pair", 2).astype(jnp.float32)
    grad_first = (both[0] + both[1]).astype(jnp.bfloat16).astype(jnp.float32)
    grad_input_norm, grad_gain_one, grad_shift_one = norm_backward(
        grad_first, normed_one, inverse_one, gain_rows[0]
    )
    grad_input = grad_hidden + grad_input_norm
    grads = (
        grad_w_qkv,
        grad_w_proj,
        grad_w_in,
        grad_w_out,
        grad_w_router,
        jnp.stack([grad_gain_one, grad_gain_two]),
        jnp.stack([grad_shift_one, grad_shift_two]),
    )
    return (grad_input.reshape(image_count, length, model_width), grads)


def make_local(n):
    def local(images, routes, w_qkv, w_proj, w_in, w_out, w_router, ln_gain, ln_bias, cotangent):
        shapes = [a.shape for a in (w_qkv, w_proj, w_in, w_out, w_router, ln_gain, ln_bias)]
        weights = gather_weights(w_qkv, w_proj, w_in, w_out, w_router, ln_gain, ln_bias, n)
        field = images.astype(jnp.float32)
        output, record = layer_forward(field, routes[0], weights)
        grad_input, grads = layer_backward(cotangent.astype(jnp.float32), record, weights)
        shards = scatter_grads(grads, n, [(1,) + tuple(s[1:]) for s in shapes])
        return (output, grad_input, *shards)

    return local


def solution(mesh):
    n = mesh.shape["dp"]
    in_specs = (
        P("dp", None, None),
        P(None, "dp", None, None),
        P(None, "dp", None, "mp"),
        P(None, "mp", "dp"),
        P(None, None, "dp", "mp"),
        P(None, None, "mp", "dp"),
        P(None, "dp", None),
        P(None, None, "dp"),
        P(None, None, "dp"),
        P("dp", None, None),
    )
    out_specs = (
        P("dp", None, None),
        P("dp", None, None),
        P(None, "dp", None, "mp"),
        P(None, "mp", "dp"),
        P(None, None, "dp", "mp"),
        P(None, None, "mp", "dp"),
        P(None, "dp", None),
        P(None, None, "dp"),
        P(None, None, "dp"),
    )
    return jax.shard_map(make_local(n), mesh=mesh, in_specs=in_specs, out_specs=out_specs, check_vma=False)
```

```python
import functools

import jax
import jax.numpy as jnp
from jax import lax
from jax.sharding import PartitionSpec as P
from jax.experimental import pallas as pl
from jax.experimental.pallas import tpu as pltpu

MESH = pl.DeviceIdType.MESH
LANES = 128

HD = 64
EXPERTS = 4
TOPK = 2
CAP = 104
EPSILON = 1e-06


def norm_forward(field, gain_row, shift_row):
    mean_value = jnp.mean(field, axis=-1, keepdims=True)
    centered = field - mean_value
    inverse = lax.rsqrt(jnp.mean(centered * centered, axis=-1, keepdims=True) + EPSILON)
    normed = centered * inverse
    return (normed * gain_row + shift_row, normed, inverse)


def norm_backward(grad_out, normed, inverse, gain_row):
    grad_gain = jnp.sum(grad_out * normed, axis=0)
    grad_shift = jnp.sum(grad_out, axis=0)
    scaled = grad_out * gain_row
    grad_in = inverse * (
        scaled
        - jnp.mean(scaled, axis=-1, keepdims=True)
        - normed * jnp.mean(scaled * normed, axis=-1, keepdims=True)
    )
    return (grad_in, grad_gain, grad_shift)


def slot_positions(chosen_ids):
    labels = jnp.arange(EXPERTS, dtype=jnp.int32)
    hit_counts = jnp.sum((chosen_ids[..., None] == labels).astype(jnp.int32), axis=-2)
    before = jnp.cumsum(hit_counts, axis=1) - hit_counts
    picked = chosen_ids[..., None] == labels
    return jnp.sum(jnp.where(picked, before[..., None, :], 0), axis=-1)


def gelu_slope(inner_pre):
    cumulative = 0.5 * (1.0 + jax.scipy.special.erf(inner_pre * 0.7071067811865476))
    density = jnp.exp(-0.5 * inner_pre * inner_pre) * 0.3989422804014327
    return cumulative + inner_pre * density


def group_of(kind):
    def chips():
        dp, mp = lax.axis_index("dp"), lax.axis_index("mp")
        return dp // 2, lambda i: (2 * i + dp % 2, mp)

    def cores():
        dp, mp = lax.axis_index("dp"), lax.axis_index("mp")
        return dp % 2, lambda i: (2 * (dp // 2) + i, mp)

    def whole():
        dp, mp = lax.axis_index("dp"), lax.axis_index("mp")
        return dp, lambda i: (i, mp)

    def pair():
        dp, mp = lax.axis_index("dp"), lax.axis_index("mp")
        return mp, lambda i: (dp, i)

    return {"chips": chips, "cores": cores, "pair": pair, "all": whole}[kind]


def exchange_kernel(m, pieces, gather, kind, x_ref, out_ref, send_sem, recv_sem, local_sem):
    me, device_of = group_of(kind)()
    step = out_ref.shape[1] // pieces
    barrier = pltpu.get_barrier_semaphore()

    def greet(k, carry):
        pl.semaphore_signal(
            barrier, inc=1, device_id=device_of(lax.rem(me + k, m)), device_id_type=MESH
        )
        return carry

    lax.fori_loop(1, m, greet, 0)
    pl.semaphore_wait(barrier, m - 1)
    own = pltpu.make_async_copy(x_ref if gather else x_ref.at[me], out_ref.at[me], local_sem)
    own.start()

    def describe(t):
        k = 1 + t // pieces
        part = pl.ds(pl.multiple_of((t % pieces) * step, step), step)
        peer = lax.rem(me + k, m)
        return pltpu.make_async_remote_copy(
            src_ref=x_ref.at[part] if gather else x_ref.at[peer, part],
            dst_ref=out_ref.at[me, part],
            send_sem=send_sem.at[t],
            recv_sem=recv_sem.at[t],
            device_id=device_of(peer),
            device_id_type=MESH,
        )

    def start(t, carry):
        describe(t).start()
        return carry

    def finish(t, carry):
        describe(t).wait()
        return carry

    count = (m - 1) * pieces
    lax.fori_loop(0, count, start, 0)
    lax.fori_loop(0, count, finish, 0)
    own.wait()


def exchange(x, m, gather, kind, collective_id, pieces=1):
    block = x.shape if gather else x.shape[1:]
    block_bytes = x.dtype.itemsize
    for d in block:
        block_bytes *= d
    count = (m - 1) * pieces
    return pl.pallas_call(
        functools.partial(exchange_kernel, m, pieces, gather, kind),
        out_shape=jax.ShapeDtypeStruct((m,) + tuple(block), x.dtype),
        in_specs=[pl.BlockSpec(memory_space=pl.ANY)],
        out_specs=pl.BlockSpec(memory_space=pl.ANY),
        scratch_shapes=[
            pltpu.SemaphoreType.DMA((count,)),
            pltpu.SemaphoreType.DMA((count,)),
            pltpu.SemaphoreType.DMA(()),
        ],
        compiler_params=pltpu.CompilerParams(collective_id=collective_id, has_side_effects=True),
        cost_estimate=pl.CostEstimate(flops=0, bytes_accessed=2 * m * block_bytes, transcendentals=0),
    )(x)


def relay_gather_kernel(chips, direct, x_ref, out_ref, sa, ra, sb, rb, sf, rf, sp, rp, sl):
    dp, mp = lax.axis_index("dp"), lax.axis_index("mp")
    n = 2 * chips
    core = dp % 2
    other = 1 - core
    chip = dp // 2
    barrier = pltpu.get_barrier_semaphore()

    def greet(k, carry):
        pl.semaphore_signal(
            barrier, inc=1, device_id=(lax.rem(dp + k, n), mp), device_id_type=MESH
        )
        return carry

    lax.fori_loop(1, n, greet, 0)
    pl.semaphore_wait(barrier, n - 1)
    own = pltpu.make_async_copy(x_ref, out_ref.at[dp], sl)
    own.start()

    def remote(src, dst, send, recv, target):
        return pltpu.make_async_remote_copy(
            src_ref=src, dst_ref=dst, send_sem=send, recv_sem=recv,
            device_id=(target, mp), device_id_type=MESH,
        )

    def same(j):
        return remote(x_ref, out_ref.at[dp], sa.at[j], ra.at[j], 2 * lax.rem(chip + j, chips) + core)

    def cross(j):
        return remote(x_ref, out_ref.at[dp], sb.at[j], rb.at[j], 2 * lax.rem(chip + j, chips) + other)

    def relay(j):
        slot = 2 * lax.rem(chip + chips - j, chips) + core
        return remote(out_ref.at[slot], out_ref.at[slot], sf.at[j], rf.at[j], 2 * chip + other)

    mate = remote(x_ref, out_ref.at[dp], sp, rp, 2 * chip + other)
    forwarded = [j for j in range(1, chips) if j not in direct]
    mate.start()
    for j in forwarded:
        same(j).start()
    for j in direct:
        cross(j).start()
    for j in direct:
        same(j).start()
    for j in forwarded:
        same(j).wait_recv()
        relay(j).start()
    for j in direct:
        same(j).wait_recv()
    for j in range(1, chips):
        same(j).wait_send()
    for j in direct:
        cross(j).wait()
    mate.wait()
    for j in forwarded:
        relay(j).wait()
    own.wait()


def relay_gather(x, n, collective_id):
    chips = n // 2
    direct = tuple(j for j in range(1, chips) if j % 4 == 0)
    block_bytes = x.dtype.itemsize
    for d in x.shape:
        block_bytes *= d
    return pl.pallas_call(
        functools.partial(relay_gather_kernel, chips, direct),
        out_shape=jax.ShapeDtypeStruct((n,) + tuple(x.shape), x.dtype),
        in_specs=[pl.BlockSpec(memory_space=pl.ANY)],
        out_specs=pl.BlockSpec(memory_space=pl.ANY),
        scratch_shapes=[pltpu.SemaphoreType.DMA((chips,))] * 6
        + [pltpu.SemaphoreType.DMA(())] * 3,
        compiler_params=pltpu.CompilerParams(collective_id=collective_id, has_side_effects=True),
        cost_estimate=pl.CostEstimate(flops=0, bytes_accessed=2 * n * block_bytes, transcendentals=0),
    )(x)


def relay_reduce_kernel(chips, direct, y_ref, out_same, out_cross, pin, sbuf, ss, rs, sc, rc, sr, rr, sl):
    dp, mp = lax.axis_index("dp"), lax.axis_index("mp")
    n = 2 * chips
    core = dp % 2
    other = 1 - core
    chip = dp // 2
    mate_id = 2 * chip + other
    barrier = pltpu.get_barrier_semaphore()

    def greet(k, carry):
        pl.semaphore_signal(
            barrier, inc=1, device_id=(lax.rem(dp + k, n), mp), device_id_type=MESH
        )
        return carry

    lax.fori_loop(1, n, greet, 0)
    pl.semaphore_wait(barrier, n - 1)
    own = pltpu.make_async_copy(y_ref.at[dp], out_same.at[0], sl)
    own.start()

    def remote(src, dst, send, recv, target):
        return pltpu.make_async_remote_copy(
            src_ref=src, dst_ref=dst, send_sem=send, recv_sem=recv,
            device_id=(target, mp), device_id_type=MESH,
        )

    def target(j, c):
        return 2 * lax.rem(chip + j, chips) + c

    slot_of = {j: i + 1 for i, j in enumerate(direct)}
    forwarded = [j for j in range(1, chips) if j not in direct]

    def same(j):
        src = y_ref.at[target(j, core)] if j in direct else sbuf.at[j]
        return remote(src, out_same.at[j], ss.at[j], rs.at[j], target(j, core))

    def cross(j):
        i = slot_of[j]
        return remote(y_ref.at[target(j, other)], out_cross.at[i], sc.at[i], rc.at[i], target(j, other))

    def relay(j):
        return remote(y_ref.at[target(j, other)], pin.at[j], sr.at[j], rr.at[j], mate_id)

    mate = remote(y_ref.at[mate_id], out_cross.at[0], sc.at[0], rc.at[0], mate_id)
    for j in forwarded:
        relay(j).start()
    mate.start()
    for j in direct:
        cross(j).start()
        same(j).start()
    for j in forwarded:
        relay(j).wait_recv()
        total = y_ref[target(j, core)].astype(jnp.float32) + pin[j].astype(jnp.float32)
        sbuf[j] = total.astype(sbuf.dtype)
        same(j).start()
    for j in forwarded:
        relay(j).wait_send()
    for j in range(1, chips):
        same(j).wait()
    for j in direct:
        cross(j).wait()
    mate.wait()
    own.wait()


def relay_reduce(y, n, collective_id):
    chips = n // 2
    direct = tuple(j for j in range(1, chips) if j % 4 == 0)
    block = tuple(y.shape[1:])
    block_bytes = y.dtype.itemsize
    for d in block:
        block_bytes *= d
    same, cross = pl.pallas_call(
        functools.partial(relay_reduce_kernel, chips, direct),
        out_shape=(
            jax.ShapeDtypeStruct((chips,) + block, y.dtype),
            jax.ShapeDtypeStruct((len(direct) + 1,) + block, y.dtype),
        ),
        in_specs=[pl.BlockSpec(memory_space=pltpu.VMEM)],
        out_specs=(pl.BlockSpec(memory_space=pl.ANY), pl.BlockSpec(memory_space=pl.ANY)),
        scratch_shapes=[pltpu.VMEM((chips,) + block, y.dtype)] * 2
        + [pltpu.SemaphoreType.DMA((chips,))] * 6
        + [pltpu.SemaphoreType.DMA(())],
        compiler_params=pltpu.CompilerParams(collective_id=collective_id, has_side_effects=True),
        cost_estimate=pl.CostEstimate(flops=0, bytes_accessed=3 * n * block_bytes, transcendentals=0),
    )(y)
    return jnp.sum(same.astype(jnp.float32), axis=0) + jnp.sum(cross.astype(jnp.float32), axis=0)


def padded_rows(size, dtype_rows=16):
    rows = -(-size // LANES)
    return -(-rows // dtype_rows) * dtype_rows


def shard_sizes(w_qkv, w_proj, w_in, w_out, w_router, ln_gain, ln_bias):
    return [a.size for a in (w_qkv, w_proj, w_in, w_out, w_router, ln_gain, ln_bias)]


def gather_weights(w_qkv, w_proj, w_in, w_out, w_router, ln_gain, ln_bias, n):
    parts = (w_qkv, w_proj, w_in, w_out, w_router, ln_gain, ln_bias)
    flat = jnp.concatenate([a.reshape(-1) for a in parts])
    total = flat.shape[0]
    rows = padded_rows(total)
    flat = jnp.pad(flat, (0, rows * LANES - total)).reshape(rows, LANES)
    full = relay_gather(flat, n, 0).reshape(n, rows * LANES)
    pieces = []
    start = 0
    for a in parts:
        pieces.append(full[:, start:start + a.size].reshape((n,) + a.shape[1:]))
        start += a.size
    q, p, i, o, r, g, b = pieces
    gq = q.reshape((-1,) + w_qkv.shape[2:])
    gr = r.reshape((-1,) + w_router.shape[2:])
    gg = g.transpose(1, 0, 2).reshape(ln_gain.shape[1], -1)
    gb = b.transpose(1, 0, 2).reshape(ln_bias.shape[1], -1)
    return (gq, p, i, o, gr, gg, gb)


def scatter_grads(grads, n, shapes):
    gq, gp, gi, go, gr, gg, gb = grads
    rows = [
        gq.reshape(n, -1),
        gp.reshape(n, -1),
        gi.reshape(n, -1),
        go.reshape(n, -1),
        gr.reshape(n, -1),
        gg.reshape(gg.shape[0], n, -1).transpose(1, 0, 2).reshape(n, -1),
        gb.reshape(gb.shape[0], n, -1).transpose(1, 0, 2).reshape(n, -1),
    ]
    packed = jnp.concatenate(rows, axis=1)
    total = packed.shape[1]
    count = padded_rows(total)
    packed = jnp.pad(packed, ((0, 0), (0, count * LANES - total))).reshape(n, count, LANES)
    mine = relay_reduce(packed.astype(jnp.bfloat16), n, 1).reshape(-1)
    outs = []
    start = 0
    for shape in shapes:
        size = 1
        for d in shape:
            size *= d
        outs.append(mine[start:start + size].reshape(shape))
        start += size
    return outs


def layer_forward(field, chosen_ids, weights):
    w_qkv, w_proj, w_in, w_out, w_router, ln_gain, ln_bias = weights
    image_count, length, model_width = field.shape
    row_count = image_count * length
    head_count = w_qkv.shape[2] // HD
    score_scale = HD ** (-0.5)
    gain_rows = ln_gain.astype(jnp.float32)
    shift_rows = ln_bias.astype(jnp.float32)
    flat = field.reshape(row_count, model_width)
    first, normed_one, inverse_one = norm_forward(flat, gain_rows[0], shift_rows[0])
    first = first.astype(jnp.bfloat16)
    projected = jnp.einsum("rd,dcf->rcf", first, w_qkv, preferred_element_type=jnp.float32).astype(
        jnp.bfloat16
    )
    projected = projected.reshape(image_count, length, 3, head_count, HD)
    queries = projected[:, :, 0]
    key_rows = projected[:, :, 1]
    value_rows = projected[:, :, 2]
    scores = (
        jnp.einsum("bqhe,bkhe->bhqk", queries, key_rows, preferred_element_type=jnp.float32)
        * score_scale
    )
    log_total = jax.nn.logsumexp(scores, axis=-1)
    attn_weights = jnp.exp(scores - log_total[..., None]).astype(jnp.bfloat16)
    attended = jnp.einsum(
        "bhqk,bkhe->bqhe", attn_weights, value_rows, preferred_element_type=jnp.float32
    )
    attended = attended.astype(jnp.bfloat16).reshape(row_count, head_count * HD)
    partial_attn = jnp.einsum(
        "rf,jfk->rjk", attended, w_proj, preferred_element_type=jnp.float32
    ).reshape(row_count, model_width)
    hidden = flat + lax.psum(partial_attn, "mp")
    second, normed_two, inverse_two = norm_forward(hidden, gain_rows[1], shift_rows[1])
    second = second.astype(jnp.bfloat16)
    logits = jnp.dot(second, w_router, preferred_element_type=jnp.float32)
    router = jax.nn.softmax(logits, axis=-1)
    labels = jnp.arange(EXPERTS, dtype=jnp.int32)
    ids_flat = chosen_ids.reshape(row_count, TOPK)
    chosen = (ids_flat[:, :, None] == labels).astype(jnp.float32)
    gate_values = jnp.sum(router[:, None, :] * chosen, axis=-1)
    per_image = EXPERTS * CAP
    image_base = (jnp.arange(image_count, dtype=jnp.int32) * per_image)[:, None, None]
    slot_index = (chosen_ids * CAP + slot_positions(chosen_ids) + image_base).reshape(-1)
    owners = (
        jnp.full((image_count * per_image,), row_count, jnp.int32)
        .at[slot_index]
        .set(jnp.repeat(jnp.arange(row_count, dtype=jnp.int32), TOPK))
    )
    slot_gate = (
        jnp.zeros((image_count * per_image,), jnp.float32).at[slot_index].set(gate_values.reshape(-1))
    )
    padded = jnp.concatenate([second, jnp.zeros((1, model_width), jnp.bfloat16)], axis=0)
    slot_rows = jnp.take(padded, owners, axis=0).reshape(image_count, EXPERTS, CAP, model_width)
    slot_split = slot_rows.reshape(slot_rows.shape[:3] + w_in.shape[:1] + w_in.shape[2:3])
    inner_pre = jnp.einsum("becjk,jekf->becf", slot_split, w_in, preferred_element_type=jnp.float32)
    activated = jax.nn.gelu(inner_pre, approximate=False).astype(jnp.bfloat16)
    produced = jnp.einsum("becf,jefk->becjk", activated, w_out, preferred_element_type=jnp.float32)
    produced = produced.reshape(image_count * per_image, model_width)
    picked = jnp.take(produced, slot_index, axis=0).reshape(row_count, TOPK, model_width)
    partial_moe = jnp.sum(gate_values[:, :, None] * picked, axis=1)
    halves = partial_moe.astype(jnp.bfloat16).reshape((2, -1) + partial_moe.shape[1:])
    both = exchange(halves, 2, True, "pair", 3, pieces=2).astype(jnp.float32)
    both = both.reshape((2,) + partial_moe.shape)
    output = hidden + (both[0] + both[1]).astype(jnp.bfloat16).astype(jnp.float32)
    record = (
        normed_one, inverse_one, first, projected, log_total, attended, normed_two, inverse_two,
        second, router, chosen, slot_index, owners, slot_gate, slot_rows, inner_pre, activated, picked,
    )
    return (output.reshape(image_count, length, model_width), record)


def layer_backward(grad_field, record, weights):
    w_qkv, w_proj, w_in, w_out, w_router, ln_gain, ln_bias = weights
    (
        normed_one, inverse_one, first, projected, log_total, attended, normed_two, inverse_two,
        second, router, chosen, slot_index, owners, slot_gate, slot_rows, inner_pre, activated, picked,
    ) = record
    image_count, length, model_width = grad_field.shape
    row_count = image_count * length
    head_count = projected.shape[3]
    score_scale = HD ** (-0.5)
    gain_rows = ln_gain.astype(jnp.float32)
    grad_flat = grad_field.reshape(row_count, model_width)
    padded_grad = jnp.concatenate([grad_flat, jnp.zeros((1, model_width), jnp.float32)], axis=0)
    grad_slots = (jnp.take(padded_grad, owners, axis=0) * slot_gate[:, None]).astype(jnp.bfloat16)
    split = (w_out.shape[0], w_out.shape[3])
    grad_slots = grad_slots.reshape((image_count, EXPERTS, CAP) + split)
    slot_split = slot_rows.reshape((image_count, EXPERTS, CAP) + split)
    grad_w_out = jnp.einsum(
        "becf,becjk->jefk", activated, grad_slots, preferred_element_type=jnp.float32
    )
    grad_act = jnp.einsum("becjk,jefk->becf", grad_slots, w_out, preferred_element_type=jnp.float32)
    grad_inner = (grad_act * gelu_slope(inner_pre)).astype(jnp.bfloat16)
    grad_w_in = jnp.einsum(
        "becjk,becf->jekf", slot_split, grad_inner, preferred_element_type=jnp.float32
    )
    grad_slot_rows = jnp.einsum(
        "becf,jekf->becjk", grad_inner, w_in, preferred_element_type=jnp.float32
    )
    grad_slot_rows = grad_slot_rows.reshape(image_count * EXPERTS * CAP, model_width)
    partial_second = jnp.sum(
        jnp.take(grad_slot_rows, slot_index, axis=0).reshape(row_count, TOPK, model_width), axis=1
    )
    partial_gate = jnp.sum(picked * grad_flat[:, None, :], axis=-1)
    joined = lax.psum(jnp.concatenate([partial_second, partial_gate], axis=1), "mp")
    grad_second, grad_gate = joined[:, :model_width], joined[:, model_width:]
    grad_router = jnp.sum(grad_gate[:, :, None] * chosen, axis=1)
    grad_logits = router * (grad_router - jnp.sum(router * grad_router, axis=-1, keepdims=True))
    grad_logits = grad_logits.astype(jnp.bfloat16)
    grad_w_router = jnp.dot(second.T, grad_logits, preferred_element_type=jnp.float32)
    grad_second = grad_second + jnp.dot(grad_logits, w_router.T, preferred_element_type=jnp.float32)
    grad_from_norm, grad_gain_two, grad_shift_two = norm_backward(
        grad_second, normed_two, inverse_two, gain_rows[1]
    )
    grad_hidden = grad_flat + grad_from_norm
    grad_hidden_low = grad_hidden.astype(jnp.bfloat16)
    grad_hidden_split = grad_hidden_low.reshape((row_count,) + split)
    grad_w_proj = jnp.einsum(
        "rf,rjk->jfk", attended, grad_hidden_split, preferred_element_type=jnp.float32
    )
    grad_attended = jnp.einsum(
        "rjk,jfk->rf", grad_hidden_split, w_proj, preferred_element_type=jnp.float32
    ).astype(jnp.bfloat16)
    grad_attended = grad_attended.reshape(image_count, length, head_count, HD)
    queries = projected[:, :, 0]
    key_rows = projected[:, :, 1]
    value_rows = projected[:, :, 2]
    scores = (
        jnp.einsum("bqhe,bkhe->bhqk", queries, key_rows, preferred_element_type=jnp.float32)
        * score_scale
    )
    probs = jnp.exp(scores - log_total[..., None])
    grad_values = jnp.einsum(
        "bhqk,bqhe->bkhe", probs.astype(jnp.bfloat16), grad_attended,
        preferred_element_type=jnp.float32,
    )
    grad_probs = jnp.einsum(
        "bqhe,bkhe->bhqk", grad_attended, value_rows, preferred_element_type=jnp.float32
    )
    grad_scores = (
        probs * (grad_probs - jnp.sum(probs * grad_probs, axis=-1, keepdims=True))
    ).astype(jnp.bfloat16)
    grad_queries = (
        jnp.einsum("bhqk,bkhe->bqhe", grad_scores, key_rows, preferred_element_type=jnp.float32)
        * score_scale
    )
    grad_keys = (
        jnp.einsum("bhqk,bqhe->bkhe", grad_scores, queries, preferred_element_type=jnp.float32)
        * score_scale
    )
    grad_projected = jnp.stack([grad_queries, grad_keys, grad_values], axis=2).astype(jnp.bfloat16)
    grad_projected = grad_projected.reshape(row_count, 3, head_count * HD)
    grad_w_qkv = jnp.einsum(
        "rd,rcf->dcf", first, grad_projected, preferred_element_type=jnp.float32
    )
    partial_first = jnp.einsum(
        "rcf,dcf->rd", grad_projected, w_qkv, preferred_element_type=jnp.float32
    )
    halves = partial_first.astype(jnp.bfloat16).reshape((2, -1) + partial_first.shape[1:])
    both = exchange(halves, 2, True, "pair", 2, pieces=2).astype(jnp.float32)
    both = both.reshape((2,) + partial_first.shape)
    grad_first = (both[0] + both[1]).astype(jnp.bfloat16).astype(jnp.float32)
    grad_input_norm, grad_gain_one, grad_shift_one = norm_backward(
        grad_first, normed_one, inverse_one, gain_rows[0]
    )
    grad_input = grad_hidden + grad_input_norm
    grads = (
        grad_w_qkv,
        grad_w_proj,
        grad_w_in,
        grad_w_out,
        grad_w_router,
        jnp.stack([grad_gain_one, grad_gain_two]),
        jnp.stack([grad_shift_one, grad_shift_two]),
    )
    return (grad_input.reshape(image_count, length, model_width), grads)


def make_local(n):
    def local(images, routes, w_qkv, w_proj, w_in, w_out, w_router, ln_gain, ln_bias, cotangent):
        shapes = [a.shape for a in (w_qkv, w_proj, w_in, w_out, w_router, ln_gain, ln_bias)]
        weights = gather_weights(w_qkv, w_proj, w_in, w_out, w_router, ln_gain, ln_bias, n)
        field = images.astype(jnp.float32)
        output, record = layer_forward(field, routes[0], weights)
        grad_input, grads = layer_backward(cotangent.astype(jnp.float32), record, weights)
        shards = scatter_grads(grads, n, [(1,) + tuple(s[1:]) for s in shapes])
        return (output, grad_input, *shards)

    return local


def solution(mesh):
    n = mesh.shape["dp"]
    in_specs = (
        P("dp", None, None),
        P(None, "dp", None, None),
        P(None, "dp", None, "mp"),
        P(None, "mp", "dp"),
        P(None, None, "dp", "mp"),
        P(None, None, "mp", "dp"),
        P(None, "dp", None),
        P(None, None, "dp"),
        P(None, None, "dp"),
        P("dp", None, None),
    )
    out_specs = (
        P("dp", None, None),
        P("dp", None, None),
        P(None, "dp", None, "mp"),
        P(None, "mp", "dp"),
        P(None, None, "dp", "mp"),
        P(None, None, "mp", "dp"),
        P(None, "dp", None),
        P(None, None, "dp"),
        P(None, None, "dp"),
    )
    return jax.shard_map(make_local(n), mesh=mesh, in_specs=in_specs, out_specs=out_specs, check_vma=False)
```

```python
import functools

import jax
import jax.numpy as jnp
from jax import lax
from jax.sharding import PartitionSpec as P
from jax.experimental import pallas as pl
from jax.experimental.pallas import tpu as pltpu

MESH = pl.DeviceIdType.MESH
LANES = 128

HD = 64
EXPERTS = 4
TOPK = 2
CAP = 104
EPSILON = 1e-06


def norm_forward(field, gain_row, shift_row):
    mean_value = jnp.mean(field, axis=-1, keepdims=True)
    centered = field - mean_value
    inverse = lax.rsqrt(jnp.mean(centered * centered, axis=-1, keepdims=True) + EPSILON)
    normed = centered * inverse
    return (normed * gain_row + shift_row, normed, inverse)


def norm_backward(grad_out, normed, inverse, gain_row):
    grad_gain = jnp.sum(grad_out * normed, axis=0)
    grad_shift = jnp.sum(grad_out, axis=0)
    scaled = grad_out * gain_row
    grad_in = inverse * (
        scaled
        - jnp.mean(scaled, axis=-1, keepdims=True)
        - normed * jnp.mean(scaled * normed, axis=-1, keepdims=True)
    )
    return (grad_in, grad_gain, grad_shift)


def slot_positions(chosen_ids):
    labels = jnp.arange(EXPERTS, dtype=jnp.int32)
    hit_counts = jnp.sum((chosen_ids[..., None] == labels).astype(jnp.int32), axis=-2)
    before = jnp.cumsum(hit_counts, axis=1) - hit_counts
    picked = chosen_ids[..., None] == labels
    return jnp.sum(jnp.where(picked, before[..., None, :], 0), axis=-1)


def gelu_slope(inner_pre):
    cumulative = 0.5 * (1.0 + jax.scipy.special.erf(inner_pre * 0.7071067811865476))
    density = jnp.exp(-0.5 * inner_pre * inner_pre) * 0.3989422804014327
    return cumulative + inner_pre * density


def group_of(kind):
    def chips():
        dp, mp = lax.axis_index("dp"), lax.axis_index("mp")
        return dp // 2, lambda i: (2 * i + dp % 2, mp)

    def cores():
        dp, mp = lax.axis_index("dp"), lax.axis_index("mp")
        return dp % 2, lambda i: (2 * (dp // 2) + i, mp)

    def whole():
        dp, mp = lax.axis_index("dp"), lax.axis_index("mp")
        return dp, lambda i: (i, mp)

    def pair():
        dp, mp = lax.axis_index("dp"), lax.axis_index("mp")
        return mp, lambda i: (dp, i)

    return {"chips": chips, "cores": cores, "pair": pair, "all": whole}[kind]


def exchange_kernel(m, pieces, gather, kind, x_ref, out_ref, send_sem, recv_sem, local_sem):
    me, device_of = group_of(kind)()
    step = out_ref.shape[1] // pieces
    barrier = pltpu.get_barrier_semaphore()

    def greet(k, carry):
        pl.semaphore_signal(
            barrier, inc=1, device_id=device_of(lax.rem(me + k, m)), device_id_type=MESH
        )
        return carry

    lax.fori_loop(1, m, greet, 0)
    pl.semaphore_wait(barrier, m - 1)
    own = pltpu.make_async_copy(x_ref if gather else x_ref.at[me], out_ref.at[me], local_sem)
    own.start()

    def describe(t):
        k = 1 + t // pieces
        part = pl.ds(pl.multiple_of((t % pieces) * step, step), step)
        peer = lax.rem(me + k, m)
        return pltpu.make_async_remote_copy(
            src_ref=x_ref.at[part] if gather else x_ref.at[peer, part],
            dst_ref=out_ref.at[me, part],
            send_sem=send_sem.at[t],
            recv_sem=recv_sem.at[t],
            device_id=device_of(peer),
            device_id_type=MESH,
        )

    def start(t, carry):
        describe(t).start()
        return carry

    def finish(t, carry):
        describe(t).wait()
        return carry

    count = (m - 1) * pieces
    lax.fori_loop(0, count, start, 0)
    lax.fori_loop(0, count, finish, 0)
    own.wait()


def exchange(x, m, gather, kind, collective_id, pieces=1):
    block = x.shape if gather else x.shape[1:]
    block_bytes = x.dtype.itemsize
    for d in block:
        block_bytes *= d
    count = (m - 1) * pieces
    return pl.pallas_call(
        functools.partial(exchange_kernel, m, pieces, gather, kind),
        out_shape=jax.ShapeDtypeStruct((m,) + tuple(block), x.dtype),
        in_specs=[pl.BlockSpec(memory_space=pl.ANY)],
        out_specs=pl.BlockSpec(memory_space=pl.ANY),
        scratch_shapes=[
            pltpu.SemaphoreType.DMA((count,)),
            pltpu.SemaphoreType.DMA((count,)),
            pltpu.SemaphoreType.DMA(()),
        ],
        compiler_params=pltpu.CompilerParams(collective_id=collective_id, has_side_effects=True),
        cost_estimate=pl.CostEstimate(flops=0, bytes_accessed=2 * m * block_bytes, transcendentals=0),
    )(x)


def relay_gather_kernel(chips, direct, x_ref, out_ref, sa, ra, sb, rb, sf, rf, sp, rp, sl):
    dp, mp = lax.axis_index("dp"), lax.axis_index("mp")
    n = 2 * chips
    core = dp % 2
    other = 1 - core
    chip = dp // 2
    barrier = pltpu.get_barrier_semaphore()

    def greet(k, carry):
        pl.semaphore_signal(
            barrier, inc=1, device_id=(lax.rem(dp + k, n), mp), device_id_type=MESH
        )
        return carry

    lax.fori_loop(1, n, greet, 0)
    pl.semaphore_wait(barrier, n - 1)
    own = pltpu.make_async_copy(x_ref, out_ref.at[dp], sl)
    own.start()

    def remote(src, dst, send, recv, target):
        return pltpu.make_async_remote_copy(
            src_ref=src, dst_ref=dst, send_sem=send, recv_sem=recv,
            device_id=(target, mp), device_id_type=MESH,
        )

    def same(j):
        return remote(x_ref, out_ref.at[dp], sa.at[j], ra.at[j], 2 * lax.rem(chip + j, chips) + core)

    def cross(j):
        return remote(x_ref, out_ref.at[dp], sb.at[j], rb.at[j], 2 * lax.rem(chip + j, chips) + other)

    def relay(j):
        slot = 2 * lax.rem(chip + chips - j, chips) + core
        return remote(out_ref.at[slot], out_ref.at[slot], sf.at[j], rf.at[j], 2 * chip + other)

    mate = remote(x_ref, out_ref.at[dp], sp, rp, 2 * chip + other)
    forwarded = [j for j in range(1, chips) if j not in direct]
    mate.start()
    for j in forwarded:
        same(j).start()
    for j in direct:
        cross(j).start()
    for j in direct:
        same(j).start()
    for j in forwarded:
        same(j).wait_recv()
        relay(j).start()
    for j in direct:
        same(j).wait_recv()
    for j in range(1, chips):
        same(j).wait_send()
    for j in direct:
        cross(j).wait()
    mate.wait()
    for j in forwarded:
        relay(j).wait()
    own.wait()


def relay_gather(x, n, collective_id):
    chips = n // 2
    direct = tuple(j for j in range(1, chips) if j % 4 == 0)
    block_bytes = x.dtype.itemsize
    for d in x.shape:
        block_bytes *= d
    return pl.pallas_call(
        functools.partial(relay_gather_kernel, chips, direct),
        out_shape=jax.ShapeDtypeStruct((n,) + tuple(x.shape), x.dtype),
        in_specs=[pl.BlockSpec(memory_space=pl.ANY)],
        out_specs=pl.BlockSpec(memory_space=pl.ANY),
        scratch_shapes=[pltpu.SemaphoreType.DMA((chips,))] * 6
        + [pltpu.SemaphoreType.DMA(())] * 3,
        compiler_params=pltpu.CompilerParams(collective_id=collective_id, has_side_effects=True),
        cost_estimate=pl.CostEstimate(flops=0, bytes_accessed=2 * n * block_bytes, transcendentals=0),
    )(x)


def relay_reduce_kernel(chips, direct, y_ref, out_same, out_cross, pin, sbuf, ss, rs, sc, rc, sr, rr, sl):
    dp, mp = lax.axis_index("dp"), lax.axis_index("mp")
    n = 2 * chips
    core = dp % 2
    other = 1 - core
    chip = dp // 2
    mate_id = 2 * chip + other
    barrier = pltpu.get_barrier_semaphore()

    def greet(k, carry):
        pl.semaphore_signal(
            barrier, inc=1, device_id=(lax.rem(dp + k, n), mp), device_id_type=MESH
        )
        return carry

    lax.fori_loop(1, n, greet, 0)
    pl.semaphore_wait(barrier, n - 1)
    own = pltpu.make_async_copy(y_ref.at[dp], out_same.at[0], sl)
    own.start()

    def remote(src, dst, send, recv, target):
        return pltpu.make_async_remote_copy(
            src_ref=src, dst_ref=dst, send_sem=send, recv_sem=recv,
            device_id=(target, mp), device_id_type=MESH,
        )

    def target(j, c):
        return 2 * lax.rem(chip + j, chips) + c

    slot_of = {j: i + 1 for i, j in enumerate(direct)}
    forwarded = [j for j in range(1, chips) if j not in direct]

    def same(j):
        src = y_ref.at[target(j, core)] if j in direct else sbuf.at[j]
        return remote(src, out_same.at[j], ss.at[j], rs.at[j], target(j, core))

    def cross(j):
        i = slot_of[j]
        return remote(y_ref.at[target(j, other)], out_cross.at[i], sc.at[i], rc.at[i], target(j, other))

    def relay(j):
        return remote(y_ref.at[target(j, other)], pin.at[j], sr.at[j], rr.at[j], mate_id)

    mate = remote(y_ref.at[mate_id], out_cross.at[0], sc.at[0], rc.at[0], mate_id)
    for j in forwarded:
        relay(j).start()
    mate.start()
    for j in direct:
        cross(j).start()
        same(j).start()
    for j in forwarded:
        relay(j).wait_recv()
        total = y_ref[target(j, core)].astype(jnp.float32) + pin[j].astype(jnp.float32)
        sbuf[j] = total.astype(sbuf.dtype)
        same(j).start()
    for j in forwarded:
        relay(j).wait_send()
    for j in range(1, chips):
        same(j).wait()
    for j in direct:
        cross(j).wait()
    mate.wait()
    own.wait()


def relay_reduce(y, n, collective_id):
    chips = n // 2
    direct = tuple(j for j in range(1, chips) if j % 4 == 0)
    block = tuple(y.shape[1:])
    block_bytes = y.dtype.itemsize
    for d in block:
        block_bytes *= d
    same, cross = pl.pallas_call(
        functools.partial(relay_reduce_kernel, chips, direct),
        out_shape=(
            jax.ShapeDtypeStruct((chips,) + block, y.dtype),
            jax.ShapeDtypeStruct((len(direct) + 1,) + block, y.dtype),
        ),
        in_specs=[pl.BlockSpec(memory_space=pltpu.VMEM)],
        out_specs=(pl.BlockSpec(memory_space=pl.ANY), pl.BlockSpec(memory_space=pl.ANY)),
        scratch_shapes=[pltpu.VMEM((chips,) + block, y.dtype)] * 2
        + [pltpu.SemaphoreType.DMA((chips,))] * 6
        + [pltpu.SemaphoreType.DMA(())],
        compiler_params=pltpu.CompilerParams(collective_id=collective_id, has_side_effects=True),
        cost_estimate=pl.CostEstimate(flops=0, bytes_accessed=3 * n * block_bytes, transcendentals=0),
    )(y)
    return jnp.sum(same.astype(jnp.float32), axis=0) + jnp.sum(cross.astype(jnp.float32), axis=0)


def padded_rows(size, dtype_rows=16):
    rows = -(-size // LANES)
    return -(-rows // dtype_rows) * dtype_rows


def shard_sizes(w_qkv, w_proj, w_in, w_out, w_router, ln_gain, ln_bias):
    return [a.size for a in (w_qkv, w_proj, w_in, w_out, w_router, ln_gain, ln_bias)]


def gather_weights(w_qkv, w_proj, w_in, w_out, w_router, ln_gain, ln_bias, n):
    parts = (w_qkv, w_proj, w_in, w_out, w_router, ln_gain, ln_bias)
    flat = jnp.concatenate([a.reshape(-1) for a in parts])
    total = flat.shape[0]
    rows = padded_rows(total)
    flat = jnp.pad(flat, (0, rows * LANES - total)).reshape(rows, LANES)
    full = relay_gather(flat, n, 0).reshape(n, rows * LANES)
    pieces = []
    start = 0
    for a in parts:
        pieces.append(full[:, start:start + a.size].reshape((n,) + a.shape[1:]))
        start += a.size
    q, p, i, o, r, g, b = pieces
    gq = q.reshape((-1,) + w_qkv.shape[2:])
    gr = r.reshape((-1,) + w_router.shape[2:])
    gg = g.transpose(1, 0, 2).reshape(ln_gain.shape[1], -1)
    gb = b.transpose(1, 0, 2).reshape(ln_bias.shape[1], -1)
    return (gq, p, i, o, gr, gg, gb)


def scatter_grads(grads, n, shapes):
    gq, gp, gi, go, gr, gg, gb = grads
    rows = [
        gq.reshape(n, -1),
        gp.reshape(n, -1),
        gi.reshape(n, -1),
        go.reshape(n, -1),
        gr.reshape(n, -1),
        gg.reshape(gg.shape[0], n, -1).transpose(1, 0, 2).reshape(n, -1),
        gb.reshape(gb.shape[0], n, -1).transpose(1, 0, 2).reshape(n, -1),
    ]
    packed = jnp.concatenate(rows, axis=1)
    total = packed.shape[1]
    count = padded_rows(total)
    packed = jnp.pad(packed, ((0, 0), (0, count * LANES - total))).reshape(n, count, LANES)
    mine = relay_reduce(packed.astype(jnp.bfloat16), n, 1).reshape(-1)
    outs = []
    start = 0
    for shape in shapes:
        size = 1
        for d in shape:
            size *= d
        outs.append(mine[start:start + size].reshape(shape))
        start += size
    return outs


def layer_forward(field, chosen_ids, weights):
    w_qkv, w_proj, w_in, w_out, w_router, ln_gain, ln_bias = weights
    image_count, length, model_width = field.shape
    row_count = image_count * length
    head_count = w_qkv.shape[2] // HD
    score_scale = HD ** (-0.5)
    gain_rows = ln_gain.astype(jnp.float32)
    shift_rows = ln_bias.astype(jnp.float32)
    flat = field.reshape(row_count, model_width)
    first, normed_one, inverse_one = norm_forward(flat, gain_rows[0], shift_rows[0])
    first = first.astype(jnp.bfloat16)
    projected = jnp.einsum("rd,dcf->rcf", first, w_qkv, preferred_element_type=jnp.float32).astype(
        jnp.bfloat16
    )
    projected = projected.reshape(image_count, length, 3, head_count, HD)
    queries = projected[:, :, 0]
    key_rows = projected[:, :, 1]
    value_rows = projected[:, :, 2]
    scores = (
        jnp.einsum("bqhe,bkhe->bhqk", queries, key_rows, preferred_element_type=jnp.float32)
        * score_scale
    )
    log_total = jax.nn.logsumexp(scores, axis=-1)
    attn_weights = jnp.exp(scores - log_total[..., None]).astype(jnp.bfloat16)
    attended = jnp.einsum(
        "bhqk,bkhe->bqhe", attn_weights, value_rows, preferred_element_type=jnp.float32
    )
    attended = attended.astype(jnp.bfloat16).reshape(row_count, head_count * HD)
    partial_attn = jnp.einsum(
        "rf,jfk->rjk", attended, w_proj, preferred_element_type=jnp.float32
    ).reshape(row_count, model_width)
    hidden = flat + lax.psum(partial_attn, "mp")
    second, normed_two, inverse_two = norm_forward(hidden, gain_rows[1], shift_rows[1])
    second = second.astype(jnp.bfloat16)
    logits = jnp.dot(second, w_router, preferred_element_type=jnp.float32)
    router = jax.nn.softmax(logits, axis=-1)
    labels = jnp.arange(EXPERTS, dtype=jnp.int32)
    ids_flat = chosen_ids.reshape(row_count, TOPK)
    chosen = (ids_flat[:, :, None] == labels).astype(jnp.float32)
    gate_values = jnp.sum(router[:, None, :] * chosen, axis=-1)
    per_image = EXPERTS * CAP
    image_base = (jnp.arange(image_count, dtype=jnp.int32) * per_image)[:, None, None]
    slot_index = (chosen_ids * CAP + slot_positions(chosen_ids) + image_base).reshape(-1)
    owners = (
        jnp.full((image_count * per_image,), row_count, jnp.int32)
        .at[slot_index]
        .set(jnp.repeat(jnp.arange(row_count, dtype=jnp.int32), TOPK))
    )
    slot_gate = (
        jnp.zeros((image_count * per_image,), jnp.float32).at[slot_index].set(gate_values.reshape(-1))
    )
    padded = jnp.concatenate([second, jnp.zeros((1, model_width), jnp.bfloat16)], axis=0)
    slot_rows = jnp.take(padded, owners, axis=0).reshape(image_count, EXPERTS, CAP, model_width)
    slot_split = slot_rows.reshape(slot_rows.shape[:3] + w_in.shape[:1] + w_in.shape[2:3])
    inner_pre = jnp.einsum("becjk,jekf->becf", slot_split, w_in, preferred_element_type=jnp.float32)
    activated = jax.nn.gelu(inner_pre, approximate=False).astype(jnp.bfloat16)
    produced = jnp.einsum("becf,jefk->becjk", activated, w_out, preferred_element_type=jnp.float32)
    produced = produced.reshape(image_count * per_image, model_width)
    picked = jnp.take(produced, slot_index, axis=0).reshape(row_count, TOPK, model_width)
    partial_moe = jnp.sum(gate_values[:, :, None] * picked, axis=1)
    halves = partial_moe.astype(jnp.bfloat16).reshape((6, -1, LANES))
    both = exchange(halves, 2, True, "pair", 3, pieces=6).astype(jnp.float32)
    both = both.reshape((2,) + partial_moe.shape)
    output = hidden + (both[0] + both[1]).astype(jnp.bfloat16).astype(jnp.float32)
    record = (
        normed_one, inverse_one, first, projected, log_total, attended, normed_two, inverse_two,
        second, router, chosen, slot_index, owners, slot_gate, slot_rows, inner_pre, activated, picked,
    )
    return (output.reshape(image_count, length, model_width), record)


def layer_backward(grad_field, record, weights):
    w_qkv, w_proj, w_in, w_out, w_router, ln_gain, ln_bias = weights
    (
        normed_one, inverse_one, first, projected, log_total, attended, normed_two, inverse_two,
        second, router, chosen, slot_index, owners, slot_gate, slot_rows, inner_pre, activated, picked,
    ) = record
    image_count, length, model_width = grad_field.shape
    row_count = image_count * length
    head_count = projected.shape[3]
    score_scale = HD ** (-0.5)
    gain_rows = ln_gain.astype(jnp.float32)
    grad_flat = grad_field.reshape(row_count, model_width)
    padded_grad = jnp.concatenate([grad_flat, jnp.zeros((1, model_width), jnp.float32)], axis=0)
    grad_slots = (jnp.take(padded_grad, owners, axis=0) * slot_gate[:, None]).astype(jnp.bfloat16)
    split = (w_out.shape[0], w_out.shape[3])
    grad_slots = grad_slots.reshape((image_count, EXPERTS, CAP) + split)
    slot_split = slot_rows.reshape((image_count, EXPERTS, CAP) + split)
    grad_w_out = jnp.einsum(
        "becf,becjk->jefk", activated, grad_slots, preferred_element_type=jnp.float32
    )
    grad_act = jnp.einsum("becjk,jefk->becf", grad_slots, w_out, preferred_element_type=jnp.float32)
    grad_inner = (grad_act * gelu_slope(inner_pre)).astype(jnp.bfloat16)
    grad_w_in = jnp.einsum(
        "becjk,becf->jekf", slot_split, grad_inner, preferred_element_type=jnp.float32
    )
    grad_slot_rows = jnp.einsum(
        "becf,jekf->becjk", grad_inner, w_in, preferred_element_type=jnp.float32
    )
    grad_slot_rows = grad_slot_rows.reshape(image_count * EXPERTS * CAP, model_width)
    partial_second = jnp.sum(
        jnp.take(grad_slot_rows, slot_index, axis=0).reshape(row_count, TOPK, model_width), axis=1
    )
    partial_gate = jnp.sum(picked * grad_flat[:, None, :], axis=-1)
    joined = lax.psum(jnp.concatenate([partial_second, partial_gate], axis=1), "mp")
    grad_second, grad_gate = joined[:, :model_width], joined[:, model_width:]
    grad_router = jnp.sum(grad_gate[:, :, None] * chosen, axis=1)
    grad_logits = router * (grad_router - jnp.sum(router * grad_router, axis=-1, keepdims=True))
    grad_logits = grad_logits.astype(jnp.bfloat16)
    grad_w_router = jnp.dot(second.T, grad_logits, preferred_element_type=jnp.float32)
    grad_second = grad_second + jnp.dot(grad_logits, w_router.T, preferred_element_type=jnp.float32)
    grad_from_norm, grad_gain_two, grad_shift_two = norm_backward(
        grad_second, normed_two, inverse_two, gain_rows[1]
    )
    grad_hidden = grad_flat + grad_from_norm
    grad_hidden_low = grad_hidden.astype(jnp.bfloat16)
    grad_hidden_split = grad_hidden_low.reshape((row_count,) + split)
    grad_w_proj = jnp.einsum(
        "rf,rjk->jfk", attended, grad_hidden_split, preferred_element_type=jnp.float32
    )
    grad_attended = jnp.einsum(
        "rjk,jfk->rf", grad_hidden_split, w_proj, preferred_element_type=jnp.float32
    ).astype(jnp.bfloat16)
    grad_attended = grad_attended.reshape(image_count, length, head_count, HD)
    queries = projected[:, :, 0]
    key_rows = projected[:, :, 1]
    value_rows = projected[:, :, 2]
    scores = (
        jnp.einsum("bqhe,bkhe->bhqk", queries, key_rows, preferred_element_type=jnp.float32)
        * score_scale
    )
    probs = jnp.exp(scores - log_total[..., None])
    grad_values = jnp.einsum(
        "bhqk,bqhe->bkhe", probs.astype(jnp.bfloat16), grad_attended,
        preferred_element_type=jnp.float32,
    )
    grad_probs = jnp.einsum(
        "bqhe,bkhe->bhqk", grad_attended, value_rows, preferred_element_type=jnp.float32
    )
    grad_scores = (
        probs * (grad_probs - jnp.sum(probs * grad_probs, axis=-1, keepdims=True))
    ).astype(jnp.bfloat16)
    grad_queries = (
        jnp.einsum("bhqk,bkhe->bqhe", grad_scores, key_rows, preferred_element_type=jnp.float32)
        * score_scale
    )
    grad_keys = (
        jnp.einsum("bhqk,bqhe->bkhe", grad_scores, queries, preferred_element_type=jnp.float32)
        * score_scale
    )
    grad_projected = jnp.stack([grad_queries, grad_keys, grad_values], axis=2).astype(jnp.bfloat16)
    grad_projected = grad_projected.reshape(row_count, 3, head_count * HD)
    grad_w_qkv = jnp.einsum(
        "rd,rcf->dcf", first, grad_projected, preferred_element_type=jnp.float32
    )
    partial_first = jnp.einsum(
        "rcf,dcf->rd", grad_projected, w_qkv, preferred_element_type=jnp.float32
    )
    halves = partial_first.astype(jnp.bfloat16).reshape((6, -1, LANES))
    both = exchange(halves, 2, True, "pair", 2, pieces=6).astype(jnp.float32)
    both = both.reshape((2,) + partial_first.shape)
    grad_first = (both[0] + both[1]).astype(jnp.bfloat16).astype(jnp.float32)
    grad_input_norm, grad_gain_one, grad_shift_one = norm_backward(
        grad_first, normed_one, inverse_one, gain_rows[0]
    )
    grad_input = grad_hidden + grad_input_norm
    grads = (
        grad_w_qkv,
        grad_w_proj,
        grad_w_in,
        grad_w_out,
        grad_w_router,
        jnp.stack([grad_gain_one, grad_gain_two]),
        jnp.stack([grad_shift_one, grad_shift_two]),
    )
    return (grad_input.reshape(image_count, length, model_width), grads)


def make_local(n):
    def local(images, routes, w_qkv, w_proj, w_in, w_out, w_router, ln_gain, ln_bias, cotangent):
        shapes = [a.shape for a in (w_qkv, w_proj, w_in, w_out, w_router, ln_gain, ln_bias)]
        weights = gather_weights(w_qkv, w_proj, w_in, w_out, w_router, ln_gain, ln_bias, n)
        field = images.astype(jnp.float32)
        output, record = layer_forward(field, routes[0], weights)
        grad_input, grads = layer_backward(cotangent.astype(jnp.float32), record, weights)
        shards = scatter_grads(grads, n, [(1,) + tuple(s[1:]) for s in shapes])
        return (output, grad_input, *shards)

    return local


def solution(mesh):
    n = mesh.shape["dp"]
    in_specs = (
        P("dp", None, None),
        P(None, "dp", None, None),
        P(None, "dp", None, "mp"),
        P(None, "mp", "dp"),
        P(None, None, "dp", "mp"),
        P(None, None, "mp", "dp"),
        P(None, "dp", None),
        P(None, None, "dp"),
        P(None, None, "dp"),
        P("dp", None, None),
    )
    out_specs = (
        P("dp", None, None),
        P("dp", None, None),
        P(None, "dp", None, "mp"),
        P(None, "mp", "dp"),
        P(None, None, "dp", "mp"),
        P(None, None, "mp", "dp"),
        P(None, "dp", None),
        P(None, None, "dp"),
        P(None, None, "dp"),
    )
    return jax.shard_map(make_local(n), mesh=mesh, in_specs=in_specs, out_specs=out_specs, check_vma=False)
```
